32 devices in a mesh: dp: 16 (over z, x, core), tensor: 2 (over y).
Axes of the slice: x: 2, y: 2, z: 4, core: 2. Of those that a mesh axis runs over, the one named last changes fastest.
Arguments:
- tokens: bfloat16 [32, 256, 768], P('dp', 'tensor'), may hold values from -6 to 6
- w_qkv: bfloat16 [3, 768, 768], P(None, 'dp', 'tensor'), may hold values from -0.21875 to 0.21875
- qv_bias: float32 [2, 768], replicated, may hold values from -3 to 3
- w_proj: bfloat16 [768, 768], P(('tensor', 'dp')), may hold values from -2.5 to 2.5
- proj_bias: float32 [768], replicated, may hold values from -3 to 3
- w_up: bfloat16 [768, 3072], P('dp', 'tensor'), may hold values from -0.21875 to 0.21875
- up_bias: float32 [3072], replicated, may hold values from -3 to 3
- w_down: bfloat16 [3072, 768], P(('tensor', 'dp')), may hold values from -0.15625 to 0.15625
- down_bias: float32 [768], replicated, may hold values from -3 to 3
- norm1_gain: float32 [768], replicated, may hold values from 0.1 to 1.9
- norm1_shift: float32 [768], replicated, may hold values from -2 to 2
- norm2_gain: float32 [768], replicated, may hold values from 0.1 to 1.9
- norm2_shift: float32 [768], replicated, may hold values from -2 to 2
- rel_rows: bfloat16 [31, 64], replicated, may hold values from -0.59765625 to 0.59765625
- rel_cols: bfloat16 [31, 64], replicated, may hold values from -0.59765625 to 0.59765625
- cotangent: bfloat16 [32, 256, 768], P('dp', 'tensor'), may hold values from -6 to 6
Outputs:
- block_out: bfloat16 [32, 256, 768], P('dp', 'tensor')
- grad_tokens: float32 [32, 256, 768], P('dp', 'tensor')
- grad_w_qkv: float32 [3, 768, 768], P(None, 'dp', 'tensor')
- grad_qv_bias: float32 [2, 768], replicated
- grad_w_proj: float32 [768, 768], P(('tensor', 'dp'))
- grad_proj_bias: float32 [768], replicated
- grad_w_up: float32 [768, 3072], P('dp', 'tensor')
- grad_up_bias: float32 [3072], replicated
- grad_w_down: float32 [3072, 768], P(('tensor', 'dp'))
- grad_down_bias: float32 [768], replicated
- grad_norm1_gain: float32 [768], replicated
- grad_norm1_shift: float32 [768], replicated
- grad_norm2_gain: float32 [768], replicated
- grad_norm2_shift: float32 [768], replicated
- grad_rel_rows: float32 [31, 64], replicated
- grad_rel_cols: float32 [31, 64], replicated
The draws below stay inside these ranges and needn't reach their ends.
All inputs are finite; a program needn't handle non-finite values.
Results may differ from the reference program's by a relative error of at most 0.015.
Values may be sent and summed in bfloat16 or wider, within the bound.
A program may use at most 192 MiB of HBM per device.

```python
import jax
import jax.numpy as jnp
from jax import lax

D = 768
HEADS = 12
HD = 64
FF = 3072
GRID = 16
TOK = 256
RELS = 31
IMAGES = 32


def strengthened(values, own_key, source, target, blocks, factor):
    owner, partner = [(jnp.arange(values.shape[position]) // (values.shape[position] // blocks)).reshape([-1 if axis == position else 1 for axis in range(values.ndim)]) for position in (source, target)]
    chosen = jax.random.permutation(own_key, blocks)[partner]
    strong = (owner == chosen) | (owner == (partner + blocks // 2) % blocks)
    return jnp.where(strong, factor * values, values)


def block_levels(rng, shape, split, smallest, top_value):
    gain = 1.0
    for dim, shards_of in split:
        draws = jax.random.uniform(jax.random.fold_in(jax.random.fold_in(rng, 6), dim), (shards_of,), jnp.float32, smallest / len(split), top_value / len(split))
        gain = gain * jnp.repeat(jnp.exp(draws), shape[dim] // shards_of).reshape((-1,) + (1,) * (len(shape) - 1 - dim))
    return gain


def gaussian(stream_key, dims, spread, most, pieces=(), kind=jnp.bfloat16):
    values = spread * jax.random.normal(stream_key, dims, jnp.float32)
    if pieces:
        values = values * block_levels(stream_key, dims, pieces, -0.22, 0.18)
    return jnp.clip(values, -most, most).astype(kind)


def bell_draw_with(own_key, shape, width, most, split, heavy, kind=jnp.bfloat16):
    values = width * jax.random.normal(own_key, shape, jnp.float32)
    if split:
        values = values * block_levels(own_key, shape, split, -0.22, 0.18)
    return jnp.clip(strengthened(values, jax.random.fold_in(own_key, 3), *heavy), -most, most).astype(kind)


def setup_inputs(seed: int = 0) -> dict:
    keys = jax.random.split(jax.random.key(seed), 17)
    return {
        "tokens": bell_draw_with(keys[0], (IMAGES, TOK, D), 1.0, 6.0, ((0, 16), (1, 2)), (0, 2, 16, 2.0)),
        "w_qkv": gaussian(keys[1], (3, D, D), D ** -0.5, 0.21875, ((1, 16), (2, 2))),
        "qv_bias": gaussian(keys[2], (2, D), 0.5, 3.0, (), jnp.float32),
        "w_proj": gaussian(keys[3], (D, D), (D // 128) ** -0.5, 2.5, ((0, 32),)),
        "proj_bias": gaussian(keys[4], (D,), 0.5, 3.0, (), jnp.float32),
        "w_up": gaussian(keys[5], (D, FF), D ** -0.5, 0.21875, ((0, 16), (1, 2))),
        "up_bias": gaussian(keys[6], (FF,), 0.5, 3.0, (), jnp.float32),
        "w_down": gaussian(keys[7], (FF, D), (FF // 2) ** -0.5, 0.15625, ((0, 32),)),
        "down_bias": gaussian(keys[8], (D,), 0.5, 3.0, (), jnp.float32),
        "norm1_gain": jnp.clip(1.0 + 0.18 * jax.random.normal(keys[9], (D,), jnp.float32), 0.1, 1.9),
        "norm1_shift": gaussian(keys[10], (D,), 0.3, 2.0, (), jnp.float32),
        "norm2_gain": jnp.clip(1.0 + 0.18 * jax.random.normal(keys[11], (D,), jnp.float32), 0.1, 1.9),
        "norm2_shift": gaussian(keys[12], (D,), 0.3, 2.0, (), jnp.float32),
        "rel_rows": gaussian(keys[13], (RELS, HD), 0.1, 0.59765625),
        "rel_cols": gaussian(keys[14], (RELS, HD), 0.1, 0.59765625),
        "cotangent": gaussian(keys[15], (IMAGES, TOK, D), 1.0, 6.0, ((0, 16), (1, 2))),
    }


@jax.custom_vjp
def low(v):
    return lax.optimization_barrier(v.astype(jnp.bfloat16)).astype(jnp.float32)

@jax.custom_vjp
def low_back(v):
    return v

def low_keep(v):
    return (low(v), None)

def low_pass(kept, grad):
    return (grad,)

def back_keep(v):
    return (v, None)

def back_low(kept, grad):
    return (low(grad),)
low.defvjp(low_keep, low_pass)
low_back.defvjp(back_keep, back_low)
eps_norm = 1e-06

def layer_norm(values, gain_vec, shift_vec):
    row_mean = lax.optimization_barrier(jnp.mean(values, axis=-1, keepdims=True))
    centred = values - row_mean
    second_moment = lax.optimization_barrier(jnp.mean(centred * centred, axis=-1, keepdims=True))
    return centred * lax.rsqrt(second_moment + eps_norm) * gain_vec + shift_vec

def block_forward(query_blk, key_all, value_all, rows_blk, cols_full):
    grid_rows = query_blk.shape[0] // GRID
    head_count = query_blk.shape[1]
    highest = lax.Precision.HIGHEST
    scores = jnp.einsum('qhc,khc->hqk', query_blk, key_all, precision=highest) * HD ** (-0.5)
    query_grid = query_blk.reshape(grid_rows, GRID, head_count, HD)
    along_rows = jnp.einsum('awhc,akc->hawk', query_grid, rows_blk, precision=highest)
    along_cols = jnp.einsum('awhc,wkc->hawk', query_grid, cols_full, precision=highest)
    scores = scores.reshape(head_count, grid_rows, GRID, GRID, GRID) + along_rows[..., :, None] + along_cols[..., None, :]
    scores = low_back(scores.reshape(head_count, grid_rows * GRID, GRID * GRID))
    probs = low(jax.nn.softmax(scores, axis=-1))
    return jnp.einsum('hqk,khc->qhc', probs, value_all, precision=highest)

def forward_image(image_rows, w_qkv, qv_bias, w_proj, proj_bias, w_up, up_bias, w_down, down_bias, norm1_gain, norm1_shift, norm2_gain, norm2_shift, rel_rows, rel_cols):
    highest = lax.Precision.HIGHEST
    first_norm = low(layer_norm(image_rows, norm1_gain, norm1_shift))
    bias_full = jnp.stack([qv_bias[0], jnp.zeros_like(qv_bias[0]), qv_bias[1]])
    proj_qkv = jnp.einsum('td,sde->ste', first_norm, w_qkv, precision=highest) + bias_full[:, None, :]
    proj_qkv = low_back(low(proj_qkv)).reshape(3, TOK, HEADS, HD)
    grid_idx = jnp.arange(GRID, dtype=jnp.int32)
    offsets = grid_idx[:, None] - grid_idx[None, :] + (GRID - 1)
    rows_full = rel_rows[offsets]
    cols_full = rel_cols[offsets]
    block_rows = min(512, TOK)
    block_count = TOK // block_rows
    grid_rows = block_rows // GRID
    blocks = proj_qkv[0].reshape(block_count, block_rows, HEADS, HD)

    def one_block(packed):
        query_blk, block_idx = packed
        rows_blk = lax.dynamic_slice_in_dim(rows_full, block_idx * grid_rows, grid_rows, 0)
        return block_forward(query_blk, proj_qkv[1], proj_qkv[2], rows_blk, cols_full)
    mixed_out = lax.map(jax.checkpoint(one_block), (blocks, jnp.arange(block_count, dtype=jnp.int32)))
    mixed_out = low_back(low(mixed_out.reshape(TOK, D)))
    middle = image_rows + (low_back(jnp.dot(mixed_out, w_proj, precision=highest)) + proj_bias)
    second_norm = low(layer_norm(middle, norm2_gain, norm2_shift))
    pre_act = low_back(jnp.dot(second_norm, w_up, precision=highest) + up_bias)
    activated = low(jax.nn.gelu(pre_act, approximate=False))
    return middle + (low_back(jnp.dot(activated, w_down, precision=highest)) + down_bias)

def reference(tokens, w_qkv, qv_bias, w_proj, proj_bias, w_up, up_bias, w_down, down_bias, norm1_gain, norm1_shift, norm2_gain, norm2_shift, rel_rows, rel_cols, cotangent):
    params = tuple((entry.astype(jnp.float32) for entry in (w_qkv, qv_bias, w_proj, proj_bias, w_up, up_bias, w_down, down_bias, norm1_gain, norm1_shift, norm2_gain, norm2_shift, rel_rows, rel_cols)))

    def scan_step(totals, packed):
        image_rows, grad_out = packed
        result, pull_back = jax.vjp(forward_image, image_rows.astype(jnp.float32), *params)
        grad_list = pull_back(grad_out.astype(jnp.float32))
        totals = tuple((left_term + right_term for left_term, right_term in zip(totals, grad_list[1:])))
        return (totals, (result.astype(jnp.bfloat16), grad_list[0]))
    zero_init = tuple((jnp.zeros(entry.shape, jnp.float32) for entry in params))
    totals, (results, grad_tokens) = lax.scan(scan_step, zero_init, (tokens, cotangent))
    return (results, grad_tokens, totals[0], totals[1], totals[2], totals[3], totals[4], totals[5], totals[6], totals[7], totals[8], totals[9], totals[10], totals[11], totals[12], totals[13])
```

```python
import functools

import jax
import jax.numpy as jnp
from jax import lax
from jax.experimental import pallas as pl
from jax.experimental.pallas import tpu as pltpu
from jax.sharding import PartitionSpec as P

D = 768
HD = 64
FF = 3072
GRID = 16
TOK = 256
RELS = 31
NZ, NX, NC = 4, 2, 2
RING = NZ * NX * NC
IMG = 2
PAIR = 2 * HD
CH = 64
EPS = 1e-06
F32 = jnp.float32
BF = jnp.bfloat16
MESH = pl.DeviceIdType.MESH
SCALE = HD ** (-0.5)
QKV_M, PROJ_M, UP_M, DOWN_M = range(4)


def nn(a, b):
    return lax.dot_general(a, b, (((1,), (0,)), ((), ())), preferred_element_type=F32)


def nt(a, b):
    return lax.dot_general(a, b, (((1,), (1,)), ((), ())), preferred_element_type=F32)


def tn(a, b):
    return lax.dot_general(a, b, (((0,), (0,)), ((), ())), preferred_element_type=F32)


def iota(shape, dim):
    return lax.broadcasted_iota(jnp.int32, shape, dim)


def one_hot(cond):
    return jnp.where(cond, 1.0, 0.0).astype(BF)


def mean_last(v):
    return jnp.sum(v, axis=-1, keepdims=True) * (1.0 / v.shape[-1])


def normalize(v):
    centred = v - mean_last(v)
    rstd = lax.rsqrt(mean_last(centred * centred) + EPS)
    return centred * rstd, rstd


def norm_back(grad, n, rstd, gain):
    e = grad * gain
    return (e - mean_last(e) - n * mean_last(e * n)) * rstd


def spread_rows(v):
    return jnp.concatenate(
        [pltpu.roll(v[g * GRID : (g + 1) * GRID], g, 1) if g else v[:GRID] for g in range(GRID)], axis=0
    )


def spread_cols(v):
    return jnp.concatenate(
        [
            pltpu.roll(v[g * GRID : (g + 1) * GRID], 0, 1, stride=1, stride_axis=0)
            for g in range(GRID)
        ],
        axis=0,
    )


NAMES_IN = (
    "tok", "cot", "sq", "sp", "su", "sd",
    "qvb", "pjb", "upb", "dnb", "g1", "b1",
    "g2", "b2", "relr", "relc",
)
NAMES_OUT = (
    "o_blk", "o_gtok", "o_gq", "o_gp", "o_gu", "o_gd",
    "o_sm", "o_rel",
)


def scratch_table(width, hid):
    pairs = width // PAIR
    half = TOK // 2
    shards = [(3, D // RING, width), (width // RING, D), (D // RING, hid), (hid // RING, D)]
    table = {
        "XT": ((IMG, TOK, D), BF),
        "CT": ((IMG, TOK, D), BF),
        "WPB": ((width, D), BF),
        "FL": ((IMG, TOK, D), BF),
        "QKV": ((3, pairs, IMG, TOK, PAIR), BF),
        "PT": ((pairs, IMG, 2, TOK, TOK), BF),
        "MX": ((IMG, TOK, width), BF),
        "AP": ((IMG, TOK, D), BF),
        "APR": ((IMG, TOK, D), BF),
        "MID": ((IMG, TOK, D), F32),
        "N2": ((IMG, TOK, D), F32),
        "RS2": ((IMG, TOK, 128), F32),
        "SEC": ((IMG, TOK, D), BF),
        "ACT": ((IMG, TOK, hid), BF),
        "GEL": ((IMG, TOK, hid), BF),
        "DP": ((IMG, TOK, D), BF),
        "DPR": ((IMG, half, D), BF),
        "GPRE": ((IMG, TOK, hid), BF),
        "GS": ((IMG, TOK, D), BF),
        "GSR": ((IMG, TOK, D), BF),
        "GM": ((IMG, half, D), F32),
        "MIDL": ((IMG, TOK, D), BF),
        "GMX": ((IMG, TOK, width), BF),
        "GQKV": ((3, IMG, TOK, width), BF),
        "GF": ((IMG, TOK, D), BF),
        "GFR": ((IMG, half, D), BF),
        "RG": ((PAIR, PAIR), F32),
        "TBF": ((PAIR, PAIR), BF),
        "TBB": ((PAIR, PAIR), BF),
        "OHF": ((TOK, PAIR), BF),
        "OHB": ((TOK, PAIR), BF),
        "MSK": ((4, 16, PAIR), BF),
        "SMS": ((6, 16, D), F32),
        "SMR": ((5, 16, D), F32),
        "SRS": ((6, 64, 128), F32),
        "SRR": ((5, 64, 128), F32),
    }
    for i, shard in enumerate(shards):
        table[f"W{i}"] = ((NZ, NX, NC) + shard, BF)
        table[f"G{i}"] = ((NZ, NX, NC) + shard, BF)
        table[f"C{i}"] = ((NZ, NX) + shard, BF)
        table[f"X{i}"] = ((NZ,) + shard, BF)
        table[f"Z{i}"] = ((NZ - 1,) + shard, BF)
    sems = {
        "agz": (4, 3),
        "agx": (4, 4),
        "agc": (4, 8),
        "ysem": (10,),
        "rsc": (4,),
        "rsx": (4, 4),
        "rsz": (4, 3),
        "ars": (5, 2),
    }
    return table, sems, shards


class Refs:
    pass


def block_kernel(ratio, width, hid, names, *refs):
    k = Refs()
    for name, ref in zip(names, refs):
        setattr(k, name, ref)
    pairs = width // PAIR
    half = TOK // 2
    dp = lax.axis_index("dp")
    t = lax.axis_index("tensor")
    sub = lax.rem(dp, ratio)
    s = dp // ratio
    z, x, c = s // (NX * NC), lax.rem(s // NC, NX), lax.rem(s, NC)

    def device(zz, xx, cc, tt=t):
        return (((zz * NX + xx) * NC + cc) * ratio + sub, tt)

    def zrot(step):
        return lax.rem(z + step, NZ)

    core_peer, x_peer, y_peer = device(z, x, 1 - c), device(z, 1 - x, c), device(z, x, c, 1 - t)
    z_near = z + 1 - 2 * lax.rem(z, 2)
    z_far = lax.rem(z + 2, NZ)
    own0 = pl.multiple_of(t * half, half)
    other0 = pl.multiple_of((1 - t) * half, half)

    def remote(src, dst, sems, idx, peer):
        return pltpu.make_async_remote_copy(
            src_ref=src,
            dst_ref=dst,
            send_sem=getattr(k, sems + "_s").at[idx],
            recv_sem=getattr(k, sems + "_r").at[idx],
            device_id=peer,
            device_id_type=MESH,
        )

    shard_in = [k.sq, k.sp, k.su, k.sd]
    W = [k.W0, k.W1, k.W2, k.W3]
    G = [k.G0, k.G1, k.G2, k.G3]
    C = [k.C0, k.C1, k.C2, k.C3]
    X = [k.X0, k.X1, k.X2, k.X3]
    Z = [k.Z0, k.Z1, k.Z2, k.Z3]

    def ag_z(m, i):
        return remote(shard_in[m], W[m].at[z, x, c], "agz", (m, i - 1), device(zrot(i), x, c))

    def ag_x(m, i):
        zz = zrot(NZ - i)
        src = shard_in[m] if i == 0 else W[m].at[zz, x, c]
        return remote(src, W[m].at[zz, x, c], "agx", (m, i), x_peer)

    def ag_c(m, i, other):
        zz = zrot(NZ - i)
        xx = 1 - x if other else x
        src = shard_in[m] if i == 0 and not other else W[m].at[zz, xx, c]
        return remote(src, W[m].at[zz, xx, c], "agc", (m, i + 4 * other), core_peer)

    def ag_start(m):
        for i in (2, 1, 3):
            ag_z(m, i).start()
        ag_x(m, 0).start()
        ag_c(m, 0, 0).start()
        W[m][z, x, c] = shard_in[m][...]

    def ag_zdone(m):
        for i in (1, 3, 2):
            ag_z(m, i).wait_recv()
            ag_x(m, i).start()
            ag_c(m, i, 0).start()

    def ag_xdone(m):
        for i in (0, 1, 3, 2):
            ag_x(m, i).wait_recv()
            ag_c(m, i, 1).start()

    def ag_done(m):
        for other in (0, 1):
            for i in (0, 1, 3, 2):
                ag_c(m, i, other).wait_recv()

    def rs_core(m):
        return remote(G[m].at[:, :, 1 - c], C[m], "rsc", (m,), core_peer)

    def rs_x(m, zz):
        return remote(G[m].at[zz, 1 - x, c], X[m].at[zz], "rsx", (m, zz), x_peer)

    def rs_z(m, i):
        return remote(G[m].at[zrot(i), x, c], Z[m].at[i - 1], "rsz", (m, i - 1), device(zrot(i), x, c))

    def add_into(dst, where, src, which):
        if len(dst.shape) - len(where) == 3:
            for j in range(3):
                dst[(*where, j)] = dst[(*where, j)] + src[(*which, j)]
        else:
            dst[where] = dst[where] + src[which]

    def rs_core_done(m):
        rs_core(m).wait_recv()

        @pl.loop(0, NZ * NX)
        def _(i):
            zz, xx = i // NX, lax.rem(i, NX)
            add_into(G[m], (zz, xx, c), C[m], (zz, xx))

        for zz in range(NZ):
            rs_x(m, zz).start()

    def rs_x_done(m):
        for zz in range(NZ):
            rs_x(m, zz).wait_recv()

        @pl.loop(0, NZ)
        def _(zz):
            add_into(G[m], (zz, x, c), X[m], (zz,))

        for i in (2, 1, 3):
            rs_z(m, i).start()

    def rs_z_done(m, out):
        for i in (1, 2, 3):
            rs_z(m, i).wait_recv()
        parts = range(3) if m == QKV_M else (None,)
        for j in parts:
            at = () if j is None else (j,)
            total = G[m][(z, x, c, *at)].astype(F32)
            for i in range(3):
                total = total + Z[m][(i, *at)].astype(F32)
            if j is None:
                out[...] = total
            else:
                out[j] = total

    def y_rows(img, base):
        return (img, pl.ds(base, half))

    def y_tok():
        return remote(k.tok, k.XT.at[:, pl.ds(own0, half)], "ysem", (0,), y_peer)

    def y_cot():
        return remote(k.cot, k.CT.at[:, pl.ds(own0, half)], "ysem", (1,), y_peer)

    def y_attn(img):
        return remote(k.AP.at[img], k.APR.at[img], "ysem", (2 + img,), y_peer)

    def y_mlp(img):
        return remote(k.DP.at[img, pl.ds(other0, half)], k.DPR.at[img], "ysem", (4 + img,), y_peer)

    def y_sec(img):
        return remote(k.GS.at[img], k.GSR.at[img], "ysem", (6 + img,), y_peer)

    def y_first(img):
        return remote(k.GF.at[img, pl.ds(other0, half)], k.GFR.at[img], "ysem", (8 + img,), y_peer)

    def rows(base, i):
        return pl.ds(pl.multiple_of(base + i * CH, CH), CH)

    barrier = pltpu.get_barrier_semaphore()
    peers = [core_peer, x_peer, y_peer] + [device(zrot(i), x, c) for i in (1, 2, 3)]
    for peer in peers:
        pl.semaphore_signal(barrier, inc=1, device_id=peer, device_id_type=MESH)
    pl.semaphore_wait(barrier, len(peers))

    ag_start(QKV_M)
    y_tok().start()
    ag_start(PROJ_M)
    ag_start(UP_M)
    ag_start(DOWN_M)
    y_cot().start()

    lane = iota((TOK, PAIR), 1)
    lane64 = lax.rem(lane, HD)
    urow, ucol = iota((TOK, PAIR), 0) // GRID, lax.rem(iota((TOK, PAIR), 0), GRID)
    shifted = lax.rem(lane + (PAIR - GRID + 1), HD)
    seg, pos = shifted // GRID, lax.rem(shifted, GRID)
    k.OHF[...] = one_hot(((seg < 2) & (urow == pos)) | ((seg >= 2) & (ucol == pos)))
    k.OHB[...] = one_hot(
        ((lane64 < GRID) & (urow == GRID - 1 - lane64))
        | ((lane64 >= 2 * GRID) & (lane64 < 3 * GRID) & (ucol == 3 * GRID - 1 - lane64))
    )
    mlane = iota((16, PAIR), 1)
    in_first = mlane < HD
    ext_first = (mlane >= GRID - 1) & (mlane < HD + GRID - 1)
    k.MSK[0] = one_hot(in_first)
    k.MSK[1] = one_hot(mlane >= HD)
    k.MSK[2] = one_hot(ext_first)
    k.MSK[3] = one_hot((mlane < GRID - 1) | (mlane >= HD + GRID - 1))
    tl, td = iota((PAIR, RELS), 0), iota((PAIR, RELS), 1)
    fwd_tab = jnp.zeros((PAIR, PAIR), F32)
    bwd_tab = jnp.zeros((PAIR, PAIR), F32)
    for head in range(2):
        place = one_hot(iota((HD, PAIR), 1) == iota((HD, PAIR), 0) + head * HD)
        for base, rel in ((0, k.relr), (32, k.relc)):
            wide = nn(rel[...], place).astype(BF)
            at = tl - (head * HD + base)
            fwd_tab = fwd_tab + nn(one_hot(at == RELS - 1 - td), wide)
            bwd_tab = bwd_tab + nn(one_hot(at == td), wide)
    k.TBF[...] = fwd_tab.astype(BF)
    k.TBB[...] = bwd_tab.astype(BF)
    k.SMS[0] = jnp.zeros((16, D), F32)
    k.RG[...] = jnp.zeros((PAIR, PAIR), F32)

    def first_norm(base):
        @pl.loop(0, IMG)
        def _(img):
            @pl.loop(0, half // CH)
            def _(i):
                at = rows(base, i)
                n, _ = normalize(k.XT[img, at].astype(F32))
                k.FL[img, at] = (n * k.g1[...] + k.b1[...]).astype(BF)

    for img in range(IMG):
        k.XT[img, pl.ds(own0, half)] = k.tok[img]
        k.CT[img, pl.ds(own0, half)] = k.cot[img]
    first_norm(own0)
    ag_zdone(QKV_M)
    y_tok().wait_recv()
    first_norm(other0)
    ag_xdone(QKV_M)
    ag_zdone(PROJ_M)
    ag_done(QKV_M)

    lanes_w = pl.ds(pl.multiple_of(t * width, 128), width)
    for i in range(3):

        @pl.loop(0, IMG)
        def _(img):
            out = nn(k.FL[img], W[0][:, :, :, i].reshape(D, width))
            if i != 1:
                out = out + k.qvb[i // 2 : i // 2 + 1, lanes_w]
            low = out.astype(BF)
            for p in range(pairs):
                k.QKV[i, p, img] = low[:, p * PAIR : (p + 1) * PAIR]

    ag_zdone(UP_M)
    ag_xdone(PROJ_M)

    def head_mask(i):
        return k.MSK[i][0:1]

    def attend(step):
        img, p = step // pairs, lax.rem(step, pairs)
        q, key, val = k.QKV[0, p, img], k.QKV[1, p, img], k.QKV[2, p, img]
        qr = nt(q, k.TBF[...])
        ext = jnp.where(
            (lane64 >= 15) & (lane64 < 31),
            spread_rows(qr),
            jnp.where((lane64 >= 47) & (lane64 < 63), spread_cols(qr), 0.0),
        )
        high = ext.astype(BF).astype(F32)
        ext = (high + pltpu.roll(ext - high, GRID, 1)).astype(BF)
        k_ext = jnp.concatenate([key, k.OHF[...]], axis=1)
        probs, vals = [], []
        for head in range(2):
            q_ext = jnp.concatenate(
                [q * (head_mask(head) * SCALE).astype(BF), ext * head_mask(2 + head)], axis=1
            )
            scores = nt(k_ext, q_ext)
            e = jnp.exp(scores - jnp.max(scores, axis=0, keepdims=True))
            low = (e * (1.0 / jnp.sum(e, axis=0, keepdims=True))).astype(BF)
            k.PT[p, img, head] = low
            probs.append(low)
            vals.append(val * head_mask(head))
        mixed = tn(jnp.concatenate(probs, axis=0), jnp.concatenate(vals, axis=0))
        k.MX[img, :, pl.ds(pl.multiple_of(p * PAIR, PAIR), PAIR)] = mixed.astype(BF)

    def project(img):
        for j in range(D // 256):
            cols = slice(j * 256, (j + 1) * 256)
            k.AP[img, :, cols] = nn(k.MX[img], k.WPB[:, cols]).astype(BF)
        y_attn(img).start()

    @pl.loop(0, pairs)
    def _(step):
        attend(step)

    ag_xdone(UP_M)
    ag_zdone(DOWN_M)
    ag_done(PROJ_M)

    @pl.loop(0, RING)
    def _(i):
        zz, xx, cc = i // (NX * NC), lax.rem(i // NC, NX), lax.rem(i, NC)
        k.G1F[pl.ds(pl.multiple_of(i * (width // RING), 8), width // RING)] = W[1][zz, xx, cc].astype(F32)

    k.WPB[...] = k.G1F[...].astype(BF)
    project(0)

    @pl.loop(pairs, 2 * pairs)
    def _(step):
        attend(step)

    project(1)
    ag_xdone(DOWN_M)
    ag_done(UP_M)

    def second(img):
        y_attn(img).wait_recv()

        @pl.loop(0, TOK // CH)
        def _(i):
            at = rows(0, i)
            mid = (
                k.XT[img, at].astype(F32)
                + k.AP[img, at].astype(F32)
                + k.APR[img, at].astype(F32)
                + k.pjb[...]
            )
            k.MID[img, at] = mid
            n, rstd = normalize(mid)
            k.N2[img, at] = n
            k.RS2[img, at] = jnp.broadcast_to(rstd, (CH, 128))
            k.SEC[img, at] = (n * k.g2[...] + k.b2[...]).astype(BF)

        @pl.loop(0, hid // 256)
        def _(j):
            cols = pl.ds(pl.multiple_of(j * 256, 256), 256)
            bias = k.upb[0:1, pl.ds(pl.multiple_of(t * hid + j * 256, 256), 256)]
            pre = nn(k.SEC[img], W[2][:, :, :, :, cols].reshape(D, 256)) + bias
            phi = 0.5 + 0.5 * lax.erf(pre * 0.7071067811865476)
            k.ACT[img, :, cols] = (pre * phi).astype(BF)
            k.GEL[img, :, cols] = (phi + pre * (0.3989422804014327 * jnp.exp(-0.5 * pre * pre))).astype(BF)

    second(0)
    second(1)
    ag_done(DOWN_M)

    def down(img):
        @pl.loop(0, D // 256)
        def _(j):
            cols = pl.ds(pl.multiple_of(j * 256, 256), 256)
            k.DP[img, :, cols] = nn(k.ACT[img], W[3][:, :, :, :, cols].reshape(hid, 256)).astype(BF)

        y_mlp(img).start()

    y_cot().wait_recv()

    tile = hid // NZ

    @pl.loop(0, NZ)
    def _(m):
        lhs = k.ACT[:, :, pl.ds(pl.multiple_of(m * tile, 128), tile)].reshape(IMG * TOK, tile)
        for j in range(D // 256):
            cols = slice(j * 256, (j + 1) * 256)
            out = tn(lhs, k.CT[:, :, cols].reshape(IMG * TOK, 256)).astype(BF)
            G[3][m, :, :, :, cols] = out.reshape(NX, NC, hid // RING, 256)

    rs_core(DOWN_M).start()

    @pl.loop(0, NZ)
    def _(m):
        cols = pl.ds(pl.multiple_of(m * tile, 128), tile)
        sums = jnp.zeros((1, tile), F32)
        for img in range(IMG):
            grad = nt(k.CT[img], W[3][m].reshape(tile, D)) * k.GEL[img, :, cols].astype(F32)
            low = grad.astype(BF)
            k.GPRE[img, :, cols] = low
            sums = sums + jnp.sum(low.astype(F32), axis=0, keepdims=True)
        per_row = D // tile
        k.SMS[0, pl.ds(8 + t * (hid // D) + m // per_row, 1), pl.ds(pl.multiple_of(lax.rem(m, per_row) * tile, 128), tile)] = sums

    for img in range(IMG):

        @pl.loop(0, 2)
        def _(j):
            w = W[2][pl.ds(j * 2, 2)].reshape(D // 2, hid)
            k.GS[img, :, pl.ds(pl.multiple_of(j * (D // 2), 128), D // 2)] = nt(k.GPRE[img], w).astype(BF)

        y_sec(img).start()

    rs_core_done(DOWN_M)

    @pl.loop(0, hid // 256)
    def _(j):
        cols = pl.ds(pl.multiple_of(j * 256, 256), 256)
        rhs = k.GPRE[:, :, cols].reshape(IMG * TOK, 256)
        for m in range(2):
            lhs = k.SEC[:, :, m * (D // 2) : (m + 1) * (D // 2)].reshape(IMG * TOK, D // 2)
            out = tn(lhs, rhs).astype(BF)
            G[2][2 * m : 2 * m + 2, :, :, :, cols] = out.reshape(2, NX, NC, D // RING, 256)

    rs_core(UP_M).start()
    down(0)
    down(1)
    rs_core_done(UP_M)

    def middle_back(img, base, own):
        zero = jnp.zeros((1, D), F32)

        def chunk(i, sums):
            at = rows(base, i)
            grad = k.GS[img, at].astype(F32) + k.GSR[img, at].astype(F32)
            n = k.N2[img, at]
            rstd = jnp.concatenate([k.RS2[img, at]] * (D // 128), axis=1)
            cot = k.CT[img, at].astype(F32)
            gm = cot + norm_back(grad, n, rstd, k.g2[...])
            k.MIDL[img, at] = gm.astype(BF)
            if own:
                k.GM[img, rows(0, i)] = gm
                terms = (grad * n, grad, gm, cot)
                sums = tuple(a + jnp.sum(b, axis=0, keepdims=True) for a, b in zip(sums, terms))
            return sums

        return lax.fori_loop(0, half // CH, chunk, (zero,) * 4 if own else ())

    for img in range(IMG):
        y_sec(img).wait_recv()
        sums = middle_back(img, own0, True)
        for row, value in zip((2, 3, 6, 7), sums):
            k.SMS[0, row : row + 1] = k.SMS[0, row : row + 1] + value
        middle_back(img, other0, False)
        k.GMX[img] = nt(k.MIDL[img], k.WPB[...]).astype(BF)

    for j in range(D // 256):
        cols = slice(j * 256, (j + 1) * 256)
        out = tn(k.MX[...].reshape(IMG * TOK, width), k.MIDL[:, :, cols].reshape(IMG * TOK, 256))
        G[1][:, :, :, :, cols] = out.reshape(NZ, NX, NC, width // RING, 256).astype(BF)
    rs_core(PROJ_M).start()
    rs_x_done(DOWN_M)

    def attend_back(step):
        img, p = step // pairs, lax.rem(step, pairs)
        cols = pl.ds(pl.multiple_of(p * PAIR, PAIR), PAIR)
        q, key, val = k.QKV[0, p, img], k.QKV[1, p, img], k.QKV[2, p, img]
        gmx = k.GMX[img, :, cols]
        pts, gss, gms, qs, kes = [], [], [], [], []
        for head in range(2):
            m = head_mask(head)
            low = k.PT[p, img, head]
            probs = low.astype(F32)
            gp = nt(val * m, gmx)
            inner = jnp.sum(gp * probs, axis=0, keepdims=True)
            pts.append(low)
            gss.append((probs * (gp - inner)).astype(BF))
            gms.append(gmx * m)
            qs.append(q * (m * SCALE).astype(BF))
            kes.append(jnp.concatenate([key * (m * SCALE).astype(BF), k.OHB[...] * m], axis=1))
        grad_v = nn(jnp.concatenate(pts, axis=1), jnp.concatenate(gms, axis=0))
        grad_k = nn(jnp.concatenate(gss, axis=1), jnp.concatenate(qs, axis=0))
        both = tn(jnp.concatenate(gss, axis=0), jnp.concatenate(kes, axis=0))
        rel = both[:, PAIR:]
        rel = jnp.where(lane64 < 32, spread_rows(rel), spread_cols(rel))
        high = rel.astype(BF)
        rest = (rel - high.astype(F32)).astype(BF)
        grad_q = both[:, :PAIR] + nn(
            jnp.concatenate([high, rest], axis=1), jnp.concatenate([k.TBB[...]] * 2, axis=0)
        )
        k.RG[...] += tn(jnp.concatenate([high, rest], axis=0), jnp.concatenate([q, q], axis=0))
        lanes = pl.ds(pl.multiple_of(t * width + p * PAIR, PAIR), PAIR)
        for i, grad in enumerate((grad_q, grad_k, grad_v)):
            low = grad.astype(BF)
            k.GQKV[i, img, :, cols] = low
            if i != 1:
                row = 4 + i // 2
                k.SMS[0, row : row + 1, lanes] = k.SMS[0, row : row + 1, lanes] + jnp.sum(
                    low.astype(F32), axis=0, keepdims=True
                )

    @pl.loop(0, pairs)
    def _(step):
        attend_back(step)

    rs_core_done(PROJ_M)
    rs_x_done(UP_M)

    @pl.loop(pairs, 2 * pairs)
    def _(step):
        attend_back(step)

    for i in range(3):

        @pl.loop(0, 2)
        def _(m):
            lhs = k.FL[:, :, pl.ds(pl.multiple_of(m * (D // 2), 128), D // 2)].reshape(IMG * TOK, D // 2)
            out = tn(lhs, k.GQKV[i].reshape(IMG * TOK, width)).astype(BF)
            G[0][pl.ds(2 * m, 2), :, :, i] = out.reshape(2, NX, NC, D // RING, width)

    rs_core(QKV_M).start()

    for img in range(IMG):

        @pl.loop(0, 2)
        def _(m):
            total = jnp.zeros((TOK, D // 2), F32)
            for i in range(3):
                total = total + nt(k.GQKV[i, img], W[0][pl.ds(2 * m, 2), :, :, i].reshape(D // 2, width))
            k.GF[img, :, pl.ds(pl.multiple_of(m * (D // 2), 128), D // 2)] = total.astype(BF)

        y_first(img).start()

    rs_core_done(QKV_M)
    rs_x_done(PROJ_M)

    for img in range(IMG):
        y_mlp(img).wait_recv()
        y_first(img).wait_recv()

        def finish(i, sums):
            at, here = rows(own0, i), rows(0, i)
            k.o_blk[img, here] = (
                k.MID[img, at] + k.DP[img, at].astype(F32) + k.DPR[img, here].astype(F32) + k.dnb[...]
            ).astype(BF)
            n, rstd = normalize(k.tok[img, here].astype(F32))
            grad = k.GF[img, at].astype(F32) + k.GFR[img, here].astype(F32)
            k.o_gtok[img, here] = k.GM[img, here] + norm_back(grad, n, rstd, k.g1[...])
            terms = (grad * n, grad)
            return tuple(a + jnp.sum(b, axis=0, keepdims=True) for a, b in zip(sums, terms))

        sums = lax.fori_loop(0, half // CH, finish, (jnp.zeros((1, D), F32),) * 2)
        for row, value in enumerate(sums):
            k.SMS[0, row : row + 1] = k.SMS[0, row : row + 1] + value

    rg = k.RG[...]
    turned = pltpu.roll(rg, HD, 1)
    k.SRS[0, 0:32] = rg[0:32] + turned[64:96]
    k.SRS[0, 32:64] = rg[32:64] + turned[96:128]

    ar_peers = [core_peer, x_peer, y_peer, device(z_near, x, c), device(z_far, x, c)]

    def ar(i):
        return (
            remote(k.SMS.at[i], k.SMR.at[i], "ars", (i, 0), ar_peers[i]),
            remote(k.SRS.at[i], k.SRR.at[i], "ars", (i, 1), ar_peers[i]),
        )

    def ar_step(i):
        for copy in ar(i):
            copy.wait_recv()
        k.SMS[i + 1] = k.SMS[i] + k.SMR[i]
        k.SRS[i + 1] = k.SRS[i] + k.SRR[i]
        if i < 4:
            for copy in ar(i + 1):
                copy.start()

    for copy in ar(0):
        copy.start()
    ar_step(0)
    rs_x_done(QKV_M)
    rs_z_done(DOWN_M, k.o_gd)
    ar_step(1)
    rs_z_done(UP_M, k.o_gu)
    ar_step(2)
    rs_z_done(PROJ_M, k.o_gp)
    ar_step(3)
    ar_step(4)
    k.o_sm[...] = k.SMS[5]
    k.o_rel[...] = k.SRS[5]
    rs_z_done(QKV_M, k.o_gq)

    for m in range(4):
        for i in (1, 2, 3):
            ag_z(m, i).wait_send()
            rs_z(m, i).wait_send()
        for i in range(4):
            ag_x(m, i).wait_send()
            ag_c(m, i, 0).wait_send()
            ag_c(m, i, 1).wait_send()
            rs_x(m, i).wait_send()
        rs_core(m).wait_send()
    for copy in (y_tok(), y_cot()):
        copy.wait_send()
    for img in range(IMG):
        for make in (y_attn, y_mlp, y_sec, y_first):
            make(img).wait_send()
    for i in range(5):
        for copy in ar(i):
            copy.wait_send()


def fused_block(ratio, args):
    width, hid = args[2].shape[2], args[4].shape[1]
    table, sems, shards = scratch_table(width, hid)
    table["G1F"] = ((width, D), F32)
    names = list(NAMES_IN) + list(NAMES_OUT) + list(table)
    scratch = [pltpu.VMEM(shape, kind) for shape, kind in table.values()]
    for name, shape in sems.items():
        names += [name + "_s", name + "_r"]
        scratch += [pltpu.SemaphoreType.DMA(shape)] * 2
    tok = args[0].shape
    outs = [(tok, BF), (tok, F32)] + [(shape, F32) for shape in shards] + [((16, D), F32), ((64, 128), F32)]
    vmem = pl.BlockSpec(memory_space=pltpu.VMEM)
    return pl.pallas_call(
        functools.partial(block_kernel, ratio, width, hid, names),
        out_shape=[jax.ShapeDtypeStruct(shape, kind) for shape, kind in outs],
        in_specs=[vmem] * len(NAMES_IN),
        out_specs=[vmem] * len(outs),
        scratch_shapes=scratch,
        compiler_params=pltpu.CompilerParams(
            collective_id=0, has_side_effects=True, vmem_limit_bytes=62 << 20
        ),
        name="fused_block",
    )(*args)


def on_device(dp_size, *args):
    (tokens, w_qkv, qv_bias, w_proj, proj_bias, w_up, up_bias, w_down, down_bias,
     norm1_gain, norm1_shift, norm2_gain, norm2_shift, rel_rows, rel_cols, cotangent) = args
    ratio = dp_size // RING
    weights = [w_qkv, w_proj, w_up, w_down]
    dims = (1, 0, 0, 0)
    groups = [[i * ratio + j for j in range(ratio)] for i in range(RING)]
    across = [[i * ratio + j for i in range(RING)] for j in range(ratio)]
    if ratio > 1:
        weights = [
            lax.all_gather(w, "dp", axis=dim, tiled=True, axis_index_groups=groups)
            for w, dim in zip(weights, dims)
        ]
    flat = lambda v: v.reshape(1, -1)
    outs = fused_block(
        ratio,
        (tokens, cotangent, *weights, qv_bias, flat(proj_bias), flat(up_bias), flat(down_bias),
         flat(norm1_gain), flat(norm1_shift), flat(norm2_gain), flat(norm2_shift), rel_rows, rel_cols),
    )
    block_out, grad_tokens, *grads, small, rel = outs
    if ratio > 1:
        grads = [
            lax.psum_scatter(g, "dp", scatter_dimension=dim, tiled=True, axis_index_groups=groups)
            for g, dim in zip(grads, dims)
        ]
        small, rel = lax.psum((small, rel), "dp", axis_index_groups=groups)
    return (
        block_out,
        grad_tokens,
        grads[0],
        small[4:6],
        grads[1],
        small[6],
        grads[2],
        small[8:12].reshape(-1),
        grads[3],
        small[7],
        small[0],
        small[1],
        small[2],
        small[3],
        rel[:RELS, :HD],
        rel[32 : 32 + RELS, :HD],
    )


def solution(mesh):
    split = P("dp", "tensor", None)
    specs = (split, P(None, "dp", "tensor"), P(), P(("tensor", "dp"), None), P(), P("dp", "tensor"), P(),
             P(("tensor", "dp"), None))
    return jax.shard_map(
        functools.partial(on_device, mesh.shape["dp"]),
        mesh=mesh,
        in_specs=specs + (P(),) * 7 + (split,),
        out_specs=(split,) + specs + (P(),) * 7,
        check_vma=False,
    )
```

```python
import functools

import jax
import jax.numpy as jnp
from jax import lax
from jax.experimental import pallas as pl
from jax.experimental.pallas import tpu as pltpu
from jax.sharding import PartitionSpec as P

D = 768
HD = 64
FF = 3072
GRID = 16
TOK = 256
RELS = 31
NZ, NX, NC = 4, 2, 2
RING = NZ * NX * NC
IMG = 2
PAIR = 2 * HD
CH = 64
EPS = 1e-06
F32 = jnp.float32
BF = jnp.bfloat16
MESH = pl.DeviceIdType.MESH
SCALE = HD ** (-0.5)
QKV_M, PROJ_M, UP_M, DOWN_M = range(4)


def nn(a, b):
    return lax.dot_general(a, b, (((1,), (0,)), ((), ())), preferred_element_type=F32)


def nt(a, b):
    return lax.dot_general(a, b, (((1,), (1,)), ((), ())), preferred_element_type=F32)


def tn(a, b):
    return lax.dot_general(a, b, (((0,), (0,)), ((), ())), preferred_element_type=F32)


def iota(shape, dim):
    return lax.broadcasted_iota(jnp.int32, shape, dim)


def one_hot(cond):
    return jnp.where(cond, 1.0, 0.0).astype(BF)


def mean_last(v):
    return jnp.sum(v, axis=-1, keepdims=True) * (1.0 / v.shape[-1])


def normalize(v):
    centred = v - mean_last(v)
    rstd = lax.rsqrt(mean_last(centred * centred) + EPS)
    return centred * rstd, rstd


def norm_back(grad, n, rstd, gain):
    e = grad * gain
    return (e - mean_last(e) - n * mean_last(e * n)) * rstd


def spread_rows(v):
    return jnp.concatenate(
        [pltpu.roll(v[g * GRID : (g + 1) * GRID], g, 1) if g else v[:GRID] for g in range(GRID)], axis=0
    )


def spread_cols(v):
    return jnp.concatenate(
        [
            pltpu.roll(v[g * GRID : (g + 1) * GRID], 0, 1, stride=1, stride_axis=0)
            for g in range(GRID)
        ],
        axis=0,
    )


NAMES_IN = (
    "tok", "cot", "sq", "sp", "su", "sd",
    "qvb", "pjb", "upb", "dnb", "g1", "b1",
    "g2", "b2", "relr", "relc",
)
NAMES_OUT = (
    "o_blk", "o_gtok", "o_gq", "o_gp", "o_gu", "o_gd",
    "o_sm", "o_rel",
)


def scratch_table(width, hid):
    pairs = width // PAIR
    half = TOK // 2
    shards = [(3, D // RING, width), (width // RING, D), (D // RING, hid), (hid // RING, D)]
    table = {
        "XT": ((IMG, TOK, D), BF),
        "CT": ((IMG, TOK, D), BF),
        "WPB": ((width, D), BF),
        "FL": ((IMG, TOK, D), BF),
        "QKV": ((3, pairs, IMG, TOK, PAIR), BF),
        "PT": ((pairs, IMG, 2, TOK, TOK), BF),
        "MX": ((IMG, TOK, width), BF),
        "AP": ((IMG, TOK, D), BF),
        "APR": ((IMG, TOK, D), BF),
        "MID": ((IMG, TOK, D), F32),
        "N2": ((IMG, TOK, D), F32),
        "RS2": ((IMG, TOK, 128), F32),
        "SEC": ((IMG, TOK, D), BF),
        "ACT": ((IMG, TOK, hid), BF),
        "GEL": ((IMG, TOK, hid), BF),
        "DP": ((IMG, TOK, D), BF),
        "DPR": ((IMG, half, D), BF),
        "GPRE": ((IMG, TOK, hid), BF),
        "GS": ((IMG, TOK, D), BF),
        "GSR": ((IMG, TOK, D), BF),
        "GM": ((IMG, half, D), F32),
        "MIDL": ((IMG, TOK, D), BF),
        "GMX": ((IMG, TOK, width), BF),
        "GQKV": ((3, IMG, TOK, width), BF),
        "GF": ((IMG, TOK, D), BF),
        "GFR": ((IMG, half, D), BF),
        "RG": ((PAIR, PAIR), F32),
        "TBF": ((PAIR, PAIR), BF),
        "TBB": ((PAIR, PAIR), BF),
        "OHF": ((TOK, PAIR), BF),
        "OHB": ((TOK, PAIR), BF),
        "MSK": ((4, 16, PAIR), BF),
        "PAR": ((6, 1, D), F32),
        "UPB": ((1, hid), F32),
        "S0": ((4, 8, D), F32),
        "S1": ((4, 2, D), F32),
        "S2": ((4, 64, 128), F32),
        "S3": ((4, 2, D), F32),
        "R0": ((7, 8, D), F32),
        "R1": ((7, 2, D), F32),
        "R2": ((7, 64, 128), F32),
        "R3": ((7, 2, D), F32),
    }
    for i, shard in enumerate(shards):
        table[f"W{i}"] = ((NZ, NX, NC) + shard, BF)
        table[f"G{i}"] = ((NZ, NX, NC) + shard, BF)
        table[f"C{i}"] = ((NZ, NX) + shard, BF)
        table[f"X{i}"] = ((NZ,) + shard, BF)
        table[f"Z{i}"] = ((NZ - 1,) + shard, BF)
    sems = {
        "agz": (4, 3),
        "agx": (4, 4),
        "agc": (4, 8),
        "ysem": (10,),
        "rsc": (4,),
        "rsx": (4, 4),
        "rsz": (4, 3),
        "ars": (4, 7),
    }
    return table, sems, shards


class Refs:
    pass


def block_kernel(ratio, width, hid, names, *refs):
    k = Refs()
    for name, ref in zip(names, refs):
        setattr(k, name, ref)
    pairs = width // PAIR
    half = TOK // 2
    dp = lax.axis_index("dp")
    t = lax.axis_index("tensor")
    sub = lax.rem(dp, ratio)
    s = dp // ratio
    z, x, c = s // (NX * NC), lax.rem(s // NC, NX), lax.rem(s, NC)

    def device(zz, xx, cc, tt=t):
        return (((zz * NX + xx) * NC + cc) * ratio + sub, tt)

    z_of = (z, z + 1 - 2 * lax.rem(z, 2), lax.rem(z + 2, NZ), NZ - 1 - z)
    core_peer, x_peer, y_peer = device(z, x, 1 - c), device(z, 1 - x, c), device(z, x, c, 1 - t)
    xy_peer = device(z, 1 - x, c, 1 - t)
    z_peer = [device(zz, x, c) for zz in z_of]
    own0 = pl.multiple_of(t * half, half)
    other0 = pl.multiple_of((1 - t) * half, half)

    def remote(src, dst, sems, idx, peer):
        return pltpu.make_async_remote_copy(
            src_ref=src,
            dst_ref=dst,
            send_sem=getattr(k, sems + "_s").at[idx],
            recv_sem=getattr(k, sems + "_r").at[idx],
            device_id=peer,
            device_id_type=MESH,
        )

    shard_in = [k.sq, k.sp, k.su, k.sd]
    W = [k.W0, k.W1, k.W2, k.W3]
    G = [k.G0, k.G1, k.G2, k.G3]
    C = [k.C0, k.C1, k.C2, k.C3]
    X = [k.X0, k.X1, k.X2, k.X3]
    Z = [k.Z0, k.Z1, k.Z2, k.Z3]

    def ag_z(m, i):
        return remote(shard_in[m], W[m].at[z, x, c], "agz", (m, i - 1), z_peer[i])

    def ag_x(m, i):
        src = shard_in[m] if i == 0 else W[m].at[z_of[i], x, c]
        return remote(src, W[m].at[z_of[i], x, c], "agx", (m, i), x_peer)

    def ag_c(m, i, other):
        xx = 1 - x if other else x
        src = shard_in[m] if i == 0 and not other else W[m].at[z_of[i], xx, c]
        return remote(src, W[m].at[z_of[i], xx, c], "agc", (m, i + 4 * other), core_peer)

    def ag_send(m, slots):
        for i in slots:
            ag_z(m, i).start()

    def ag_own(m):
        ag_x(m, 0).start()
        ag_c(m, 0, 0).start()

    def ag_pass(m, slots):
        for i in slots:
            ag_z(m, i).wait_recv()
            ag_x(m, i).start()
            ag_c(m, i, 0).start()

    def ag_cross(m, slots=(0, 1, 2, 3)):
        for i in slots:
            ag_x(m, i).wait_recv()
            ag_c(m, i, 1).start()

    def ag_done(m):
        for other in (0, 1):
            for i in range(NZ):
                ag_c(m, i, other).wait_recv()

    def rs_core(m):
        return remote(G[m].at[:, :, 1 - c], C[m], "rsc", (m,), core_peer)

    def rs_x(m, i):
        return remote(G[m].at[z_of[i], 1 - x, c], X[m].at[i], "rsx", (m, i), x_peer)

    def rs_z(m, i):
        return remote(G[m].at[z_of[i], x, c], Z[m].at[i - 1], "rsz", (m, i - 1), z_peer[i])

    def add_into(dst, where, src, which):
        if len(dst.shape) - len(where) == 3:
            for j in range(3):
                dst[(*where, j)] = dst[(*where, j)] + src[(*which, j)]
        else:
            dst[where] = dst[where] + src[which]

    def rs_core_done(m, starts=(2, 3, 1, 0)):
        rs_core(m).wait_recv()

        @pl.loop(0, NZ * NX)
        def _(i):
            zz, xx = i // NX, lax.rem(i, NX)
            add_into(G[m], (zz, xx, c), C[m], (zz, xx))

        rs_cross(m, starts)

    def rs_cross(m, slots):
        for i in slots:
            rs_x(m, i).start()

    def rs_pass(m, slots):
        for i in slots:
            rs_x(m, i).wait_recv()
            add_into(G[m], (z_of[i], x, c), X[m], (i,))
            if i:
                rs_z(m, i).start()

    def rs_done(m, out):
        for i in (1, 2, 3):
            rs_z(m, i).wait_recv()
        parts = range(3) if m == QKV_M else (None,)
        for j in parts:
            at = () if j is None else (j,)
            total = G[m][(z, x, c, *at)].astype(F32)
            for i in range(3):
                total = total + Z[m][(i, *at)].astype(F32)
            if j is None:
                out[...] = total
            else:
                out[j] = total

    S = [k.S0, k.S1, k.S2, k.S3]
    R = [k.R0, k.R1, k.R2, k.R3]
    hops = ((0,), (1, 2, 3), (4, 5, 6))

    def ar(b, i):
        step = 0 if i == 0 else 1 if i < 4 else 2
        peer = ([core_peer, x_peer, y_peer, xy_peer] + z_peer[1:])[i]
        return remote(S[b].at[step], R[b].at[i], "ars", (b, i), peer)

    def ar_send(step, *which):
        for b in which:
            for i in hops[step]:
                ar(b, i).start()

    def ar_done(step, *which):
        for b in which:
            for i in hops[step]:
                ar(b, i).wait_recv()
            if step == 0:
                S[b][1] = S[b][0] + R[b][0]
            else:
                first, i = S[b][step], hops[step][0]
                S[b][step + 1] = (first + R[b][i]) + (R[b][i + 1] + R[b][i + 2])

    def y_rows(img, base):
        return (img, pl.ds(base, half))

    def y_tok():
        return remote(k.tok, k.XT.at[:, pl.ds(own0, half)], "ysem", (0,), y_peer)

    def y_cot():
        return remote(k.cot, k.CT.at[:, pl.ds(own0, half)], "ysem", (1,), y_peer)

    def y_attn(img):
        return remote(k.AP.at[img], k.APR.at[img], "ysem", (2 + img,), y_peer)

    def y_mlp(img):
        return remote(k.DP.at[img, pl.ds(other0, half)], k.DPR.at[img], "ysem", (4 + img,), y_peer)

    def y_sec(img):
        return remote(k.GS.at[img], k.GSR.at[img], "ysem", (6 + img,), y_peer)

    def y_first(img):
        return remote(k.GF.at[img, pl.ds(other0, half)], k.GFR.at[img], "ysem", (8 + img,), y_peer)

    def rows(base, i):
        return pl.ds(pl.multiple_of(base + i * CH, CH), CH)

    barrier = pltpu.get_barrier_semaphore()
    peers = [core_peer, x_peer, y_peer, xy_peer] + z_peer[1:]
    for peer in peers:
        pl.semaphore_signal(barrier, inc=1, device_id=peer, device_id_type=MESH)
    pl.semaphore_wait(barrier, len(peers))

    ag_send(QKV_M, (1, 2))
    y_tok().start()
    for m in range(4):
        ag_own(m)

    for row, ref in enumerate((k.g1, k.b1, k.g2, k.b2, k.pjb, k.dnb)):
        k.PAR[row] = ref[...].reshape(1, D)
    g1, b1, g2, b2, pjb, dnb = (k.PAR.at[row] for row in range(6))
    k.UPB[...] = k.upb[pl.ds(pl.multiple_of(t * hid, 128), hid)].reshape(1, hid)
    lane = iota((TOK, PAIR), 1)
    lane64 = lax.rem(lane, HD)
    urow, ucol = iota((TOK, PAIR), 0) // GRID, lax.rem(iota((TOK, PAIR), 0), GRID)
    shifted = lax.rem(lane + (PAIR - GRID + 1), HD)
    seg, pos = shifted // GRID, lax.rem(shifted, GRID)
    k.OHF[...] = one_hot(((seg < 2) & (urow == pos)) | ((seg >= 2) & (ucol == pos)))
    k.OHB[...] = one_hot(
        ((lane64 < GRID) & (urow == GRID - 1 - lane64))
        | ((lane64 >= 2 * GRID) & (lane64 < 3 * GRID) & (ucol == 3 * GRID - 1 - lane64))
    )
    mlane = iota((16, PAIR), 1)
    in_first = mlane < HD
    ext_first = (mlane >= GRID - 1) & (mlane < HD + GRID - 1)
    k.MSK[0] = one_hot(in_first)
    k.MSK[1] = one_hot(mlane >= HD)
    k.MSK[2] = one_hot(ext_first)
    k.MSK[3] = one_hot((mlane < GRID - 1) | (mlane >= HD + GRID - 1))
    tl, td = iota((PAIR, RELS), 0), iota((PAIR, RELS), 1)
    fwd_tab = jnp.zeros((PAIR, PAIR), F32)
    bwd_tab = jnp.zeros((PAIR, PAIR), F32)
    for head in range(2):
        place = one_hot(iota((HD, PAIR), 1) == iota((HD, PAIR), 0) + head * HD)
        for base, rel in ((0, k.relr), (32, k.relc)):
            wide = nn(rel[...], place).astype(BF)
            at = tl - (head * HD + base)
            fwd_tab = fwd_tab + nn(one_hot(at == RELS - 1 - td), wide)
            bwd_tab = bwd_tab + nn(one_hot(at == td), wide)
    k.TBF[...] = fwd_tab.astype(BF)
    k.TBB[...] = bwd_tab.astype(BF)
    k.S0[0] = jnp.zeros((8, D), F32)
    k.S1[0] = jnp.zeros((2, D), F32)
    k.S3[0] = jnp.zeros((2, D), F32)
    k.RG[...] = jnp.zeros((PAIR, PAIR), F32)

    def first_norm(base):
        @pl.loop(0, IMG)
        def _(img):
            @pl.loop(0, half // CH)
            def _(i):
                at = rows(base, i)
                n, _ = normalize(k.XT[img, at].astype(F32))
                k.FL[img, at] = (n * g1[...] + b1[...]).astype(BF)

    for img in range(IMG):
        k.XT[img, pl.ds(own0, half)] = k.tok[img]
        k.CT[img, pl.ds(own0, half)] = k.cot[img]
    first_norm(own0)
    ag_send(QKV_M, (3,))
    for m in range(4):
        W[m][z, x, c] = shard_in[m][...]
    ag_pass(QKV_M, (1, 2))
    ag_send(PROJ_M, (1, 2, 3))
    ag_pass(QKV_M, (3,))
    ag_send(UP_M, (1, 2))
    y_tok().wait_recv()
    y_cot().start()
    first_norm(other0)
    ag_cross(QKV_M)
    ag_done(QKV_M)

    lanes_w = pl.ds(pl.multiple_of(t * width, 128), width)
    for i in range(3):

        @pl.loop(0, IMG)
        def _(img):
            out = nn(k.FL[img], W[0][:, :, :, i].reshape(D, width))
            if i != 1:
                out = out + k.qvb[i // 2 : i // 2 + 1, lanes_w]
            low = out.astype(BF)
            for p in range(pairs):
                k.QKV[i, p, img] = low[:, p * PAIR : (p + 1) * PAIR]

    ag_pass(PROJ_M, (1, 2, 3))
    ag_send(UP_M, (3,))

    def head_mask(i):
        return k.MSK[i][0:1]

    def attend(step):
        img, p = step // pairs, lax.rem(step, pairs)
        q, key, val = k.QKV[0, p, img], k.QKV[1, p, img], k.QKV[2, p, img]
        qr = nt(q, k.TBF[...])
        ext = jnp.where(
            (lane64 >= 15) & (lane64 < 31),
            spread_rows(qr),
            jnp.where((lane64 >= 47) & (lane64 < 63), spread_cols(qr), 0.0),
        )
        high = ext.astype(BF).astype(F32)
        ext = (high + pltpu.roll(ext - high, GRID, 1)).astype(BF)
        k_ext = jnp.concatenate([key, k.OHF[...]], axis=1)
        probs, vals = [], []
        for head in range(2):
            q_ext = jnp.concatenate(
                [q * (head_mask(head) * SCALE).astype(BF), ext * head_mask(2 + head)], axis=1
            )
            scores = nt(k_ext, q_ext)
            e = jnp.exp(scores - jnp.max(scores, axis=0, keepdims=True))
            low = (e * (1.0 / jnp.sum(e, axis=0, keepdims=True))).astype(BF)
            k.PT[p, img, head] = low
            probs.append(low)
            vals.append(val * head_mask(head))
        mixed = tn(jnp.concatenate(probs, axis=0), jnp.concatenate(vals, axis=0))
        k.MX[img, :, pl.ds(pl.multiple_of(p * PAIR, PAIR), PAIR)] = mixed.astype(BF)

    def project(img):
        for j in range(D // 256):
            cols = slice(j * 256, (j + 1) * 256)
            k.AP[img, :, cols] = nn(k.MX[img], k.WPB[:, cols]).astype(BF)
        y_attn(img).start()

    @pl.loop(0, pairs)
    def _(step):
        attend(step)

    ag_pass(UP_M, (1, 2))
    ag_send(DOWN_M, (1, 2))
    ag_cross(PROJ_M)
    ag_done(PROJ_M)

    @pl.loop(0, RING)
    def _(i):
        zz, xx, cc = i // (NX * NC), lax.rem(i // NC, NX), lax.rem(i, NC)
        k.G1F[pl.ds(pl.multiple_of(i * (width // RING), 8), width // RING)] = W[1][zz, xx, cc].astype(F32)

    k.WPB[...] = k.G1F[...].astype(BF)
    project(0)

    @pl.loop(pairs, 2 * pairs)
    def _(step):
        attend(step)

    ag_pass(UP_M, (3,))
    ag_send(DOWN_M, (3,))
    project(1)
    ag_pass(DOWN_M, (1, 2))
    ag_cross(UP_M)
    ag_done(UP_M)

    def second(img):
        y_attn(img).wait_recv()

        @pl.loop(0, TOK // CH)
        def _(i):
            at = rows(0, i)
            mid = (
                k.XT[img, at].astype(F32)
                + k.AP[img, at].astype(F32)
                + k.APR[img, at].astype(F32)
                + pjb[...]
            )
            k.MID[img, at] = mid
            n, rstd = normalize(mid)
            k.N2[img, at] = n
            k.RS2[img, at] = jnp.broadcast_to(rstd, (CH, 128))
            k.SEC[img, at] = (n * g2[...] + b2[...]).astype(BF)

        @pl.loop(0, hid // 256)
        def _(j):
            cols = pl.ds(pl.multiple_of(j * 256, 256), 256)
            bias = k.UPB[:, cols]
            pre = nn(k.SEC[img], W[2][:, :, :, :, cols].reshape(D, 256)) + bias
            phi = 0.5 + 0.5 * lax.erf(pre * 0.7071067811865476)
            k.ACT[img, :, cols] = (pre * phi).astype(BF)
            k.GEL[img, :, cols] = (phi + pre * (0.3989422804014327 * jnp.exp(-0.5 * pre * pre))).astype(BF)

    second(0)
    ag_pass(DOWN_M, (3,))
    ag_cross(DOWN_M)
    second(1)
    ag_done(DOWN_M)

    def down(img):
        @pl.loop(0, D // 256)
        def _(j):
            cols = pl.ds(pl.multiple_of(j * 256, 256), 256)
            k.DP[img, :, cols] = nn(k.ACT[img], W[3][:, :, :, :, cols].reshape(hid, 256)).astype(BF)

    y_cot().wait_recv()

    tile = hid // NZ

    @pl.loop(0, NZ)
    def _(m):
        lhs = k.ACT[:, :, pl.ds(pl.multiple_of(m * tile, 128), tile)].reshape(IMG * TOK, tile)
        for j in range(D // 256):
            cols = slice(j * 256, (j + 1) * 256)
            out = tn(lhs, k.CT[:, :, cols].reshape(IMG * TOK, 256)).astype(BF)
            G[3][m, :, :, :, cols] = out.reshape(NX, NC, hid // RING, 256)

    rs_core(DOWN_M).start()

    per_row = D // tile
    for img in range(IMG):

        @pl.loop(0, NZ)
        def _(m):
            cols = pl.ds(pl.multiple_of(m * tile, 128), tile)
            grad = nt(k.CT[img], W[3][m].reshape(tile, D)) * k.GEL[img, :, cols].astype(F32)
            low = grad.astype(BF)
            k.GPRE[img, :, cols] = low
            row = pl.ds(4 + t * (hid // D) + m // per_row, 1)
            lanes = pl.ds(pl.multiple_of(lax.rem(m, per_row) * tile, 128), tile)
            k.S0[0, row, lanes] = k.S0[0, row, lanes] + jnp.sum(low.astype(F32), axis=0, keepdims=True)

        @pl.loop(0, 2)
        def _(j):
            w = W[2][pl.ds(j * 2, 2)].reshape(D // 2, hid)
            k.GS[img, :, pl.ds(pl.multiple_of(j * (D // 2), 128), D // 2)] = nt(k.GPRE[img], w).astype(BF)

        y_sec(img).start()

    rs_core_done(DOWN_M)

    @pl.loop(0, hid // 256)
    def _(j):
        cols = pl.ds(pl.multiple_of(j * 256, 256), 256)
        rhs = k.GPRE[:, :, cols].reshape(IMG * TOK, 256)
        for m in range(2):
            lhs = k.SEC[:, :, m * (D // 2) : (m + 1) * (D // 2)].reshape(IMG * TOK, D // 2)
            out = tn(lhs, rhs).astype(BF)
            G[2][2 * m : 2 * m + 2, :, :, :, cols] = out.reshape(2, NX, NC, D // RING, 256)

    rs_core(UP_M).start()
    down(0)
    down(1)
    rs_core_done(UP_M)

    def middle_back(img, base, own):
        zero = jnp.zeros((1, D), F32)

        def chunk(i, sums):
            at = rows(base, i)
            grad = k.GS[img, at].astype(F32) + k.GSR[img, at].astype(F32)
            n = k.N2[img, at]
            rstd = jnp.concatenate([k.RS2[img, at]] * (D // 128), axis=1)
            cot = k.CT[img, at].astype(F32)
            gm = cot + norm_back(grad, n, rstd, g2[...])
            k.MIDL[img, at] = gm.astype(BF)
            if own:
                k.GM[img, rows(0, i)] = gm
                terms = (grad * n, grad, gm, cot)
                sums = tuple(a + jnp.sum(b, axis=0, keepdims=True) for a, b in zip(sums, terms))
            return sums

        return lax.fori_loop(0, half // CH, chunk, (zero,) * 4 if own else ())

    def middle(img):
        y_sec(img).wait_recv()
        sums = middle_back(img, own0, True)
        for row, value in enumerate(sums):
            k.S0[0, row : row + 1] = k.S0[0, row : row + 1] + value
        middle_back(img, other0, False)
        k.GMX[img] = nt(k.MIDL[img], k.WPB[...]).astype(BF)

    def attend_back(step):
        img, p = step // pairs, lax.rem(step, pairs)
        cols = pl.ds(pl.multiple_of(p * PAIR, PAIR), PAIR)
        q, key, val = k.QKV[0, p, img], k.QKV[1, p, img], k.QKV[2, p, img]
        gmx = k.GMX[img, :, cols]
        pts, gss, gms, qs, kes = [], [], [], [], []
        for head in range(2):
            m = head_mask(head)
            low = k.PT[p, img, head]
            probs = low.astype(F32)
            gp = nt(val * m, gmx)
            inner = jnp.sum(gp * probs, axis=0, keepdims=True)
            pts.append(low)
            gss.append((probs * (gp - inner)).astype(BF))
            gms.append(gmx * m)
            qs.append(q * (m * SCALE).astype(BF))
            kes.append(jnp.concatenate([key * (m * SCALE).astype(BF), k.OHB[...] * m], axis=1))
        grad_v = nn(jnp.concatenate(pts, axis=1), jnp.concatenate(gms, axis=0))
        grad_k = nn(jnp.concatenate(gss, axis=1), jnp.concatenate(qs, axis=0))
        both = tn(jnp.concatenate(gss, axis=0), jnp.concatenate(kes, axis=0))
        rel = both[:, PAIR:]
        rel = jnp.where(lane64 < 32, spread_rows(rel), spread_cols(rel))
        high = rel.astype(BF)
        rest = (rel - high.astype(F32)).astype(BF)
        grad_q = both[:, :PAIR] + nn(
            jnp.concatenate([high, rest], axis=1), jnp.concatenate([k.TBB[...]] * 2, axis=0)
        )
        k.RG[...] += tn(jnp.concatenate([high, rest], axis=0), jnp.concatenate([q, q], axis=0))
        lanes = pl.ds(pl.multiple_of(t * width + p * PAIR, PAIR), PAIR)
        for i, grad in enumerate((grad_q, grad_k, grad_v)):
            low = grad.astype(BF)
            k.GQKV[i, img, :, cols] = low
            if i != 1:
                row = i // 2
                k.S1[0, row : row + 1, lanes] = k.S1[0, row : row + 1, lanes] + jnp.sum(
                    low.astype(F32), axis=0, keepdims=True
                )

    middle(0)

    @pl.loop(0, pairs)
    def _(step):
        attend_back(step)

    rs_pass(DOWN_M, (2, 3))
    middle(1)
    ar_send(0, 0)
    for img in range(IMG):
        y_mlp(img).start()

    for j in range(D // 256):
        cols = slice(j * 256, (j + 1) * 256)
        out = tn(k.MX[...].reshape(IMG * TOK, width), k.MIDL[:, :, cols].reshape(IMG * TOK, 256))
        G[1][:, :, :, :, cols] = out.reshape(NZ, NX, NC, width // RING, 256).astype(BF)
    rs_core(PROJ_M).start()
    rs_pass(DOWN_M, (1, 0))
    ar_done(0, 0)
    ar_send(1, 0)

    @pl.loop(pairs, 2 * pairs)
    def _(step):
        attend_back(step)

    rg = k.RG[...]
    turned = pltpu.roll(rg, HD, 1)
    k.S2[0, 0:32] = rg[0:32] + turned[64:96]
    k.S2[0, 32:64] = rg[32:64] + turned[96:128]
    ar_send(0, 1, 2)

    for i in range(3):

        @pl.loop(0, 2)
        def _(m):
            lhs = k.FL[:, :, pl.ds(pl.multiple_of(m * (D // 2), 128), D // 2)].reshape(IMG * TOK, D // 2)
            out = tn(lhs, k.GQKV[i].reshape(IMG * TOK, width)).astype(BF)
            G[0][pl.ds(2 * m, 2), :, :, i] = out.reshape(2, NX, NC, D // RING, width)

    rs_core(QKV_M).start()
    rs_core_done(PROJ_M)

    for img in range(IMG):

        @pl.loop(0, 2)
        def _(m):
            total = jnp.zeros((TOK, D // 2), F32)
            for i in range(3):
                total = total + nt(k.GQKV[i, img], W[0][pl.ds(2 * m, 2), :, :, i].reshape(D // 2, width))
            k.GF[img, :, pl.ds(pl.multiple_of(m * (D // 2), 128), D // 2)] = total.astype(BF)

        y_first(img).start()
        if img == 0:
            rs_pass(UP_M, (2, 3, 1, 0))
            rs_core_done(QKV_M, (2, 3))
            ar_done(0, 1, 2)
            ar_send(1, 1, 2)
            ar_done(1, 0)
            ar_send(2, 0)

    rs_pass(PROJ_M, (2, 3, 1, 0))
    rs_cross(QKV_M, (1, 0))
    rs_done(DOWN_M, k.o_gd)
    rs_pass(QKV_M, (2, 3))
    ar_done(1, 1, 2)
    ar_send(2, 1, 2)

    for img in range(IMG):
        y_mlp(img).wait_recv()
        y_first(img).wait_recv()

        def finish(i, sums):
            at, here = rows(own0, i), rows(0, i)
            k.o_blk[img, here] = (
                k.MID[img, at] + k.DP[img, at].astype(F32) + k.DPR[img, here].astype(F32) + dnb[...]
            ).astype(BF)
            n, rstd = normalize(k.tok[img, here].astype(F32))
            grad = k.GF[img, at].astype(F32) + k.GFR[img, here].astype(F32)
            k.o_gtok[img, here] = k.GM[img, here] + norm_back(grad, n, rstd, g1[...])
            terms = (grad * n, grad)
            return tuple(a + jnp.sum(b, axis=0, keepdims=True) for a, b in zip(sums, terms))

        sums = lax.fori_loop(0, half // CH, finish, (jnp.zeros((1, D), F32),) * 2)
        for row, value in enumerate(sums):
            k.S3[0, row : row + 1] = k.S3[0, row : row + 1] + value

    ar_send(0, 3)
    rs_pass(QKV_M, (1, 0))
    ar_done(0, 3)
    ar_send(1, 3)
    rs_done(UP_M, k.o_gu)
    ar_done(2, 0)
    ar_done(1, 3)
    ar_send(2, 3)
    rs_done(PROJ_M, k.o_gp)
    ar_done(2, 1, 2)
    k.o_sm[0:8] = k.S0[3]
    k.o_sm[8:10] = k.S1[3]
    k.o_rel[...] = k.S2[3]
    ar_done(2, 3)
    k.o_sm[10:12] = k.S3[3]
    rs_done(QKV_M, k.o_gq)

    for m in range(4):
        for i in (1, 2, 3):
            ag_z(m, i).wait_send()
            rs_z(m, i).wait_send()
        for i in range(4):
            ag_x(m, i).wait_send()
            ag_c(m, i, 0).wait_send()
            ag_c(m, i, 1).wait_send()
            rs_x(m, i).wait_send()
        rs_core(m).wait_send()
    for copy in (y_tok(), y_cot()):
        copy.wait_send()
    for img in range(IMG):
        for make in (y_attn, y_mlp, y_sec, y_first):
            make(img).wait_send()
    for b in range(4):
        for i in range(7):
            ar(b, i).wait_send()


def fused_block(ratio, args):
    width, hid = args[2].shape[2], args[4].shape[1]
    table, sems, shards = scratch_table(width, hid)
    table["G1F"] = ((width, D), F32)
    names = list(NAMES_IN) + list(NAMES_OUT) + list(table)
    scratch = [pltpu.VMEM(shape, kind) for shape, kind in table.values()]
    for name, shape in sems.items():
        names += [name + "_s", name + "_r"]
        scratch += [pltpu.SemaphoreType.DMA(shape)] * 2
    tok = args[0].shape
    outs = [(tok, BF), (tok, F32)] + [(shape, F32) for shape in shards] + [((16, D), F32), ((64, 128), F32)]
    vmem = pl.BlockSpec(memory_space=pltpu.VMEM)
    return pl.pallas_call(
        functools.partial(block_kernel, ratio, width, hid, names),
        out_shape=[jax.ShapeDtypeStruct(shape, kind) for shape, kind in outs],
        in_specs=[vmem] * len(NAMES_IN),
        out_specs=[vmem] * len(outs),
        scratch_shapes=scratch,
        compiler_params=pltpu.CompilerParams(
            collective_id=0, has_side_effects=True, vmem_limit_bytes=62 << 20
        ),
        name="fused_block",
    )(*args)


def finish_kernel(*refs):
    big, (small, rel), outs = refs[:6], refs[6:8], refs[8:24]
    held, sem_in, sem = refs[24:30], refs[30], refs[31]
    where = (0, 1, 2, 4, 6, 8)
    loads = [pltpu.make_async_copy(src, dst, sem_in.at[n]) for n, (src, dst) in enumerate(zip(big, held))]
    copies = [pltpu.make_async_copy(src, outs[i], sem.at[n]) for n, (src, i) in enumerate(zip(held, where))]
    for copy in loads:
        copy.start()
    for load, copy in zip(loads, copies):
        load.wait()
        copy.start()
    outs[3][...] = small[8:10]
    for i, row in ((5, 2), (9, 3), (10, 10), (11, 11), (12, 0), (13, 1)):
        outs[i][...] = small[row : row + 1].reshape(D)
    for j in range(FF // D):
        outs[7][j * D : (j + 1) * D] = small[4 + j : 5 + j].reshape(D)
    outs[14][...] = rel[:RELS, :HD]
    outs[15][...] = rel[32 : 32 + RELS, :HD]
    for copy in copies:
        copy.wait()


def hand_out(block_out, grad_tokens, grads, small, rel):
    big = [block_out, grad_tokens, *grads]
    vec = jax.ShapeDtypeStruct((D,), F32)
    table = jax.ShapeDtypeStruct((RELS, HD), F32)
    like = [jax.ShapeDtypeStruct(v.shape, v.dtype) for v in big]
    outs = [like[0], like[1], like[2], jax.ShapeDtypeStruct((2, D), F32), like[3], vec, like[4],
            jax.ShapeDtypeStruct((FF,), F32), like[5], vec, vec, vec, vec, vec, table, table]
    vmem, whole = pl.BlockSpec(memory_space=pltpu.VMEM), pl.BlockSpec(memory_space=pl.ANY)
    return pl.pallas_call(
        finish_kernel,
        out_shape=outs,
        in_specs=[whole] * 6 + [vmem] * 2,
        out_specs=[whole if i in (0, 1, 2, 4, 6, 8) else vmem for i in range(16)],
        scratch_shapes=[pltpu.VMEM(v.shape, v.dtype) for v in big] + [pltpu.SemaphoreType.DMA((6,))] * 2,
        compiler_params=pltpu.CompilerParams(vmem_limit_bytes=62 << 20),
        name="hand_out",
    )(*big, small, rel)


def on_device(dp_size, *args):
    (tokens, w_qkv, qv_bias, w_proj, proj_bias, w_up, up_bias, w_down, down_bias,
     norm1_gain, norm1_shift, norm2_gain, norm2_shift, rel_rows, rel_cols, cotangent) = args
    ratio = dp_size // RING
    weights = [w_qkv, w_proj, w_up, w_down]
    dims = (1, 0, 0, 0)
    groups = [[i * ratio + j for j in range(ratio)] for i in range(RING)]
    across = [[i * ratio + j for i in range(RING)] for j in range(ratio)]
    if ratio > 1:
        weights = [
            lax.all_gather(w, "dp", axis=dim, tiled=True, axis_index_groups=groups)
            for w, dim in zip(weights, dims)
        ]
    outs = fused_block(
        ratio,
        (tokens, cotangent, *weights, qv_bias, proj_bias, up_bias, down_bias,
         norm1_gain, norm1_shift, norm2_gain, norm2_shift, rel_rows, rel_cols),
    )
    block_out, grad_tokens, *grads, small, rel = outs
    if ratio > 1:
        grads = [
            lax.psum_scatter(g, "dp", scatter_dimension=dim, tiled=True, axis_index_groups=groups)
            for g, dim in zip(grads, dims)
        ]
        small, rel = lax.psum((small, rel), "dp", axis_index_groups=groups)
    return hand_out(block_out, grad_tokens, grads, small, rel)


def solution(mesh):
    split = P("dp", "tensor", None)
    specs = (split, P(None, "dp", "tensor"), P(), P(("tensor", "dp"), None), P(), P("dp", "tensor"), P(),
             P(("tensor", "dp"), None))
    return jax.shard_map(
        functools.partial(on_device, mesh.shape["dp"]),
        mesh=mesh,
        in_specs=specs + (P(),) * 7 + (split,),
        out_specs=(split,) + specs + (P(),) * 7,
        check_vma=False,
    )
```

```python
import functools

import jax
import jax.numpy as jnp
from jax import lax
from jax.experimental import pallas as pl
from jax.experimental.pallas import tpu as pltpu
from jax.sharding import PartitionSpec as P

D = 768
HD = 64
FF = 3072
GRID = 16
TOK = 256
RELS = 31
NZ, NX, NC = 4, 2, 2
RING = NZ * NX * NC
IMG = 2
PAIR = 2 * HD
CH = 64
EPS = 1e-06
F32 = jnp.float32
BF = jnp.bfloat16
MESH = pl.DeviceIdType.MESH
SCALE = HD ** (-0.5)
QKV_M, PROJ_M, UP_M, DOWN_M = range(4)


def nn(a, b):
    return lax.dot_general(a, b, (((1,), (0,)), ((), ())), preferred_element_type=F32)


def nt(a, b):
    return lax.dot_general(a, b, (((1,), (1,)), ((), ())), preferred_element_type=F32)


def tn(a, b):
    return lax.dot_general(a, b, (((0,), (0,)), ((), ())), preferred_element_type=F32)


def iota(shape, dim):
    return lax.broadcasted_iota(jnp.int32, shape, dim)


def one_hot(cond):
    return jnp.where(cond, 1.0, 0.0).astype(BF)


def mean_last(v):
    return jnp.sum(v, axis=-1, keepdims=True) * (1.0 / v.shape[-1])


def normalize(v):
    centred = v - mean_last(v)
    rstd = lax.rsqrt(mean_last(centred * centred) + EPS)
    return centred * rstd, rstd


def norm_back(grad, n, rstd, gain):
    e = grad * gain
    return (e - mean_last(e) - n * mean_last(e * n)) * rstd


def spread_rows(v):
    return jnp.concatenate(
        [pltpu.roll(v[g * GRID : (g + 1) * GRID], g, 1) if g else v[:GRID] for g in range(GRID)], axis=0
    )


def spread_cols(v):
    return jnp.concatenate(
        [
            pltpu.roll(v[g * GRID : (g + 1) * GRID], 0, 1, stride=1, stride_axis=0)
            for g in range(GRID)
        ],
        axis=0,
    )


NAMES_IN = (
    "tok", "cot", "sq", "sp", "su", "sd",
    "qvb", "pjb", "upb", "dnb", "g1", "b1",
    "g2", "b2", "relr", "relc",
)
NAMES_OUT = (
    "o_blk", "o_gtok", "o_gq", "o_gp", "o_gu", "o_gd",
    "o_sm", "o_rel",
)


def scratch_table(width, hid):
    pairs = width // PAIR
    half = TOK // 2
    shards = [(3, D // RING, width), (width // RING, D), (D // RING, hid), (hid // RING, D)]
    gathered = [shards[0], (2,) + shards[1], shards[2], shards[3]]
    table = {
        "XT": ((IMG, TOK, D), BF),
        "CT": ((IMG, TOK, D), BF),
        "WPB": ((2, width, D), BF),
        "PSH": ((2, width // RING, D), BF),
        "N1": ((IMG, TOK, D), BF),
        "FL": ((IMG, TOK, D), BF),
        "QKV": ((3, pairs, IMG, TOK, PAIR), BF),
        "PT": ((pairs, IMG, 2, TOK, TOK), BF),
        "MX": ((2, IMG, TOK, width), BF),
        "MID": ((IMG, TOK, D), F32),
        "N2": ((IMG, TOK, D), F32),
        "RS2": ((IMG, TOK, 128), F32),
        "SEC": ((IMG, TOK, D), BF),
        "ACT": ((IMG, TOK, hid), BF),
        "GEL": ((IMG, TOK, hid), BF),
        "DP": ((IMG, TOK, D), BF),
        "DPR": ((IMG, half, D), BF),
        "GPRE": ((IMG, TOK, hid), BF),
        "GS": ((IMG, TOK, D), BF),
        "GSR": ((IMG, TOK, D), BF),
        "GM": ((IMG, half, D), F32),
        "MIDL": ((IMG, TOK, D), BF),
        "GMX": ((IMG, TOK, width), BF),
        "GQKV": ((3, IMG, TOK, width), BF),
        "GF": ((IMG, TOK, D), BF),
        "GFR": ((IMG, half, D), BF),
        "RG": ((PAIR, PAIR), F32),
        "TBF": ((PAIR, PAIR), BF),
        "TBB": ((PAIR, PAIR), BF),
        "OHF": ((TOK, PAIR), BF),
        "OHB": ((TOK, PAIR), BF),
        "MSK": ((4, 16, PAIR), BF),
        "PAR": ((6, 1, D), F32),
        "UPB": ((1, hid), F32),
        "S0": ((4, 8, D), F32),
        "S1": ((4, 4, D), F32),
        "S2": ((4, 32, 128), F32),
        "R0": ((7, 8, D), F32),
        "R1": ((7, 4, D), F32),
        "R2": ((7, 32, 128), F32),
    }
    for i, shard in enumerate(shards):
        table[f"W{i}"] = ((NZ, NX, NC) + gathered[i], BF)
        table[f"G{i}"] = ((NZ, NX, NC) + shard, BF)
        table[f"C{i}"] = ((NZ, NX) + shard, BF)
        table[f"X{i}"] = ((NZ,) + shard, BF)
        table[f"Z{i}"] = ((NZ - 1,) + shard, BF)
    sems = {
        "agz": (4, 3),
        "agh": (4, 4),
        "agx": (4, 4),
        "agc": (4, 8),
        "ysem": (11,),
        "rsc": (4,),
        "rsx": (4, 4),
        "rsz": (4, 3),
        "ars": (3, 7),
    }
    return table, sems, shards


class Refs:
    pass


def block_kernel(ratio, width, hid, names, *refs):
    k = Refs()
    for name, ref in zip(names, refs):
        setattr(k, name, ref)
    pairs = width // PAIR
    half = TOK // 2
    dp = lax.axis_index("dp")
    t = lax.axis_index("tensor")
    sub = lax.rem(dp, ratio)
    s = dp // ratio
    z, x, c = s // (NX * NC), lax.rem(s // NC, NX), lax.rem(s, NC)

    def device(zz, xx, cc, tt=t):
        return (((zz * NX + xx) * NC + cc) * ratio + sub, tt)

    z_of = (z, z + 1 - 2 * lax.rem(z, 2), lax.rem(z + 2, NZ), NZ - 1 - z)
    core_peer, x_peer, y_peer = device(z, x, 1 - c), device(z, 1 - x, c), device(z, x, c, 1 - t)
    xy_peer = device(z, 1 - x, c, 1 - t)
    z_peer = [device(zz, x, c) for zz in z_of]
    own0 = pl.multiple_of(t * half, half)
    other0 = pl.multiple_of((1 - t) * half, half)

    def remote(src, dst, sems, idx, peer):
        return pltpu.make_async_remote_copy(
            src_ref=src,
            dst_ref=dst,
            send_sem=getattr(k, sems + "_s").at[idx],
            recv_sem=getattr(k, sems + "_r").at[idx],
            device_id=peer,
            device_id_type=MESH,
        )

    shard_in = [k.sq, k.PSH, k.su, k.sd]
    W = [k.W0, k.W1, k.W2, k.W3]
    G = [k.G0, k.G1, k.G2, k.G3]
    C = [k.C0, k.C1, k.C2, k.C3]
    X = [k.X0, k.X1, k.X2, k.X3]
    Z = [k.Z0, k.Z1, k.Z2, k.Z3]

    side = z // 2
    relayed = (PROJ_M, UP_M, DOWN_M)
    middle_chip = (z == 1) | (z == 2)
    relay_of = (z, z_of[1], 2 - side, 3 - 3 * side)
    origin = [relay_of if m in relayed else z_of for m in range(4)]

    def piece(m, i, other=False):
        if i == 0 and not other:
            return shard_in[m]
        return W[m].at[origin[m][i], 1 - x if other else x, c]

    def ag_z(m, i):
        return remote(shard_in[m], W[m].at[z, x, c], "agz", (m, i - 1), z_peer[i])

    def ag_relay(m, n):
        i, arrives, peer = ((0, 2, 3), (1, 3, 3), (2, 2, 1), (3, 3, 1))[n]
        return pltpu.make_async_remote_copy(
            src_ref=piece(m, i),
            dst_ref=W[m].at[origin[m][i], x, c],
            send_sem=k.agh_s.at[m, n],
            recv_sem=k.agz_r.at[m, arrives - 1],
            device_id=z_peer[peer],
            device_id_type=MESH,
        )

    def relay(m, n):
        @pl.when(middle_chip)
        def _():
            ag_relay(m, n).start()

    def ag_x(m, i):
        return remote(piece(m, i), W[m].at[origin[m][i], x, c], "agx", (m, i), x_peer)

    def ag_c(m, i, other):
        xx = 1 - x if other else x
        return remote(piece(m, i, other), W[m].at[origin[m][i], xx, c], "agc", (m, i + 4 * other), core_peer)

    def ag_send(m, slots=(1,)):
        for i in slots:
            ag_z(m, i).start()
        if m in relayed:
            relay(m, 0)

    def ag_own(m):
        ag_x(m, 0).start()
        ag_c(m, 0, 0).start()

    def ag_pass(m, slots):
        for i in slots:
            ag_z(m, i).wait_recv()
            if m in relayed:
                relay(m, i)
            ag_x(m, i).start()
            ag_c(m, i, 0).start()

    def ag_pass_middle(*pairs):
        @pl.when(middle_chip)
        def _():
            for m, i in pairs:
                ag_z(m, i).wait_recv()
                ag_relay(m, i).start()
                ag_x(m, i).start()
                ag_c(m, i, 0).start()

    def ag_pass_end(*pairs):
        @pl.when(jnp.logical_not(middle_chip))
        def _():
            for m, i in pairs:
                ag_z(m, i).wait_recv()
                ag_x(m, i).start()
                ag_c(m, i, 0).start()

    def ag_cross(m, slots=(0, 1, 2, 3)):
        for i in slots:
            ag_x(m, i).wait_recv()
            ag_c(m, i, 1).start()

    def ag_done(m):
        for other in (0, 1):
            for i in range(NZ):
                ag_c(m, i, other).wait_recv()

    def rs_core(m):
        return remote(G[m].at[:, :, 1 - c], C[m], "rsc", (m,), core_peer)

    def rs_x(m, i):
        return remote(G[m].at[z_of[i], 1 - x, c], X[m].at[i], "rsx", (m, i), x_peer)

    def rs_z(m, i):
        return remote(G[m].at[z_of[i], x, c], Z[m].at[i - 1], "rsz", (m, i - 1), z_peer[i])

    def add_into(dst, where, src, which):
        if len(dst.shape) - len(where) == 3:
            for j in range(3):
                dst[(*where, j)] = dst[(*where, j)] + src[(*which, j)]
        else:
            dst[where] = dst[where] + src[which]

    def rs_core_done(m):
        rs_core(m).wait_recv()

        @pl.loop(0, NZ * NX)
        def _(i):
            zz, xx = i // NX, lax.rem(i, NX)
            add_into(G[m], (zz, xx, c), C[m], (zz, xx))

    queue = [(m, i) for m in (DOWN_M, UP_M, PROJ_M, QKV_M) for i in (2, 3, 1, 0)]
    fed, taken = list(queue), list(queue)

    def rs_feed(count):
        for _ in range(count):
            rs_x(*fed.pop(0)).start()

    def rs_take(count, feed=0):
        for _ in range(count):
            m, i = taken.pop(0)
            rs_x(m, i).wait_recv()
            if feed:
                rs_feed(1)
                feed -= 1
            add_into(G[m], (z_of[i], x, c), X[m], (i,))
            if i:
                rs_z(m, i).start()

    def rs_done(m, out):
        for i in (1, 2, 3):
            rs_z(m, i).wait_recv()
        parts = range(3) if m == QKV_M else (None,)
        for j in parts:
            at = () if j is None else (j,)
            total = G[m][(z, x, c, *at)].astype(F32)
            for i in range(3):
                total = total + Z[m][(i, *at)].astype(F32)
            if j is None:
                out[...] = total
            else:
                out[j] = total

    S = [k.S0, k.S1, k.S2]
    R = [k.R0, k.R1, k.R2]
    hops = ((0,), (1, 2, 3), (4, 5, 6))

    def ar(b, i):
        step = 0 if i == 0 else 1 if i < 4 else 2
        peer = ([core_peer, x_peer, y_peer, xy_peer] + z_peer[1:])[i]
        return remote(S[b].at[step], R[b].at[i], "ars", (b, i), peer)

    def ar_send(step, *which):
        for b in which:
            for i in hops[step]:
                ar(b, i).start()

    def ar_done(step, *which):
        for b in which:
            for i in hops[step]:
                ar(b, i).wait_recv()
            if step == 0:
                S[b][1] = S[b][0] + R[b][0]
            else:
                first, i = S[b][step], hops[step][0]
                S[b][step + 1] = (first + R[b][i]) + (R[b][i + 1] + R[b][i + 2])

    def y_rows(img, base):
        return (img, pl.ds(base, half))

    def y_tok():
        return remote(k.tok, k.XT.at[:, pl.ds(own0, half)], "ysem", (0,), y_peer)

    def y_cot():
        return remote(k.cot, k.CT.at[:, pl.ds(own0, half)], "ysem", (1,), y_peer)

    def y_attn(img):
        return remote(k.MX.at[t, img], k.MX.at[t, img], "ysem", (2 + img,), y_peer)

    def y_proj():
        return remote(k.sp, k.PSH.at[t], "ysem", (10,), y_peer)

    def y_mlp(img):
        return remote(k.DP.at[img, pl.ds(other0, half)], k.DPR.at[img], "ysem", (4 + img,), y_peer)

    def y_sec(img):
        return remote(k.GS.at[img], k.GSR.at[img], "ysem", (6 + img,), y_peer)

    def y_first(img):
        return remote(k.GF.at[img, pl.ds(other0, half)], k.GFR.at[img], "ysem", (8 + img,), y_peer)

    def rows(base, i):
        return pl.ds(pl.multiple_of(base + i * CH, CH), CH)

    barrier = pltpu.get_barrier_semaphore()
    peers = [core_peer, x_peer, y_peer, xy_peer] + z_peer[1:]
    for peer in peers:
        pl.semaphore_signal(barrier, inc=1, device_id=peer, device_id_type=MESH)
    pl.semaphore_wait(barrier, len(peers))

    ag_send(QKV_M, (1, 2))
    y_proj().start()
    y_tok().start()
    ag_own(QKV_M)

    for row, ref in enumerate((k.g1, k.b1, k.g2, k.b2, k.pjb, k.dnb)):
        k.PAR[row] = ref[...].reshape(1, D)
    g1, b1, g2, b2, pjb, dnb = (k.PAR.at[row] for row in range(6))
    k.UPB[...] = k.upb[pl.ds(pl.multiple_of(t * hid, 128), hid)].reshape(1, hid)
    lane = iota((TOK, PAIR), 1)
    lane64 = lax.rem(lane, HD)
    urow, ucol = iota((TOK, PAIR), 0) // GRID, lax.rem(iota((TOK, PAIR), 0), GRID)
    shifted = lax.rem(lane + (PAIR - GRID + 1), HD)
    seg, pos = shifted // GRID, lax.rem(shifted, GRID)
    k.OHF[...] = one_hot(((seg < 2) & (urow == pos)) | ((seg >= 2) & (ucol == pos)))
    k.OHB[...] = one_hot(
        ((lane64 < GRID) & (urow == GRID - 1 - lane64))
        | ((lane64 >= 2 * GRID) & (lane64 < 3 * GRID) & (ucol == 3 * GRID - 1 - lane64))
    )
    mlane = iota((16, PAIR), 1)
    in_first = mlane < HD
    ext_first = (mlane >= GRID - 1) & (mlane < HD + GRID - 1)
    k.MSK[0] = one_hot(in_first)
    k.MSK[1] = one_hot(mlane >= HD)
    k.MSK[2] = one_hot(ext_first)
    k.MSK[3] = one_hot((mlane < GRID - 1) | (mlane >= HD + GRID - 1))
    tl, td = iota((PAIR, RELS), 0), iota((PAIR, RELS), 1)
    fwd_tab = jnp.zeros((PAIR, PAIR), F32)
    bwd_tab = jnp.zeros((PAIR, PAIR), F32)
    for head in range(2):
        place = one_hot(iota((HD, PAIR), 1) == iota((HD, PAIR), 0) + head * HD)
        for base, rel in ((0, k.relr), (32, k.relc)):
            wide = nn(rel[...], place).astype(BF)
            at = tl - (head * HD + base)
            fwd_tab = fwd_tab + nn(one_hot(at == RELS - 1 - td), wide)
            bwd_tab = bwd_tab + nn(one_hot(at == td), wide)
    k.TBF[...] = fwd_tab.astype(BF)
    k.TBB[...] = bwd_tab.astype(BF)
    k.S0[0] = jnp.zeros((8, D), F32)
    k.S1[0] = jnp.zeros((4, D), F32)
    k.RG[...] = jnp.zeros((PAIR, PAIR), F32)

    def first_norm(base):
        @pl.loop(0, IMG)
        def _(img):
            @pl.loop(0, half // CH)
            def _(i):
                at = rows(base, i)
                n, _ = normalize(k.XT[img, at].astype(F32))
                k.N1[img, at] = n.astype(BF)
                k.FL[img, at] = (n * g1[...] + b1[...]).astype(BF)

    for img in range(IMG):
        k.XT[img, pl.ds(own0, half)] = k.tok[img]
        k.CT[img, pl.ds(own0, half)] = k.cot[img]
    k.PSH[t] = k.sp[...]
    first_norm(own0)
    ag_send(QKV_M, (3,))
    ag_own(UP_M)
    y_proj().wait_recv()
    ag_own(PROJ_M)
    for m in range(4):
        W[m][z, x, c] = shard_in[m][...]
    ag_pass(QKV_M, (1, 2))
    ag_send(UP_M)
    ag_pass(QKV_M, (3,))
    ag_send(PROJ_M)
    ag_own(DOWN_M)
    y_tok().wait_recv()
    y_cot().start()
    first_norm(other0)
    ag_pass(UP_M, (1,))
    ag_pass_middle((UP_M, 2))
    ag_cross(QKV_M)
    ag_done(QKV_M)

    lanes_w = pl.ds(pl.multiple_of(t * width, 128), width)
    for i in range(3):

        @pl.loop(0, IMG)
        def _(img):
            out = nn(k.FL[img], W[0][:, :, :, i].reshape(D, width))
            if i != 1:
                out = out + k.qvb[i // 2 : i // 2 + 1, lanes_w]
            low = out.astype(BF)
            for p in range(pairs):
                k.QKV[i, p, img] = low[:, p * PAIR : (p + 1) * PAIR]

    ag_pass(PROJ_M, (1,))
    ag_pass_end((UP_M, 2))
    ag_pass_middle((PROJ_M, 2), (UP_M, 3))
    ag_send(DOWN_M)

    def head_mask(i):
        return k.MSK[i][0:1]

    def attend(step):
        img, p = step // pairs, lax.rem(step, pairs)
        q, key, val = k.QKV[0, p, img], k.QKV[1, p, img], k.QKV[2, p, img]
        qr = nt(q, k.TBF[...])
        ext = jnp.where(
            (lane64 >= 15) & (lane64 < 31),
            spread_rows(qr),
            jnp.where((lane64 >= 47) & (lane64 < 63), spread_cols(qr), 0.0),
        )
        high = ext.astype(BF).astype(F32)
        ext = (high + pltpu.roll(ext - high, GRID, 1)).astype(BF)
        k_ext = jnp.concatenate([key, k.OHF[...]], axis=1)
        probs, vals = [], []
        for head in range(2):
            q_ext = jnp.concatenate(
                [q * (head_mask(head) * SCALE).astype(BF), ext * head_mask(2 + head)], axis=1
            )
            scores = nt(k_ext, q_ext)
            e = jnp.exp(scores - jnp.max(scores, axis=0, keepdims=True))
            low = (e * (1.0 / jnp.sum(e, axis=0, keepdims=True))).astype(BF)
            k.PT[p, img, head] = low
            probs.append(low)
            vals.append(val * head_mask(head))
        mixed = tn(jnp.concatenate(probs, axis=0), jnp.concatenate(vals, axis=0))
        k.MX[t, img, :, pl.ds(pl.multiple_of(p * PAIR, PAIR), PAIR)] = mixed.astype(BF)

    attend(0)
    attend(1)
    ag_pass_middle((PROJ_M, 3))
    ag_pass_end((PROJ_M, 2))
    attend(2)
    y_attn(0).start()
    attend(3)
    ag_pass(DOWN_M, (1,))
    ag_pass_end((UP_M, 3))
    ag_pass_middle((DOWN_M, 2))
    attend(4)
    ag_cross(UP_M, (0, 1))
    attend(5)
    y_attn(1).start()
    ag_pass_middle((DOWN_M, 3))
    ag_pass_end((PROJ_M, 3), (DOWN_M, 2))
    ag_cross(UP_M, (2, 3))
    ag_cross(PROJ_M)
    ag_done(PROJ_M)

    @pl.loop(0, RING)
    def _(i):
        zz, xx, cc = i // (NX * NC), lax.rem(i // NC, NX), lax.rem(i, NC)
        for tt in range(2):
            at = pl.ds(pl.multiple_of(tt * width + i * (width // RING), 8), width // RING)
            k.G1F[at] = W[1][zz, xx, cc, tt].astype(F32)

    k.WPB[...] = k.G1F[...].astype(BF).reshape(2, width, D)
    ag_done(UP_M)

    def second(img):
        y_attn(img).wait_recv()

        @pl.loop(0, D // 256)
        def _(j):
            cols = pl.ds(pl.multiple_of(j * 256, 256), 256)
            k.MID[img, :, cols] = nn(k.MX[0, img], k.WPB[0, :, cols]) + nn(k.MX[1, img], k.WPB[1, :, cols])

        @pl.loop(0, TOK // CH)
        def _(i):
            at = rows(0, i)
            mid = k.MID[img, at] + k.XT[img, at].astype(F32) + pjb[...]
            k.MID[img, at] = mid
            n, rstd = normalize(mid)
            k.N2[img, at] = n
            k.RS2[img, at] = jnp.broadcast_to(rstd, (CH, 128))
            k.SEC[img, at] = (n * g2[...] + b2[...]).astype(BF)

        @pl.loop(0, hid // 256)
        def _(j):
            cols = pl.ds(pl.multiple_of(j * 256, 256), 256)
            bias = k.UPB[:, cols]
            pre = nn(k.SEC[img], W[2][:, :, :, :, cols].reshape(D, 256)) + bias
            phi = 0.5 + 0.5 * lax.erf(pre * 0.7071067811865476)
            k.ACT[img, :, cols] = (pre * phi).astype(BF)
            k.GEL[img, :, cols] = (phi + pre * (0.3989422804014327 * jnp.exp(-0.5 * pre * pre))).astype(BF)

    second(0)
    ag_pass_end((DOWN_M, 3))
    ag_cross(DOWN_M, (0, 1))
    second(1)
    ag_cross(DOWN_M, (2, 3))

    def down(img):
        @pl.loop(0, D // 256)
        def _(j):
            cols = pl.ds(pl.multiple_of(j * 256, 256), 256)
            k.DP[img, :, cols] = nn(k.ACT[img], W[3][:, :, :, :, cols].reshape(hid, 256)).astype(BF)

    y_cot().wait_recv()

    tile = hid // NZ

    @pl.loop(0, NZ)
    def _(m):
        lhs = k.ACT[:, :, pl.ds(pl.multiple_of(m * tile, 128), tile)].reshape(IMG * TOK, tile)
        for j in range(D // 256):
            cols = slice(j * 256, (j + 1) * 256)
            out = tn(lhs, k.CT[:, :, cols].reshape(IMG * TOK, 256)).astype(BF)
            G[3][m, :, :, :, cols] = out.reshape(NX, NC, hid // RING, 256)

    rs_core(DOWN_M).start()

    per_row = D // tile
    ag_done(DOWN_M)

    def hidden_back(img):
        @pl.loop(0, NZ)
        def _(m):
            cols = pl.ds(pl.multiple_of(m * tile, 128), tile)
            grad = nt(k.CT[img], W[3][m].reshape(tile, D)) * k.GEL[img, :, cols].astype(F32)
            low = grad.astype(BF)
            k.GPRE[img, :, cols] = low
            row = pl.ds(4 + t * (hid // D) + m // per_row, 1)
            lanes = pl.ds(pl.multiple_of(lax.rem(m, per_row) * tile, 128), tile)
            k.S0[0, row, lanes] = k.S0[0, row, lanes] + jnp.sum(low.astype(F32), axis=0, keepdims=True)

        @pl.loop(0, 2)
        def _(j):
            w = W[2][pl.ds(j * 2, 2)].reshape(D // 2, hid)
            k.GS[img, :, pl.ds(pl.multiple_of(j * (D // 2), 128), D // 2)] = nt(k.GPRE[img], w).astype(BF)

        y_sec(img).start()

    hidden_back(0)
    rs_core_done(DOWN_M)
    rs_feed(2)
    hidden_back(1)
    rs_feed(1)

    @pl.loop(0, hid // 256)
    def _(j):
        cols = pl.ds(pl.multiple_of(j * 256, 256), 256)
        rhs = k.GPRE[:, :, cols].reshape(IMG * TOK, 256)
        for m in range(2):
            lhs = k.SEC[:, :, m * (D // 2) : (m + 1) * (D // 2)].reshape(IMG * TOK, D // 2)
            out = tn(lhs, rhs).astype(BF)
            G[2][2 * m : 2 * m + 2, :, :, :, cols] = out.reshape(2, NX, NC, D // RING, 256)

    rs_core(UP_M).start()
    rs_feed(1)
    down(0)
    down(1)
    rs_core_done(UP_M)
    rs_feed(1)
    rs_take(2, 1)

    def middle_back(img, base, own):
        zero = jnp.zeros((1, D), F32)

        def chunk(i, sums):
            at = rows(base, i)
            grad = k.GS[img, at].astype(F32) + k.GSR[img, at].astype(F32)
            n = k.N2[img, at]
            rstd = jnp.concatenate([k.RS2[img, at]] * (D // 128), axis=1)
            cot = k.CT[img, at].astype(F32)
            gm = cot + norm_back(grad, n, rstd, g2[...])
            k.MIDL[img, at] = gm.astype(BF)
            if own:
                k.GM[img, rows(0, i)] = gm
                terms = (grad * n, grad, gm, cot)
                sums = tuple(a + jnp.sum(b, axis=0, keepdims=True) for a, b in zip(sums, terms))
            return sums

        return lax.fori_loop(0, half // CH, chunk, (zero,) * 4 if own else ())

    def middle(img):
        y_sec(img).wait_recv()
        sums = middle_back(img, own0, True)
        for row, value in enumerate(sums):
            k.S0[0, row : row + 1] = k.S0[0, row : row + 1] + value
        middle_back(img, other0, False)
        k.GMX[img] = nt(k.MIDL[img], k.WPB[t]).astype(BF)

    def attend_back(step):
        img, p = step // pairs, lax.rem(step, pairs)
        cols = pl.ds(pl.multiple_of(p * PAIR, PAIR), PAIR)
        q, key, val = k.QKV[0, p, img], k.QKV[1, p, img], k.QKV[2, p, img]
        gmx = k.GMX[img, :, cols]
        pts, gss, gms, qs, kes = [], [], [], [], []
        for head in range(2):
            m = head_mask(head)
            low = k.PT[p, img, head]
            probs = low.astype(F32)
            gp = nt(val * m, gmx)
            inner = jnp.sum(gp * probs, axis=0, keepdims=True)
            pts.append(low)
            gss.append((probs * (gp - inner)).astype(BF))
            gms.append(gmx * m)
            qs.append(q * (m * SCALE).astype(BF))
            kes.append(jnp.concatenate([key * (m * SCALE).astype(BF), k.OHB[...] * m], axis=1))
        grad_v = nn(jnp.concatenate(pts, axis=1), jnp.concatenate(gms, axis=0))
        grad_k = nn(jnp.concatenate(gss, axis=1), jnp.concatenate(qs, axis=0))
        both = tn(jnp.concatenate(gss, axis=0), jnp.concatenate(kes, axis=0))
        rel = both[:, PAIR:]
        rel = jnp.where(lane64 < 32, spread_rows(rel), spread_cols(rel))
        high = rel.astype(BF)
        rest = (rel - high.astype(F32)).astype(BF)
        grad_q = both[:, :PAIR] + nn(
            jnp.concatenate([high, rest], axis=1), jnp.concatenate([k.TBB[...]] * 2, axis=0)
        )
        k.RG[...] += tn(jnp.concatenate([high, rest], axis=0), jnp.concatenate([q, q], axis=0))
        lanes = pl.ds(pl.multiple_of(t * width + p * PAIR, PAIR), PAIR)
        for i, grad in enumerate((grad_q, grad_k, grad_v)):
            low = grad.astype(BF)
            k.GQKV[i, img, :, cols] = low
            if i != 1:
                row = i // 2
                k.S1[0, row : row + 1, lanes] = k.S1[0, row : row + 1, lanes] + jnp.sum(
                    low.astype(F32), axis=0, keepdims=True
                )

    def gradient_first(img):
        @pl.loop(0, 2)
        def _(m):
            total = jnp.zeros((TOK, D // 2), F32)
            for i in range(3):
                total = total + nt(k.GQKV[i, img], W[0][pl.ds(2 * m, 2), :, :, i].reshape(D // 2, width))
            lanes = pl.ds(pl.multiple_of(m * (D // 2), 128), D // 2)
            k.GF[img, :, lanes] = total.astype(BF)
            for row, value in ((2, total * k.N1[img, :, lanes].astype(F32)), (3, total)):
                k.S1[0, row : row + 1, lanes] = k.S1[0, row : row + 1, lanes] + jnp.sum(value, axis=0, keepdims=True)

    middle(0)
    rs_take(1, 1)

    @pl.loop(0, pairs)
    def _(step):
        attend_back(step)

    rs_take(1, 1)
    gradient_first(0)
    middle(1)
    y_first(0).start()
    y_mlp(0).start()
    ar_send(0, 0)

    for j in range(D // 256):
        cols = slice(j * 256, (j + 1) * 256)
        out = tn(k.MX[t].reshape(IMG * TOK, width), k.MIDL[:, :, cols].reshape(IMG * TOK, 256))
        G[1][:, :, :, :, cols] = out.reshape(NZ, NX, NC, width // RING, 256).astype(BF)
    rs_core(PROJ_M).start()
    ar_done(0, 0)
    ar_send(1, 0)

    @pl.loop(pairs, 2 * pairs)
    def _(step):
        attend_back(step)

    rs_core_done(PROJ_M)
    rs_take(2, 2)
    gradient_first(1)
    y_first(1).start()
    rg = k.RG[...]
    turned = pltpu.roll(rg, HD, 1)
    packed = pltpu.roll(rg[32:64] + turned[96:128], HD, 1)
    k.S2[0] = jnp.where(iota((32, 128), 1) < HD, rg[0:32] + turned[64:96], packed)
    ar_send(0, 1, 2)

    for i in range(3):

        @pl.loop(0, 2)
        def _(m):
            lhs = k.FL[:, :, pl.ds(pl.multiple_of(m * (D // 2), 128), D // 2)].reshape(IMG * TOK, D // 2)
            out = tn(lhs, k.GQKV[i].reshape(IMG * TOK, width)).astype(BF)
            G[0][pl.ds(2 * m, 2), :, :, i] = out.reshape(2, NX, NC, D // RING, width)

    rs_core(QKV_M).start()
    ar_done(1, 0)
    ar_send(2, 0)
    ar_done(0, 1, 2)
    ar_send(1, 1, 2)
    rs_core_done(QKV_M)
    rs_take(2, 2)
    rs_take(2, 2)

    def finish_grad(img):
        y_first(img).wait_recv()

        @pl.loop(0, half // CH)
        def _(i):
            at, here = rows(own0, i), rows(0, i)
            n, rstd = normalize(k.tok[img, here].astype(F32))
            grad = k.GF[img, at].astype(F32) + k.GFR[img, here].astype(F32)
            k.o_gtok[img, here] = k.GM[img, here] + norm_back(grad, n, rstd, g1[...])

    def finish_block(img):
        y_mlp(img).wait_recv()

        @pl.loop(0, half // CH)
        def _(i):
            at, here = rows(own0, i), rows(0, i)
            k.o_blk[img, here] = (
                k.MID[img, at] + k.DP[img, at].astype(F32) + k.DPR[img, here].astype(F32) + dnb[...]
            ).astype(BF)

    finish_grad(0)
    finish_block(0)
    rs_take(1, 1)
    finish_grad(1)
    y_mlp(1).start()
    ar_done(1, 1, 2)
    ar_send(2, 1, 2)
    rs_take(1, 1)
    rs_done(DOWN_M, k.o_gd)
    rs_take(1)
    rs_done(UP_M, k.o_gu)
    rs_take(1)
    ar_done(2, 0)
    rs_done(PROJ_M, k.o_gp)
    finish_block(1)
    rs_take(1)
    ar_done(2, 1, 2)
    k.o_sm[0:8] = k.S0[3]
    k.o_sm[8:12] = k.S1[3]
    k.o_rel[...] = k.S2[3]
    rs_take(1)
    rs_done(QKV_M, k.o_gq)

    @pl.when(middle_chip)
    def _():
        for m in relayed:
            for n in range(4):
                ag_relay(m, n).wait_send()

    for m in range(4):
        for i in (1, 2, 3):
            if i == 1 or m not in relayed:
                ag_z(m, i).wait_send()
            rs_z(m, i).wait_send()
        for i in range(4):
            ag_x(m, i).wait_send()
            ag_c(m, i, 0).wait_send()
            ag_c(m, i, 1).wait_send()
            rs_x(m, i).wait_send()
        rs_core(m).wait_send()
    for copy in (y_tok(), y_cot(), y_proj()):
        copy.wait_send()
    for img in range(IMG):
        for make in (y_attn, y_mlp, y_sec, y_first):
            make(img).wait_send()
    for b in range(3):
        for i in range(7):
            ar(b, i).wait_send()


def fused_block(ratio, args):
    width, hid = args[2].shape[2], args[4].shape[1]
    table, sems, shards = scratch_table(width, hid)
    table["G1F"] = ((2 * width, D), F32)
    names = list(NAMES_IN) + list(NAMES_OUT) + list(table)
    scratch = [pltpu.VMEM(shape, kind) for shape, kind in table.values()]
    for name, shape in sems.items():
        names += [name + "_s", name + "_r"]
        scratch += [pltpu.SemaphoreType.DMA(shape)] * 2
    tok = args[0].shape
    outs = [(tok, BF), (tok, F32)] + [(shape, F32) for shape in shards] + [((16, D), F32), ((32, 128), F32)]
    vmem = pl.BlockSpec(memory_space=pltpu.VMEM)
    return pl.pallas_call(
        functools.partial(block_kernel, ratio, width, hid, names),
        out_shape=[jax.ShapeDtypeStruct(shape, kind) for shape, kind in outs],
        in_specs=[vmem] * len(NAMES_IN),
        out_specs=[vmem] * len(outs),
        scratch_shapes=scratch,
        compiler_params=pltpu.CompilerParams(
            collective_id=0, has_side_effects=True, vmem_limit_bytes=62 << 20
        ),
        name="fused_block",
    )(*args)


def finish_kernel(*refs):
    big, (small, rel), outs = refs[:6], refs[6:8], refs[8:24]
    held, sem_in, sem = refs[24:30], refs[30], refs[31]
    where = (0, 1, 2, 4, 6, 8)
    loads = [pltpu.make_async_copy(src, dst, sem_in.at[n]) for n, (src, dst) in enumerate(zip(big, held))]
    copies = [pltpu.make_async_copy(src, outs[i], sem.at[n]) for n, (src, i) in enumerate(zip(held, where))]
    for copy in loads:
        copy.start()
    for load, copy in zip(loads, copies):
        load.wait()
        copy.start()
    outs[3][...] = small[8:10]
    for i, row in ((5, 2), (9, 3), (10, 10), (11, 11), (12, 0), (13, 1)):
        outs[i][...] = small[row : row + 1].reshape(D)
    for j in range(FF // D):
        outs[7][j * D : (j + 1) * D] = small[4 + j : 5 + j].reshape(D)
    outs[14][...] = rel[:RELS, :HD]
    outs[15][...] = rel[:RELS, HD:]
    for copy in copies:
        copy.wait()


def hand_out(block_out, grad_tokens, grads, small, rel):
    big = [block_out, grad_tokens, *grads]
    vec = jax.ShapeDtypeStruct((D,), F32)
    table = jax.ShapeDtypeStruct((RELS, HD), F32)
    like = [jax.ShapeDtypeStruct(v.shape, v.dtype) for v in big]
    outs = [like[0], like[1], like[2], jax.ShapeDtypeStruct((2, D), F32), like[3], vec, like[4],
            jax.ShapeDtypeStruct((FF,), F32), like[5], vec, vec, vec, vec, vec, table, table]
    vmem, whole = pl.BlockSpec(memory_space=pltpu.VMEM), pl.BlockSpec(memory_space=pl.ANY)
    return pl.pallas_call(
        finish_kernel,
        out_shape=outs,
        in_specs=[whole] * 6 + [vmem] * 2,
        out_specs=[whole if i in (0, 1, 2, 4, 6, 8) else vmem for i in range(16)],
        scratch_shapes=[pltpu.VMEM(v.shape, v.dtype) for v in big] + [pltpu.SemaphoreType.DMA((6,))] * 2,
        compiler_params=pltpu.CompilerParams(vmem_limit_bytes=62 << 20),
        name="hand_out",
    )(*big, small, rel)


def on_device(dp_size, *args):
    (tokens, w_qkv, qv_bias, w_proj, proj_bias, w_up, up_bias, w_down, down_bias,
     norm1_gain, norm1_shift, norm2_gain, norm2_shift, rel_rows, rel_cols, cotangent) = args
    ratio = dp_size // RING
    weights = [w_qkv, w_proj, w_up, w_down]
    dims = (1, 0, 0, 0)
    groups = [[i * ratio + j for j in range(ratio)] for i in range(RING)]
    across = [[i * ratio + j for i in range(RING)] for j in range(ratio)]
    if ratio > 1:
        weights = [
            lax.all_gather(w, "dp", axis=dim, tiled=True, axis_index_groups=groups)
            for w, dim in zip(weights, dims)
        ]
    outs = fused_block(
        ratio,
        (tokens, cotangent, *weights, qv_bias, proj_bias, up_bias, down_bias,
         norm1_gain, norm1_shift, norm2_gain, norm2_shift, rel_rows, rel_cols),
    )
    block_out, grad_tokens, *grads, small, rel = outs
    if ratio > 1:
        grads = [
            lax.psum_scatter(g, "dp", scatter_dimension=dim, tiled=True, axis_index_groups=groups)
            for g, dim in zip(grads, dims)
        ]
        small, rel = lax.psum((small, rel), "dp", axis_index_groups=groups)
    return hand_out(block_out, grad_tokens, grads, small, rel)


def solution(mesh):
    split = P("dp", "tensor", None)
    specs = (split, P(None, "dp", "tensor"), P(), P(("tensor", "dp"), None), P(), P("dp", "tensor"), P(),
             P(("tensor", "dp"), None))
    return jax.shard_map(
        functools.partial(on_device, mesh.shape["dp"]),
        mesh=mesh,
        in_specs=specs + (P(),) * 7 + (split,),
        out_specs=(split,) + specs + (P(),) * 7,
        check_vma=False,
    )
```

```python
import functools

import jax
import jax.numpy as jnp
from jax import lax
from jax.experimental import pallas as pl
from jax.experimental.pallas import tpu as pltpu
from jax.sharding import PartitionSpec as P

D = 768
HD = 64
FF = 3072
GRID = 16
TOK = 256
RELS = 31
NZ, NX, NC = 4, 2, 2
RING = NZ * NX * NC
IMG = 2
PAIR = 2 * HD
CH = 64
EPS = 1e-06
F32 = jnp.float32
BF = jnp.bfloat16
MESH = pl.DeviceIdType.MESH
SCALE = HD ** (-0.5)
QKV_M, PROJ_M, UP_M, DOWN_M = range(4)


def nn(a, b):
    return lax.dot_general(a, b, (((1,), (0,)), ((), ())), preferred_element_type=F32)


def nt(a, b):
    return lax.dot_general(a, b, (((1,), (1,)), ((), ())), preferred_element_type=F32)


def tn(a, b):
    return lax.dot_general(a, b, (((0,), (0,)), ((), ())), preferred_element_type=F32)


def iota(shape, dim):
    return lax.broadcasted_iota(jnp.int32, shape, dim)


def one_hot(cond):
    return jnp.where(cond, 1.0, 0.0).astype(BF)


def mean_last(v):
    return jnp.sum(v, axis=-1, keepdims=True) * (1.0 / v.shape[-1])


def normalize(v):
    centred = v - mean_last(v)
    rstd = lax.rsqrt(mean_last(centred * centred) + EPS)
    return centred * rstd, rstd


def norm_back(grad, n, rstd, gain):
    e = grad * gain
    return (e - mean_last(e) - n * mean_last(e * n)) * rstd


def spread_rows(v):
    return jnp.concatenate(
        [pltpu.roll(v[g * GRID : (g + 1) * GRID], g, 1) if g else v[:GRID] for g in range(GRID)], axis=0
    )


def spread_cols(v):
    return jnp.concatenate(
        [
            pltpu.roll(v[g * GRID : (g + 1) * GRID], 0, 1, stride=1, stride_axis=0)
            for g in range(GRID)
        ],
        axis=0,
    )


NAMES_IN = (
    "tok", "cot", "sq", "sp", "su", "sd",
    "qvb", "pjb", "upb", "dnb", "g1", "b1",
    "g2", "b2", "relr", "relc",
)
NAMES_OUT = (
    "o_blk", "o_gtok", "o_gq", "o_gp", "o_gu", "o_gd",
    "o_sm", "o_rel",
)


def scratch_table(width, hid):
    pairs = width // PAIR
    half = TOK // 2
    shards = [(3, D // RING, width), (width // RING, D), (D // RING, hid), (hid // RING, D)]
    gathered = [shards[0], (2,) + shards[1], shards[2], shards[3]]
    table = {
        "XT": ((IMG, TOK, D), BF),
        "CT": ((IMG, TOK, D), BF),
        "WPB": ((2, width, D), BF),
        "PSH": ((2, width // RING, D), BF),
        "N1": ((IMG, TOK, D), BF),
        "FL": ((IMG, TOK, D), BF),
        "QKV": ((3, pairs, IMG, TOK, PAIR), BF),
        "PT": ((pairs, IMG, 2, TOK, TOK), BF),
        "MX": ((2, IMG, TOK, width), BF),
        "MID": ((IMG, TOK, D), F32),
        "N2": ((IMG, TOK, D), F32),
        "RS2": ((IMG, TOK, 128), F32),
        "SEC": ((IMG, TOK, D), BF),
        "ACT": ((IMG, TOK, hid), BF),
        "GEL": ((IMG, TOK, hid), BF),
        "DP": ((IMG, TOK, D), BF),
        "DPR": ((IMG, half, D), BF),
        "GPRE": ((IMG, TOK, hid), BF),
        "GS": ((IMG, TOK, D), BF),
        "GSR": ((IMG, TOK, D), BF),
        "GM": ((IMG, half, D), F32),
        "MIDL": ((IMG, TOK, D), BF),
        "GMX": ((IMG, TOK, width), BF),
        "GQKV": ((3, IMG, TOK, width), BF),
        "GF": ((IMG, TOK, D), BF),
        "GFR": ((IMG, half, D), BF),
        "RG": ((PAIR, PAIR), F32),
        "TBF": ((PAIR, PAIR), BF),
        "TBB": ((PAIR, PAIR), BF),
        "OHF": ((TOK, PAIR), BF),
        "OHB": ((TOK, PAIR), BF),
        "MSK": ((4, 16, PAIR), BF),
        "PAR": ((6, 1, D), F32),
        "UPB": ((1, hid), F32),
        "S0": ((4, 8, D), F32),
        "S1": ((4, 4, D), F32),
        "S2": ((4, 32, 128), F32),
        "R0": ((7, 8, D), F32),
        "R1": ((7, 4, D), F32),
        "R2": ((7, 32, 128), F32),
    }
    for i, shard in enumerate(shards):
        table[f"W{i}"] = ((NZ, NX, NC) + gathered[i], BF)
        table[f"G{i}"] = ((NZ, NX, NC) + shard, BF)
        table[f"C{i}"] = ((NZ, NX) + shard, BF)
        table[f"X{i}"] = ((NZ,) + shard, BF)
        table[f"Z{i}"] = ((NZ - 1,) + shard, BF)
        table[f"Y{i}"] = (shard, BF)
    sems = {
        "agz": (4, 3),
        "agh": (4, 4),
        "agx": (4, 4),
        "agc": (4, 8),
        "ysem": (11,),
        "rsc": (4, 4),
        "rsx": (4, 4),
        "rsz": (4, 3),
        "rsy": (4, 1),
        "ars": (3, 7),
    }
    return table, sems, shards


class Refs:
    pass


def block_kernel(ratio, width, hid, names, *refs):
    k = Refs()
    for name, ref in zip(names, refs):
        setattr(k, name, ref)
    pairs = width // PAIR
    half = TOK // 2
    dp = lax.axis_index("dp")
    t = lax.axis_index("tensor")
    sub = lax.rem(dp, ratio)
    s = dp // ratio
    z, x, c = s // (NX * NC), lax.rem(s // NC, NX), lax.rem(s, NC)

    def device(zz, xx, cc, tt=t):
        return (((zz * NX + xx) * NC + cc) * ratio + sub, tt)

    z_of = (z, z + 1 - 2 * lax.rem(z, 2), lax.rem(z + 2, NZ), NZ - 1 - z)
    core_peer, x_peer, y_peer = device(z, x, 1 - c), device(z, 1 - x, c), device(z, x, c, 1 - t)
    xy_peer = device(z, 1 - x, c, 1 - t)
    z_peer = [device(zz, x, c) for zz in z_of]
    own0 = pl.multiple_of(t * half, half)
    other0 = pl.multiple_of((1 - t) * half, half)

    def remote(src, dst, sems, idx, peer):
        return pltpu.make_async_remote_copy(
            src_ref=src,
            dst_ref=dst,
            send_sem=getattr(k, sems + "_s").at[idx],
            recv_sem=getattr(k, sems + "_r").at[idx],
            device_id=peer,
            device_id_type=MESH,
        )

    shard_in = [k.sq, k.PSH, k.su, k.sd]
    W = [k.W0, k.W1, k.W2, k.W3]
    G = [k.G0, k.G1, k.G2, k.G3]
    C = [k.C0, k.C1, k.C2, k.C3]
    X = [k.X0, k.X1, k.X2, k.X3]
    Z = [k.Z0, k.Z1, k.Z2, k.Z3]
    Y = [k.Y0, k.Y1, k.Y2, k.Y3]

    side = z // 2
    relayed = (PROJ_M, UP_M, DOWN_M)
    broad = ()
    middle_chip = (z == 1) | (z == 2)
    relay_of = (z, z_of[1], 2 - side, 3 - 3 * side)
    origin = [relay_of if m in relayed else z_of for m in range(4)]

    def piece(m, i, other=False):
        if m in broad:
            return W[m].at[origin[m][i], :, c]
        if i == 0 and not other:
            return shard_in[m]
        return W[m].at[origin[m][i], 1 - x if other else x, c]

    def ag_z(m, i):
        dst = W[m].at[z, :, c] if m in broad else W[m].at[z, x, c]
        return remote(piece(m, 0), dst, "agz", (m, i - 1), z_peer[i])

    def ag_relay(m, n):
        i, arrives, peer = ((0, 2, 3), (1, 3, 3), (2, 2, 1), (3, 3, 1))[n]
        return pltpu.make_async_remote_copy(
            src_ref=piece(m, i),
            dst_ref=piece(m, i) if m in broad else W[m].at[origin[m][i], x, c],
            send_sem=k.agh_s.at[m, n],
            recv_sem=k.agz_r.at[m, arrives - 1],
            device_id=z_peer[peer],
            device_id_type=MESH,
        )

    def relay(m, n):
        @pl.when(middle_chip)
        def _():
            ag_relay(m, n).start()

    def ag_x(m, i):
        src = shard_in[m] if m in broad else piece(m, i)
        return remote(src, W[m].at[origin[m][i], x, c], "agx", (m, i), x_peer)

    def ag_c(m, i, other):
        if m in broad:
            return remote(piece(m, i), piece(m, i), "agc", (m, i), core_peer)
        xx = 1 - x if other else x
        return remote(piece(m, i, other), W[m].at[origin[m][i], xx, c], "agc", (m, i + 4 * other), core_peer)

    def ag_send(m, slots=(1,)):
        if m in broad:
            ag_x(m, 0).wait_recv()
            ag_c(m, 0, 0).start()
        for i in slots:
            ag_z(m, i).start()
        if m in relayed:
            relay(m, 0)

    def ag_own(m):
        ag_x(m, 0).start()
        if m not in broad:
            ag_c(m, 0, 0).start()

    def ag_on(m, i, cross=True):
        if m not in broad and cross:
            ag_x(m, i).start()
        ag_c(m, i, 0).start()

    def ag_pass(m, slots, cross=True):
        for i in slots:
            ag_z(m, i).wait_recv()
            if m in relayed:
                relay(m, i)
            ag_on(m, i, cross)

    def ag_pass_middle(*pairs, cross=True):
        @pl.when(middle_chip)
        def _():
            for m, i in pairs:
                ag_z(m, i).wait_recv()
                ag_relay(m, i).start()
                ag_on(m, i, cross)

    def ag_pass_end(*pairs, cross=True):
        @pl.when(jnp.logical_not(middle_chip))
        def _():
            for m, i in pairs:
                ag_z(m, i).wait_recv()
                ag_on(m, i, cross)

    def ag_late_cross(m, slots):
        for i in slots:
            ag_x(m, i).start()

    def ag_cross(m, slots=(0, 1, 2, 3)):
        for i in slots:
            ag_x(m, i).wait_recv()
            ag_c(m, i, 1).start()

    def ag_done(m):
        for other in (0,) if m in broad else (0, 1):
            for i in range(NZ):
                ag_c(m, i, other).wait_recv()

    def rs_core(m, i):
        at = relay_of[i]
        return remote(G[m].at[at, :, 1 - c], C[m].at[at], "rsc", (m, i), core_peer)

    def rs_core_send(m, slots=(3, 2, 1, 0)):
        for i in slots:
            rs_core(m, i).start()

    def rs_x(m, i):
        return remote(G[m].at[relay_of[i], 1 - x, c], X[m].at[i], "rsx", (m, i), x_peer)

    via = jnp.where(middle_chip, 1, 2)

    def rs_z(m, i):
        slot = (None, 0, via, 1)[i]
        return pltpu.make_async_remote_copy(
            src_ref=G[m].at[relay_of[i], x, c],
            dst_ref=Z[m].at[slot],
            send_sem=k.rsz_s.at[m, i - 1],
            recv_sem=k.rsz_r.at[m, slot],
            device_id=device(relay_of[i], x, c),
            device_id_type=MESH,
        )

    def rs_arrived(m, slot):
        pltpu.make_async_remote_copy(
            src_ref=Z[m].at[slot],
            dst_ref=Z[m].at[slot],
            send_sem=k.rsz_s.at[m, slot],
            recv_sem=k.rsz_r.at[m, slot],
            device_id=z_peer[1],
            device_id_type=MESH,
        ).wait_recv()

    def rs_y(m):
        return remote(G[m].at[relay_of[3], x, c], Y[m], "rsy", (m, 0), z_peer[1])

    def rs_relay(m):
        @pl.when(middle_chip)
        def _():
            rs_y(m).wait_recv()
            add_into(G[m], (relay_of[3], x, c), Y[m], ())
            rs_z(m, 3).start()

    def add_into(dst, where, src, which):
        if len(dst.shape) - len(where) == 3:
            for j in range(3):
                dst[(*where, j)] = dst[(*where, j)] + src[(*which, j)]
        else:
            dst[where] = dst[where] + src[which or ...]

    def rs_core_done(m, slots=(3, 2, 1, 0)):
        for i in slots:
            rs_core(m, i).wait_recv()
            for xx in range(NX):
                add_into(G[m], (relay_of[i], xx, c), C[m], (relay_of[i], xx))

    queue = [(m, i) for m in (DOWN_M, UP_M, PROJ_M, QKV_M) for i in (3, 2, 1, 0)]
    fed, taken = list(queue), list(queue)

    def rs_feed(count):
        for _ in range(count):
            rs_x(*fed.pop(0)).start()

    def rs_take(count, feed=0):
        for _ in range(count):
            m, i = taken.pop(0)
            rs_x(m, i).wait_recv()
            if feed:
                rs_feed(1)
                feed -= 1
            add_into(G[m], (relay_of[i], x, c), X[m], (i,))
            if i == 3:

                @pl.when(jnp.logical_not(middle_chip))
                def _():
                    rs_y(m).start()

            elif i:
                rs_z(m, i).start()

    def rs_done(m, out):
        rs_arrived(m, 0)
        rs_arrived(m, 1)
        parts = range(3) if m == QKV_M else (None,)

        def add_slots(start, slots):
            for j in parts:
                at = () if j is None else (j,)
                here = ... if j is None else j
                total = start(at, here)
                for slot in slots:
                    total = total + Z[m][(slot, *at)].astype(F32)
                out[here] = total

        add_slots(lambda at, here: G[m][(z, x, c, *at)].astype(F32), (0, 1))

        @pl.when(middle_chip)
        def _():
            rs_arrived(m, 2)
            add_slots(lambda at, here: out[here], (2,))

    S = [k.S0, k.S1, k.S2]
    R = [k.R0, k.R1, k.R2]
    hops = ((0,), (1, 2, 3), (4, 5, 6))

    def ar(b, i):
        step = 0 if i == 0 else 1 if i < 4 else 2
        peer = ([core_peer, x_peer, y_peer, xy_peer] + z_peer[1:])[i]
        return remote(S[b].at[step], R[b].at[i], "ars", (b, i), peer)

    def ar_send(step, *which):
        for b in which:
            for i in hops[step]:
                ar(b, i).start()

    def ar_done(step, *which):
        for b in which:
            for i in hops[step]:
                ar(b, i).wait_recv()
            if step == 0:
                S[b][1] = S[b][0] + R[b][0]
            else:
                first, i = S[b][step], hops[step][0]
                S[b][step + 1] = (first + R[b][i]) + (R[b][i + 1] + R[b][i + 2])

    def y_rows(img, base):
        return (img, pl.ds(base, half))

    def y_tok():
        return remote(k.tok, k.XT.at[:, pl.ds(own0, half)], "ysem", (0,), y_peer)

    def y_cot():
        return remote(k.cot, k.CT.at[:, pl.ds(own0, half)], "ysem", (1,), y_peer)

    def y_attn(img):
        return remote(k.MX.at[t, img], k.MX.at[t, img], "ysem", (2 + img,), y_peer)

    def y_proj():
        return remote(k.sp, k.PSH.at[t], "ysem", (10,), y_peer)

    def y_mlp(img):
        return remote(k.DP.at[img, pl.ds(other0, half)], k.DPR.at[img], "ysem", (4 + img,), y_peer)

    def y_sec(img):
        return remote(k.GS.at[img], k.GSR.at[img], "ysem", (6 + img,), y_peer)

    def y_first(img):
        return remote(k.GF.at[img, pl.ds(other0, half)], k.GFR.at[img], "ysem", (8 + img,), y_peer)

    def rows(base, i):
        return pl.ds(pl.multiple_of(base + i * CH, CH), CH)

    barrier = pltpu.get_barrier_semaphore()
    peers = [core_peer, x_peer, y_peer, xy_peer] + z_peer[1:]
    for peer in peers:
        pl.semaphore_signal(barrier, inc=1, device_id=peer, device_id_type=MESH)
    pl.semaphore_wait(barrier, len(peers))

    ag_send(QKV_M, (1, 2))
    y_proj().start()
    y_tok().start()
    ag_own(QKV_M)

    for row, ref in enumerate((k.g1, k.b1, k.g2, k.b2, k.pjb, k.dnb)):
        k.PAR[row] = ref[...].reshape(1, D)
    g1, b1, g2, b2, pjb, dnb = (k.PAR.at[row] for row in range(6))
    k.UPB[...] = k.upb[pl.ds(pl.multiple_of(t * hid, 128), hid)].reshape(1, hid)
    lane = iota((TOK, PAIR), 1)
    lane64 = lax.rem(lane, HD)
    urow, ucol = iota((TOK, PAIR), 0) // GRID, lax.rem(iota((TOK, PAIR), 0), GRID)
    shifted = lax.rem(lane + (PAIR - GRID + 1), HD)
    seg, pos = shifted // GRID, lax.rem(shifted, GRID)
    k.OHF[...] = one_hot(((seg < 2) & (urow == pos)) | ((seg >= 2) & (ucol == pos)))
    k.OHB[...] = one_hot(
        ((lane64 < GRID) & (urow == GRID - 1 - lane64))
        | ((lane64 >= 2 * GRID) & (lane64 < 3 * GRID) & (ucol == 3 * GRID - 1 - lane64))
    )
    mlane = iota((16, PAIR), 1)
    in_first = mlane < HD
    ext_first = (mlane >= GRID - 1) & (mlane < HD + GRID - 1)
    k.MSK[0] = one_hot(in_first)
    k.MSK[1] = one_hot(mlane >= HD)
    k.MSK[2] = one_hot(ext_first)
    k.MSK[3] = one_hot((mlane < GRID - 1) | (mlane >= HD + GRID - 1))
    tl, td = iota((PAIR, RELS), 0), iota((PAIR, RELS), 1)
    fwd_tab = jnp.zeros((PAIR, PAIR), F32)
    bwd_tab = jnp.zeros((PAIR, PAIR), F32)
    for head in range(2):
        place = one_hot(iota((HD, PAIR), 1) == iota((HD, PAIR), 0) + head * HD)
        for base, rel in ((0, k.relr), (32, k.relc)):
            wide = nn(rel[...], place).astype(BF)
            at = tl - (head * HD + base)
            fwd_tab = fwd_tab + nn(one_hot(at == RELS - 1 - td), wide)
            bwd_tab = bwd_tab + nn(one_hot(at == td), wide)
    k.TBF[...] = fwd_tab.astype(BF)
    k.TBB[...] = bwd_tab.astype(BF)
    k.S0[0] = jnp.zeros((8, D), F32)
    k.S1[0] = jnp.zeros((4, D), F32)
    k.RG[...] = jnp.zeros((PAIR, PAIR), F32)

    def first_norm(base):
        @pl.loop(0, IMG)
        def _(img):
            @pl.loop(0, half // CH)
            def _(i):
                at = rows(base, i)
                n, _ = normalize(k.XT[img, at].astype(F32))
                k.N1[img, at] = n.astype(BF)
                k.FL[img, at] = (n * g1[...] + b1[...]).astype(BF)

    for img in range(IMG):
        k.XT[img, pl.ds(own0, half)] = k.tok[img]
        k.CT[img, pl.ds(own0, half)] = k.cot[img]
    k.PSH[t] = k.sp[...]
    y_proj().wait_recv()
    ag_own(PROJ_M)
    ag_own(UP_M)
    first_norm(own0)
    ag_send(QKV_M, (3,))
    for m in range(4):
        W[m][z, x, c] = shard_in[m][...]
    ag_pass(QKV_M, (1, 2))
    ag_send(PROJ_M)
    ag_send(UP_M)
    ag_pass(QKV_M, (3,))
    y_tok().wait_recv()
    y_cot().start()
    first_norm(other0)
    ag_pass(PROJ_M, (1,))
    ag_pass(UP_M, (1,))
    ag_pass_middle((PROJ_M, 2), (UP_M, 2))
    ag_cross(QKV_M)
    ag_done(QKV_M)

    lanes_w = pl.ds(pl.multiple_of(t * width, 128), width)
    for i in range(3):

        @pl.loop(0, IMG)
        def _(img):
            out = nn(k.FL[img], W[0][:, :, :, i].reshape(D, width))
            if i != 1:
                out = out + k.qvb[i // 2 : i // 2 + 1, lanes_w]
            low = out.astype(BF)
            for p in range(pairs):
                k.QKV[i, p, img] = low[:, p * PAIR : (p + 1) * PAIR]

    ag_pass_end((PROJ_M, 2), (UP_M, 2))
    ag_pass_middle((PROJ_M, 3), (UP_M, 3))
    ag_send(DOWN_M)
    ag_own(DOWN_M)

    def head_mask(i):
        return k.MSK[i][0:1]

    def attend(step):
        img, p = step // pairs, lax.rem(step, pairs)
        q, key, val = k.QKV[0, p, img], k.QKV[1, p, img], k.QKV[2, p, img]
        qr = nt(q, k.TBF[...])
        ext = jnp.where(
            (lane64 >= 15) & (lane64 < 31),
            spread_rows(qr),
            jnp.where((lane64 >= 47) & (lane64 < 63), spread_cols(qr), 0.0),
        )
        high = ext.astype(BF).astype(F32)
        ext = (high + pltpu.roll(ext - high, GRID, 1)).astype(BF)
        k_ext = jnp.concatenate([key, k.OHF[...]], axis=1)
        probs, vals = [], []
        for head in range(2):
            q_ext = jnp.concatenate(
                [q * (head_mask(head) * SCALE).astype(BF), ext * head_mask(2 + head)], axis=1
            )
            scores = nt(k_ext, q_ext)
            e = jnp.exp(scores - jnp.max(scores, axis=0, keepdims=True))
            low = (e * (1.0 / jnp.sum(e, axis=0, keepdims=True))).astype(BF)
            k.PT[p, img, head] = low
            probs.append(low)
            vals.append(val * head_mask(head))
        mixed = tn(jnp.concatenate(probs, axis=0), jnp.concatenate(vals, axis=0))
        k.MX[t, img, :, pl.ds(pl.multiple_of(p * PAIR, PAIR), PAIR)] = mixed.astype(BF)

    attend(0)
    attend(1)
    attend(2)
    y_attn(0).start()
    ag_pass_end((PROJ_M, 3))
    ag_cross(PROJ_M, (0, 1))
    attend(3)
    ag_pass_end((UP_M, 3))
    ag_pass(DOWN_M, (1,))
    ag_pass_middle((DOWN_M, 2))
    attend(4)
    ag_cross(UP_M, (0, 1))
    ag_cross(PROJ_M, (2, 3))
    attend(5)
    y_attn(1).start()
    ag_pass_middle((DOWN_M, 3))
    ag_pass_end((DOWN_M, 2))
    ag_done(PROJ_M)

    @pl.loop(0, RING)
    def _(i):
        zz, xx, cc = i // (NX * NC), lax.rem(i // NC, NX), lax.rem(i, NC)
        for tt in range(2):
            at = pl.ds(pl.multiple_of(tt * width + i * (width // RING), 8), width // RING)
            k.G1F[at] = W[1][zz, xx, cc, tt].astype(F32)

    k.WPB[...] = k.G1F[...].astype(BF).reshape(2, width, D)

    def second_norm(img):
        y_attn(img).wait_recv()

        @pl.loop(0, D // 256)
        def _(j):
            cols = pl.ds(pl.multiple_of(j * 256, 256), 256)
            k.MID[img, :, cols] = nn(k.MX[0, img], k.WPB[0, :, cols]) + nn(k.MX[1, img], k.WPB[1, :, cols])

        @pl.loop(0, TOK // CH)
        def _(i):
            at = rows(0, i)
            mid = k.MID[img, at] + k.XT[img, at].astype(F32) + pjb[...]
            k.MID[img, at] = mid
            n, rstd = normalize(mid)
            k.N2[img, at] = n
            k.RS2[img, at] = jnp.broadcast_to(rstd, (CH, 128))
            k.SEC[img, at] = (n * g2[...] + b2[...]).astype(BF)

    def hidden(img):
        @pl.loop(0, hid // 256)
        def _(j):
            cols = pl.ds(pl.multiple_of(j * 256, 256), 256)
            bias = k.UPB[:, cols]
            pre = nn(k.SEC[img], W[2][:, :, :, :, cols].reshape(D, 256)) + bias
            phi = 0.5 + 0.5 * lax.erf(pre * 0.7071067811865476)
            k.ACT[img, :, cols] = (pre * phi).astype(BF)
            k.GEL[img, :, cols] = (phi + pre * (0.3989422804014327 * jnp.exp(-0.5 * pre * pre))).astype(BF)

    second_norm(0)
    ag_cross(UP_M, (2, 3))
    ag_done(UP_M)
    hidden(0)
    ag_pass_end((DOWN_M, 3))
    ag_cross(DOWN_M, (0, 1))
    second_norm(1)
    hidden(1)
    ag_cross(DOWN_M, (2,))

    def down(img):
        @pl.loop(0, D // 256)
        def _(j):
            cols = pl.ds(pl.multiple_of(j * 256, 256), 256)
            k.DP[img, :, cols] = nn(k.ACT[img], W[3][:, :, :, :, cols].reshape(hid, 256)).astype(BF)

    y_cot().wait_recv()

    tile = hid // NZ

    for i in (3, 2, 1, 0):
        m = relay_of[i]
        lhs = k.ACT[:, :, pl.ds(pl.multiple_of(m * tile, 128), tile)].reshape(IMG * TOK, tile)
        for j in range(D // 256):
            cols = slice(j * 256, (j + 1) * 256)
            out = tn(lhs, k.CT[:, :, cols].reshape(IMG * TOK, 256)).astype(BF)
            G[3][m, :, :, :, cols] = out.reshape(NX, NC, hid // RING, 256)
        rs_core_send(DOWN_M, (i,))
        if i == 1:
            rs_core_done(DOWN_M, (3,))
            rs_feed(1)

    ag_cross(DOWN_M, (3,))
    rs_core_done(DOWN_M, (2,))
    rs_feed(1)
    per_row = D // tile
    ag_done(DOWN_M)

    def hidden_back(img):
        @pl.loop(0, NZ)
        def _(m):
            cols = pl.ds(pl.multiple_of(m * tile, 128), tile)
            grad = nt(k.CT[img], W[3][m].reshape(tile, D)) * k.GEL[img, :, cols].astype(F32)
            low = grad.astype(BF)
            k.GPRE[img, :, cols] = low
            row = pl.ds(4 + t * (hid // D) + m // per_row, 1)
            lanes = pl.ds(pl.multiple_of(lax.rem(m, per_row) * tile, 128), tile)
            k.S0[0, row, lanes] = k.S0[0, row, lanes] + jnp.sum(low.astype(F32), axis=0, keepdims=True)

        @pl.loop(0, 2)
        def _(j):
            w = W[2][pl.ds(j * 2, 2)].reshape(D // 2, hid)
            k.GS[img, :, pl.ds(pl.multiple_of(j * (D // 2), 128), D // 2)] = nt(k.GPRE[img], w).astype(BF)

        y_sec(img).start()

    hidden_back(0)
    rs_core_done(DOWN_M, (1, 0))
    rs_feed(1)
    hidden_back(1)
    rs_feed(1)

    @pl.loop(0, hid // 256)
    def _(j):
        cols = pl.ds(pl.multiple_of(j * 256, 256), 256)
        rhs = k.GPRE[:, :, cols].reshape(IMG * TOK, 256)
        for m in range(2):
            lhs = k.SEC[:, :, m * (D // 2) : (m + 1) * (D // 2)].reshape(IMG * TOK, D // 2)
            out = tn(lhs, rhs).astype(BF)
            G[2][2 * m : 2 * m + 2, :, :, :, cols] = out.reshape(2, NX, NC, D // RING, 256)

    rs_core_send(UP_M)
    rs_take(1)
    down(0)
    rs_core_done(UP_M)
    rs_feed(2)
    down(1)
    rs_take(1, 1)

    def middle_back(img, base, own):
        zero = jnp.zeros((1, D), F32)

        def chunk(i, sums):
            at = rows(base, i)
            grad = k.GS[img, at].astype(F32) + k.GSR[img, at].astype(F32)
            n = k.N2[img, at]
            rstd = jnp.concatenate([k.RS2[img, at]] * (D // 128), axis=1)
            cot = k.CT[img, at].astype(F32)
            gm = cot + norm_back(grad, n, rstd, g2[...])
            k.MIDL[img, at] = gm.astype(BF)
            if own:
                k.GM[img, rows(0, i)] = gm
                terms = (grad * n, grad, gm, cot)
                sums = tuple(a + jnp.sum(b, axis=0, keepdims=True) for a, b in zip(sums, terms))
            return sums

        return lax.fori_loop(0, half // CH, chunk, (zero,) * 4 if own else ())

    def middle(img):
        y_sec(img).wait_recv()
        sums = middle_back(img, own0, True)
        for row, value in enumerate(sums):
            k.S0[0, row : row + 1] = k.S0[0, row : row + 1] + value
        middle_back(img, other0, False)
        k.GMX[img] = nt(k.MIDL[img], k.WPB[t]).astype(BF)

    def attend_back(step):
        img, p = step // pairs, lax.rem(step, pairs)
        cols = pl.ds(pl.multiple_of(p * PAIR, PAIR), PAIR)
        q, key, val = k.QKV[0, p, img], k.QKV[1, p, img], k.QKV[2, p, img]
        gmx = k.GMX[img, :, cols]
        pts, gss, gms, qs, kes = [], [], [], [], []
        for head in range(2):
            m = head_mask(head)
            low = k.PT[p, img, head]
            probs = low.astype(F32)
            gp = nt(val * m, gmx)
            inner = jnp.sum(gp * probs, axis=0, keepdims=True)
            pts.append(low)
            gss.append((probs * (gp - inner)).astype(BF))
            gms.append(gmx * m)
            qs.append(q * (m * SCALE).astype(BF))
            kes.append(jnp.concatenate([key * (m * SCALE).astype(BF), k.OHB[...] * m], axis=1))
        grad_v = nn(jnp.concatenate(pts, axis=1), jnp.concatenate(gms, axis=0))
        grad_k = nn(jnp.concatenate(gss, axis=1), jnp.concatenate(qs, axis=0))
        both = tn(jnp.concatenate(gss, axis=0), jnp.concatenate(kes, axis=0))
        rel = both[:, PAIR:]
        rel = jnp.where(lane64 < 32, spread_rows(rel), spread_cols(rel))
        high = rel.astype(BF)
        rest = (rel - high.astype(F32)).astype(BF)
        grad_q = both[:, :PAIR] + nn(
            jnp.concatenate([high, rest], axis=1), jnp.concatenate([k.TBB[...]] * 2, axis=0)
        )
        k.RG[...] += tn(jnp.concatenate([high, rest], axis=0), jnp.concatenate([q, q], axis=0))
        lanes = pl.ds(pl.multiple_of(t * width + p * PAIR, PAIR), PAIR)
        for i, grad in enumerate((grad_q, grad_k, grad_v)):
            low = grad.astype(BF)
            k.GQKV[i, img, :, cols] = low
            if i != 1:
                row = i // 2
                k.S1[0, row : row + 1, lanes] = k.S1[0, row : row + 1, lanes] + jnp.sum(
                    low.astype(F32), axis=0, keepdims=True
                )

    def gradient_first(img):
        @pl.loop(0, 2)
        def _(m):
            total = jnp.zeros((TOK, D // 2), F32)
            for i in range(3):
                total = total + nt(k.GQKV[i, img], W[0][pl.ds(2 * m, 2), :, :, i].reshape(D // 2, width))
            lanes = pl.ds(pl.multiple_of(m * (D // 2), 128), D // 2)
            k.GF[img, :, lanes] = total.astype(BF)
            for row, value in ((2, total * k.N1[img, :, lanes].astype(F32)), (3, total)):
                k.S1[0, row : row + 1, lanes] = k.S1[0, row : row + 1, lanes] + jnp.sum(value, axis=0, keepdims=True)

    middle(0)
    rs_take(1, 1)
    rs_relay(DOWN_M)

    @pl.loop(0, pairs)
    def _(step):
        attend_back(step)

    rs_take(1)
    gradient_first(0)
    middle(1)
    rs_take(1)
    y_first(0).start()
    y_mlp(0).start()
    ar_send(0, 0)

    for j in range(D // 256):
        cols = slice(j * 256, (j + 1) * 256)
        out = tn(k.MX[t].reshape(IMG * TOK, width), k.MIDL[:, :, cols].reshape(IMG * TOK, 256))
        G[1][:, :, :, :, cols] = out.reshape(NZ, NX, NC, width // RING, 256).astype(BF)
    rs_core_send(PROJ_M)
    ar_done(0, 0)
    ar_send(1, 0)

    attend_back(pairs)
    rs_core_done(PROJ_M)
    rs_feed(1)
    rs_take(1, 1)
    rs_relay(UP_M)

    @pl.loop(pairs + 1, 2 * pairs)
    def _(step):
        attend_back(step)

    rs_take(1, 1)
    gradient_first(1)
    y_first(1).start()
    rg = k.RG[...]
    turned = pltpu.roll(rg, HD, 1)
    packed = pltpu.roll(rg[32:64] + turned[96:128], HD, 1)
    k.S2[0] = jnp.where(iota((32, 128), 1) < HD, rg[0:32] + turned[64:96], packed)
    ar_send(0, 1, 2)

    for far in (1, 0):
        part = 1 - side if far else side
        lhs = k.FL[:, :, pl.ds(pl.multiple_of(part * (D // 2), 128), D // 2)].reshape(IMG * TOK, D // 2)
        for i in range(3):
            out = tn(lhs, k.GQKV[i].reshape(IMG * TOK, width)).astype(BF)
            G[0][pl.ds(2 * part, 2), :, :, i] = out.reshape(2, NX, NC, D // RING, width)
        rs_core_send(QKV_M, (3, 2) if far else (1, 0))

    ar_done(1, 0)
    ar_send(2, 0)
    ar_done(0, 1, 2)
    ar_send(1, 1, 2)
    rs_take(1, 1)
    rs_core_done(QKV_M)
    rs_take(3, 3)
    rs_relay(PROJ_M)

    def finish_grad(img):
        y_first(img).wait_recv()

        @pl.loop(0, half // CH)
        def _(i):
            at, here = rows(own0, i), rows(0, i)
            n, rstd = normalize(k.tok[img, here].astype(F32))
            grad = k.GF[img, at].astype(F32) + k.GFR[img, here].astype(F32)
            k.o_gtok[img, here] = k.GM[img, here] + norm_back(grad, n, rstd, g1[...])

    def finish_block(img):
        y_mlp(img).wait_recv()

        @pl.loop(0, half // CH)
        def _(i):
            at, here = rows(own0, i), rows(0, i)
            k.o_blk[img, here] = (
                k.MID[img, at] + k.DP[img, at].astype(F32) + k.DPR[img, here].astype(F32) + dnb[...]
            ).astype(BF)

    finish_grad(0)
    finish_block(0)
    rs_take(1, 1)
    finish_grad(1)
    y_mlp(1).start()
    rs_take(1)
    ar_done(1, 1, 2)
    ar_send(2, 1, 2)
    rs_relay(QKV_M)
    rs_done(DOWN_M, k.o_gd)
    rs_take(1)
    rs_done(UP_M, k.o_gu)
    ar_done(2, 0)
    rs_done(PROJ_M, k.o_gp)
    finish_block(1)
    rs_take(1)
    ar_done(2, 1, 2)
    k.o_sm[0:8] = k.S0[3]
    k.o_sm[8:12] = k.S1[3]
    k.o_rel[...] = k.S2[3]
    rs_take(1)
    rs_done(QKV_M, k.o_gq)

    @pl.when(middle_chip)
    def _():
        for m in relayed:
            for n in range(4):
                ag_relay(m, n).wait_send()
        for m in range(4):
            rs_z(m, 3).wait_send()

    @pl.when(jnp.logical_not(middle_chip))
    def _():
        for m in range(4):
            rs_y(m).wait_send()

    for m in range(4):
        for i in (1, 2, 3):
            if i == 1 or m not in relayed:
                ag_z(m, i).wait_send()
            if i != 3:
                rs_z(m, i).wait_send()
        for i in range(4):
            if i == 0 or m not in broad:
                ag_x(m, i).wait_send()
            ag_c(m, i, 0).wait_send()
            if m not in broad:
                ag_c(m, i, 1).wait_send()
            rs_x(m, i).wait_send()
            rs_core(m, i).wait_send()
    for copy in (y_tok(), y_cot(), y_proj()):
        copy.wait_send()
    for img in range(IMG):
        for make in (y_attn, y_mlp, y_sec, y_first):
            make(img).wait_send()
    for b in range(3):
        for i in range(7):
            ar(b, i).wait_send()


def fused_block(ratio, args):
    width, hid = args[2].shape[2], args[4].shape[1]
    table, sems, shards = scratch_table(width, hid)
    table["G1F"] = ((2 * width, D), F32)
    names = list(NAMES_IN) + list(NAMES_OUT) + list(table)
    scratch = [pltpu.VMEM(shape, kind) for shape, kind in table.values()]
    for name, shape in sems.items():
        names += [name + "_s", name + "_r"]
        scratch += [pltpu.SemaphoreType.DMA(shape)] * 2
    tok = args[0].shape
    outs = [(tok, BF), (tok, F32)] + [(shape, F32) for shape in shards] + [((16, D), F32), ((32, 128), F32)]
    vmem = pl.BlockSpec(memory_space=pltpu.VMEM)
    return pl.pallas_call(
        functools.partial(block_kernel, ratio, width, hid, names),
        out_shape=[jax.ShapeDtypeStruct(shape, kind) for shape, kind in outs],
        in_specs=[vmem] * len(NAMES_IN),
        out_specs=[vmem] * len(outs),
        scratch_shapes=scratch,
        compiler_params=pltpu.CompilerParams(
            collective_id=0, has_side_effects=True, vmem_limit_bytes=62 << 20
        ),
        name="fused_block",
    )(*args)


def finish_kernel(*refs):
    big, (small, rel), outs = refs[:6], refs[6:8], refs[8:24]
    held, sem_in, sem = refs[24:30], refs[30], refs[31]
    where = (0, 1, 2, 4, 6, 8)
    loads = [pltpu.make_async_copy(src, dst, sem_in.at[n]) for n, (src, dst) in enumerate(zip(big, held))]
    copies = [pltpu.make_async_copy(src, outs[i], sem.at[n]) for n, (src, i) in enumerate(zip(held, where))]
    for copy in loads:
        copy.start()
    for load, copy in zip(loads, copies):
        load.wait()
        copy.start()
    outs[3][...] = small[8:10]
    for i, row in ((5, 2), (9, 3), (10, 10), (11, 11), (12, 0), (13, 1)):
        outs[i][...] = small[row : row + 1].reshape(D)
    for j in range(FF // D):
        outs[7][j * D : (j + 1) * D] = small[4 + j : 5 + j].reshape(D)
    outs[14][...] = rel[:RELS, :HD]
    outs[15][...] = rel[:RELS, HD:]
    for copy in copies:
        copy.wait()


def hand_out(block_out, grad_tokens, grads, small, rel):
    big = [block_out, grad_tokens, *grads]
    vec = jax.ShapeDtypeStruct((D,), F32)
    table = jax.ShapeDtypeStruct((RELS, HD), F32)
    like = [jax.ShapeDtypeStruct(v.shape, v.dtype) for v in big]
    outs = [like[0], like[1], like[2], jax.ShapeDtypeStruct((2, D), F32), like[3], vec, like[4],
            jax.ShapeDtypeStruct((FF,), F32), like[5], vec, vec, vec, vec, vec, table, table]
    vmem, whole = pl.BlockSpec(memory_space=pltpu.VMEM), pl.BlockSpec(memory_space=pl.ANY)
    return pl.pallas_call(
        finish_kernel,
        out_shape=outs,
        in_specs=[whole] * 6 + [vmem] * 2,
        out_specs=[whole if i in (0, 1, 2, 4, 6, 8) else vmem for i in range(16)],
        scratch_shapes=[pltpu.VMEM(v.shape, v.dtype) for v in big] + [pltpu.SemaphoreType.DMA((6,))] * 2,
        compiler_params=pltpu.CompilerParams(vmem_limit_bytes=62 << 20),
        name="hand_out",
    )(*big, small, rel)


def on_device(dp_size, *args):
    (tokens, w_qkv, qv_bias, w_proj, proj_bias, w_up, up_bias, w_down, down_bias,
     norm1_gain, norm1_shift, norm2_gain, norm2_shift, rel_rows, rel_cols, cotangent) = args
    ratio = dp_size // RING
    weights = [w_qkv, w_proj, w_up, w_down]
    dims = (1, 0, 0, 0)
    groups = [[i * ratio + j for j in range(ratio)] for i in range(RING)]
    across = [[i * ratio + j for i in range(RING)] for j in range(ratio)]
    if ratio > 1:
        weights = [
            lax.all_gather(w, "dp", axis=dim, tiled=True, axis_index_groups=groups)
            for w, dim in zip(weights, dims)
        ]
    outs = fused_block(
        ratio,
        (tokens, cotangent, *weights, qv_bias, proj_bias, up_bias, down_bias,
         norm1_gain, norm1_shift, norm2_gain, norm2_shift, rel_rows, rel_cols),
    )
    block_out, grad_tokens, *grads, small, rel = outs
    if ratio > 1:
        grads = [
            lax.psum_scatter(g, "dp", scatter_dimension=dim, tiled=True, axis_index_groups=groups)
            for g, dim in zip(grads, dims)
        ]
        small, rel = lax.psum((small, rel), "dp", axis_index_groups=groups)
    return hand_out(block_out, grad_tokens, grads, small, rel)


def solution(mesh):
    split = P("dp", "tensor", None)
    specs = (split, P(None, "dp", "tensor"), P(), P(("tensor", "dp"), None), P(), P("dp", "tensor"), P(),
             P(("tensor", "dp"), None))
    return jax.shard_map(
        functools.partial(on_device, mesh.shape["dp"]),
        mesh=mesh,
        in_specs=specs + (P(),) * 7 + (split,),
        out_specs=(split,) + specs + (P(),) * 7,
        check_vma=False,
    )
```

```python
import functools

import jax
import jax.numpy as jnp
from jax import lax
from jax.experimental import pallas as pl
from jax.experimental.pallas import tpu as pltpu
from jax.sharding import PartitionSpec as P

D = 768
HD = 64
FF = 3072
GRID = 16
TOK = 256
RELS = 31
NZ, NX, NC = 4, 2, 2
RING = NZ * NX * NC
IMG = 2
PAIR = 2 * HD
CH = 64
EPS = 1e-06
F32 = jnp.float32
BF = jnp.bfloat16
MESH = pl.DeviceIdType.MESH
SCALE = HD ** (-0.5)
QKV_M, PROJ_M, UP_M, DOWN_M = range(4)


def nn(a, b):
    return lax.dot_general(a, b, (((1,), (0,)), ((), ())), preferred_element_type=F32)


def nt(a, b):
    return lax.dot_general(a, b, (((1,), (1,)), ((), ())), preferred_element_type=F32)


def tn(a, b):
    return lax.dot_general(a, b, (((0,), (0,)), ((), ())), preferred_element_type=F32)


def iota(shape, dim):
    return lax.broadcasted_iota(jnp.int32, shape, dim)


def one_hot(cond):
    return jnp.where(cond, 1.0, 0.0).astype(BF)


def mean_last(v):
    return jnp.sum(v, axis=-1, keepdims=True) * (1.0 / v.shape[-1])


def normalize(v):
    centred = v - mean_last(v)
    rstd = lax.rsqrt(mean_last(centred * centred) + EPS)
    return centred * rstd, rstd


def norm_back(grad, n, rstd, gain):
    e = grad * gain
    return (e - mean_last(e) - n * mean_last(e * n)) * rstd


def spread_rows(v):
    return jnp.concatenate(
        [pltpu.roll(v[g * GRID : (g + 1) * GRID], g, 1) if g else v[:GRID] for g in range(GRID)], axis=0
    )


def spread_cols(v):
    return jnp.concatenate(
        [
            pltpu.roll(v[g * GRID : (g + 1) * GRID], 0, 1, stride=1, stride_axis=0)
            for g in range(GRID)
        ],
        axis=0,
    )


NAMES_IN = (
    "tok", "cot", "sq", "sp", "su", "sd",
    "qvb", "pjb", "upb", "dnb", "g1", "b1",
    "g2", "b2", "relr", "relc",
)
NAMES_OUT = (
    "o_blk", "o_gtok", "o_gq", "o_gp", "o_gu", "o_gd",
    "o_sm", "o_rel",
)


def scratch_table(width, hid):
    pairs = width // PAIR
    half = TOK // 2
    shards = [(3, D // RING, width), (width // RING, D), (D // RING, hid), (hid // RING, D)]
    gathered = [shards[0], (2,) + shards[1], shards[2], shards[3]]
    table = {
        "XT": ((IMG, TOK, D), BF),
        "CT": ((IMG, TOK, D), BF),
        "WPB": ((2, width, D), BF),
        "PSH": ((2, width // RING, D), BF),
        "N1": ((IMG, TOK, D), BF),
        "FL": ((IMG, TOK, D), BF),
        "QKV": ((3, pairs, IMG, TOK, PAIR), BF),
        "PT": ((pairs, IMG, 2, TOK, TOK), BF),
        "MX": ((2, IMG, TOK, width), BF),
        "MID": ((IMG, TOK, D), F32),
        "N2": ((IMG, TOK, D), F32),
        "RS2": ((IMG, TOK, 128), F32),
        "SEC": ((IMG, TOK, D), BF),
        "ACT": ((IMG, TOK, hid), BF),
        "PHI": ((IMG, TOK, hid), BF),
        "PRE": ((IMG, TOK, hid), F32),
        "DP": ((IMG, TOK, D), BF),
        "DPR": ((IMG, half, D), BF),
        "GPRE": ((IMG, TOK, hid), BF),
        "GS": ((IMG, TOK, D), BF),
        "GSR": ((IMG, TOK, D), BF),
        "GM": ((IMG, half, D), F32),
        "MIDL": ((IMG, TOK, D), BF),
        "GMX": ((IMG, TOK, width), BF),
        "GQKV": ((3, IMG, TOK, width), BF),
        "GF": ((IMG, TOK, D), BF),
        "GFR": ((IMG, half, D), BF),
        "RG": ((PAIR, PAIR), F32),
        "TBF": ((PAIR, PAIR), BF),
        "TBB": ((PAIR, PAIR), BF),
        "OHF": ((TOK, PAIR), BF),
        "OHB": ((TOK, PAIR), BF),
        "MSK": ((4, 16, PAIR), BF),
        "PAR": ((6, 1, D), F32),
        "UPB": ((1, hid), F32),
        "S0": ((4, 8, D), F32),
        "S1": ((4, 4, D), F32),
        "S2": ((4, 32, 128), F32),
        "R0": ((7, 8, D), F32),
        "R1": ((7, 4, D), F32),
        "R2": ((7, 32, 128), F32),
    }
    for i, shard in enumerate(shards):
        table[f"W{i}"] = ((NZ, NX, NC) + gathered[i], BF)
        table[f"G{i}"] = ((NZ, NX, NC) + shard, BF)
        table[f"C{i}"] = ((NZ, NX) + shard, BF)
        table[f"X{i}"] = ((NZ,) + shard, BF)
        table[f"Z{i}"] = ((NZ - 1,) + shard, BF)
        table[f"Y{i}"] = (shard, BF)
    sems = {
        "agz": (4, 3),
        "agh": (4, 4),
        "agx": (4, 4),
        "agc": (4, 8),
        "ysem": (11,),
        "rsc": (4, 4),
        "rsx": (4, 4),
        "rsz": (4, 3),
        "rsy": (4, 1),
        "ars": (3, 7),
    }
    return table, sems, shards


class Refs:
    pass


def block_kernel(ratio, width, hid, names, *refs):
    k = Refs()
    for name, ref in zip(names, refs):
        setattr(k, name, ref)
    pairs = width // PAIR
    half = TOK // 2
    dp = lax.axis_index("dp")
    t = lax.axis_index("tensor")
    sub = lax.rem(dp, ratio)
    s = dp // ratio
    z, x, c = s // (NX * NC), lax.rem(s // NC, NX), lax.rem(s, NC)

    def device(zz, xx, cc, tt=t):
        return (((zz * NX + xx) * NC + cc) * ratio + sub, tt)

    z_of = (z, z + 1 - 2 * lax.rem(z, 2), lax.rem(z + 2, NZ), NZ - 1 - z)
    core_peer, x_peer, y_peer = device(z, x, 1 - c), device(z, 1 - x, c), device(z, x, c, 1 - t)
    xy_peer = device(z, 1 - x, c, 1 - t)
    z_peer = [device(zz, x, c) for zz in z_of]
    own0 = pl.multiple_of(t * half, half)
    other0 = pl.multiple_of((1 - t) * half, half)

    def remote(src, dst, sems, idx, peer):
        return pltpu.make_async_remote_copy(
            src_ref=src,
            dst_ref=dst,
            send_sem=getattr(k, sems + "_s").at[idx],
            recv_sem=getattr(k, sems + "_r").at[idx],
            device_id=peer,
            device_id_type=MESH,
        )

    shard_in = [k.sq, k.PSH, k.su, k.sd]
    W = [k.W0, k.W1, k.W2, k.W3]
    G = [k.G0, k.G1, k.G2, k.G3]
    C = [k.C0, k.C1, k.C2, k.C3]
    X = [k.X0, k.X1, k.X2, k.X3]
    Z = [k.Z0, k.Z1, k.Z2, k.Z3]
    Y = [k.Y0, k.Y1, k.Y2, k.Y3]

    side = z // 2
    relayed = (PROJ_M, UP_M, DOWN_M)
    broad = ()
    middle_chip = (z == 1) | (z == 2)
    relay_of = (z, z_of[1], 2 - side, 3 - 3 * side)
    origin = [relay_of if m in relayed else z_of for m in range(4)]

    def piece(m, i, other=False):
        if m in broad:
            return W[m].at[origin[m][i], :, c]
        if i == 0 and not other:
            return shard_in[m]
        return W[m].at[origin[m][i], 1 - x if other else x, c]

    def ag_z(m, i):
        dst = W[m].at[z, :, c] if m in broad else W[m].at[z, x, c]
        return remote(piece(m, 0), dst, "agz", (m, i - 1), z_peer[i])

    def ag_relay(m, n):
        i, arrives, peer = ((0, 2, 3), (1, 3, 3), (2, 2, 1), (3, 3, 1))[n]
        return pltpu.make_async_remote_copy(
            src_ref=piece(m, i),
            dst_ref=piece(m, i) if m in broad else W[m].at[origin[m][i], x, c],
            send_sem=k.agh_s.at[m, n],
            recv_sem=k.agz_r.at[m, arrives - 1],
            device_id=z_peer[peer],
            device_id_type=MESH,
        )

    def relay(m, n):
        @pl.when(middle_chip)
        def _():
            ag_relay(m, n).start()

    def ag_x(m, i):
        src = shard_in[m] if m in broad else piece(m, i)
        return remote(src, W[m].at[origin[m][i], x, c], "agx", (m, i), x_peer)

    def ag_c(m, i, other):
        if m in broad:
            return remote(piece(m, i), piece(m, i), "agc", (m, i), core_peer)
        xx = 1 - x if other else x
        return remote(piece(m, i, other), W[m].at[origin[m][i], xx, c], "agc", (m, i + 4 * other), core_peer)

    def ag_send(m, slots=(1,)):
        if m in broad:
            ag_x(m, 0).wait_recv()
            ag_c(m, 0, 0).start()
        for i in slots:
            ag_z(m, i).start()
        if m in relayed:
            relay(m, 0)

    def ag_own(m):
        ag_x(m, 0).start()
        if m not in broad:
            ag_c(m, 0, 0).start()

    def ag_on(m, i, cross=True):
        if m not in broad and cross:
            ag_x(m, i).start()
        ag_c(m, i, 0).start()

    def ag_pass(m, slots, cross=True):
        for i in slots:
            ag_z(m, i).wait_recv()
            if m in relayed:
                relay(m, i)
            ag_on(m, i, cross)

    def ag_pass_middle(*pairs, cross=True):
        @pl.when(middle_chip)
        def _():
            for m, i in pairs:
                ag_z(m, i).wait_recv()
                ag_relay(m, i).start()
                ag_on(m, i, cross)

    def ag_pass_end(*pairs, cross=True):
        @pl.when(jnp.logical_not(middle_chip))
        def _():
            for m, i in pairs:
                ag_z(m, i).wait_recv()
                ag_on(m, i, cross)

    def ag_late_cross(m, slots):
        for i in slots:
            ag_x(m, i).start()

    def ag_cross(m, slots=(0, 1, 2, 3)):
        for i in slots:
            ag_x(m, i).wait_recv()
            ag_c(m, i, 1).start()

    def ag_done(m, pieces=range(NZ)):
        for other in (0,) if m in broad else (0, 1):
            for i in pieces:
                ag_c(m, i, other).wait_recv()

    def rs_core(m, i):
        at = relay_of[i]
        return remote(G[m].at[at, :, 1 - c], C[m].at[at], "rsc", (m, i), core_peer)

    def rs_core_send(m, slots=(3, 2, 1, 0)):
        for i in slots:
            rs_core(m, i).start()

    def rs_x(m, i):
        return remote(G[m].at[relay_of[i], 1 - x, c], X[m].at[i], "rsx", (m, i), x_peer)

    via = jnp.where(middle_chip, 1, 2)
    straight = (PROJ_M, QKV_M)

    def rs_z(m, i):
        slot = (None, 0, via, via if m in straight else 1)[i]
        return pltpu.make_async_remote_copy(
            src_ref=G[m].at[relay_of[i], x, c],
            dst_ref=Z[m].at[slot],
            send_sem=k.rsz_s.at[m, i - 1],
            recv_sem=k.rsz_r.at[m, slot],
            device_id=device(relay_of[i], x, c),
            device_id_type=MESH,
        )

    def rs_arrived(m, slot):
        pltpu.make_async_remote_copy(
            src_ref=Z[m].at[slot],
            dst_ref=Z[m].at[slot],
            send_sem=k.rsz_s.at[m, slot],
            recv_sem=k.rsz_r.at[m, slot],
            device_id=z_peer[1],
            device_id_type=MESH,
        ).wait_recv()

    def rs_y(m):
        return remote(G[m].at[relay_of[3], x, c], Y[m], "rsy", (m, 0), z_peer[1])

    def rs_relay(m):
        @pl.when(middle_chip)
        def _():
            rs_y(m).wait_recv()
            add_into(G[m], (relay_of[3], x, c), Y[m], ())
            rs_z(m, 3).start()

    def add_into(dst, where, src, which):
        if len(dst.shape) - len(where) == 3:
            for j in range(3):
                dst[(*where, j)] = dst[(*where, j)] + src[(*which, j)]
        else:
            dst[where] = dst[where] + src[which or ...]

    def rs_core_done(m, slots=(3, 2, 1, 0)):
        for i in slots:
            rs_core(m, i).wait_recv()
            for xx in range(NX):
                add_into(G[m], (relay_of[i], xx, c), C[m], (relay_of[i], xx))

    queue = [(m, i) for m in (DOWN_M, UP_M, PROJ_M, QKV_M) for i in (3, 2, 1, 0)]
    fed, taken = list(queue), list(queue)

    def rs_feed(count):
        for _ in range(count):
            rs_x(*fed.pop(0)).start()

    def rs_take(count, feed=0):
        for _ in range(count):
            m, i = taken.pop(0)
            rs_x(m, i).wait_recv()
            if feed:
                rs_feed(1)
                feed -= 1
            add_into(G[m], (relay_of[i], x, c), X[m], (i,))
            if i == 3 and m not in straight:

                @pl.when(jnp.logical_not(middle_chip))
                def _():
                    rs_y(m).start()

            elif i:
                rs_z(m, i).start()

    def rs_done(m, out):
        rs_arrived(m, 0)
        rs_arrived(m, 1)
        parts = range(3) if m == QKV_M else (None,)

        def add_slots(start, slots):
            for j in parts:
                at = () if j is None else (j,)
                here = ... if j is None else j
                total = start(at, here)
                for slot in slots:
                    total = total + Z[m][(slot, *at)].astype(F32)
                out[here] = total

        own = lambda at, here: G[m][(z, x, c, *at)].astype(F32)
        if m in straight:
            rs_arrived(m, 2)
            return add_slots(own, (0, 1, 2))
        add_slots(own, (0, 1))

        @pl.when(middle_chip)
        def _():
            rs_arrived(m, 2)
            add_slots(lambda at, here: out[here], (2,))

    S = [k.S0, k.S1, k.S2]
    R = [k.R0, k.R1, k.R2]
    hops = ((0,), (1, 2, 3), (4, 5, 6))

    def ar(b, i):
        step = 0 if i == 0 else 1 if i < 4 else 2
        peer = ([core_peer, x_peer, y_peer, xy_peer] + z_peer[1:])[i]
        return remote(S[b].at[step], R[b].at[i], "ars", (b, i), peer)

    def ar_send(step, *which):
        for b in which:
            for i in hops[step]:
                ar(b, i).start()

    def ar_done(step, *which):
        for b in which:
            for i in hops[step]:
                ar(b, i).wait_recv()
            if step == 0:
                S[b][1] = S[b][0] + R[b][0]
            else:
                first, i = S[b][step], hops[step][0]
                S[b][step + 1] = (first + R[b][i]) + (R[b][i + 1] + R[b][i + 2])

    def y_rows(img, base):
        return (img, pl.ds(base, half))

    def y_tok():
        return remote(k.tok, k.XT.at[:, pl.ds(own0, half)], "ysem", (0,), y_peer)

    def y_cot():
        return remote(k.cot, k.CT.at[:, pl.ds(own0, half)], "ysem", (1,), y_peer)

    def y_attn(img):
        return remote(k.MX.at[t, img], k.MX.at[t, img], "ysem", (2 + img,), y_peer)

    def y_proj():
        return remote(k.sp, k.PSH.at[t], "ysem", (10,), y_peer)

    def y_mlp(img):
        return remote(k.DP.at[img, pl.ds(other0, half)], k.DPR.at[img], "ysem", (4 + img,), y_peer)

    def y_sec(img):
        return remote(k.GS.at[img], k.GSR.at[img], "ysem", (6 + img,), y_peer)

    def y_first(img):
        return remote(k.GF.at[img, pl.ds(other0, half)], k.GFR.at[img], "ysem", (8 + img,), y_peer)

    def rows(base, i):
        return pl.ds(pl.multiple_of(base + i * CH, CH), CH)

    barrier = pltpu.get_barrier_semaphore()
    peers = [core_peer, x_peer, y_peer, xy_peer] + z_peer[1:]
    for peer in peers:
        pl.semaphore_signal(barrier, inc=1, device_id=peer, device_id_type=MESH)
    pl.semaphore_wait(barrier, len(peers))

    ag_send(QKV_M, (1, 2))
    y_proj().start()
    y_tok().start()
    ag_own(QKV_M)

    for row, ref in enumerate((k.g1, k.b1, k.g2, k.b2, k.pjb, k.dnb)):
        k.PAR[row] = ref[...].reshape(1, D)
    g1, b1, g2, b2, pjb, dnb = (k.PAR.at[row] for row in range(6))
    k.UPB[...] = k.upb[pl.ds(pl.multiple_of(t * hid, 128), hid)].reshape(1, hid)
    lane = iota((TOK, PAIR), 1)
    lane64 = lax.rem(lane, HD)
    urow, ucol = iota((TOK, PAIR), 0) // GRID, lax.rem(iota((TOK, PAIR), 0), GRID)
    shifted = lax.rem(lane + (PAIR - GRID + 1), HD)
    seg, pos = shifted // GRID, lax.rem(shifted, GRID)
    k.OHF[...] = one_hot(((seg < 2) & (urow == pos)) | ((seg >= 2) & (ucol == pos)))
    k.OHB[...] = one_hot(
        ((lane64 < GRID) & (urow == GRID - 1 - lane64))
        | ((lane64 >= 2 * GRID) & (lane64 < 3 * GRID) & (ucol == 3 * GRID - 1 - lane64))
    )
    mlane = iota((16, PAIR), 1)
    in_first = mlane < HD
    ext_first = (mlane >= GRID - 1) & (mlane < HD + GRID - 1)
    k.MSK[0] = one_hot(in_first)
    k.MSK[1] = one_hot(mlane >= HD)
    k.MSK[2] = one_hot(ext_first)
    k.MSK[3] = one_hot((mlane < GRID - 1) | (mlane >= HD + GRID - 1))
    tl, td = iota((PAIR, RELS), 0), iota((PAIR, RELS), 1)
    fwd_tab = jnp.zeros((PAIR, PAIR), F32)
    bwd_tab = jnp.zeros((PAIR, PAIR), F32)
    for head in range(2):
        place = one_hot(iota((HD, PAIR), 1) == iota((HD, PAIR), 0) + head * HD)
        for base, rel in ((0, k.relr), (32, k.relc)):
            wide = nn(rel[...], place).astype(BF)
            at = tl - (head * HD + base)
            fwd_tab = fwd_tab + nn(one_hot(at == RELS - 1 - td), wide)
            bwd_tab = bwd_tab + nn(one_hot(at == td), wide)
    k.TBF[...] = fwd_tab.astype(BF)
    k.TBB[...] = bwd_tab.astype(BF)
    k.S0[0] = jnp.zeros((8, D), F32)
    k.S1[0] = jnp.zeros((4, D), F32)
    k.RG[...] = jnp.zeros((PAIR, PAIR), F32)

    def first_norm(base):
        @pl.loop(0, IMG)
        def _(img):
            @pl.loop(0, half // CH)
            def _(i):
                at = rows(base, i)
                n, _ = normalize(k.XT[img, at].astype(F32))
                k.N1[img, at] = n.astype(BF)
                k.FL[img, at] = (n * g1[...] + b1[...]).astype(BF)

    for img in range(IMG):
        k.XT[img, pl.ds(own0, half)] = k.tok[img]
        k.CT[img, pl.ds(own0, half)] = k.cot[img]
    k.PSH[t] = k.sp[...]
    y_proj().wait_recv()
    ag_own(PROJ_M)
    ag_own(UP_M)
    first_norm(own0)
    ag_send(QKV_M, (3,))
    for m in range(4):
        W[m][z, x, c] = shard_in[m][...]
    ag_pass(QKV_M, (1, 2))
    ag_send(PROJ_M)
    ag_send(UP_M)
    ag_pass(QKV_M, (3,))
    y_tok().wait_recv()
    y_cot().start()
    first_norm(other0)
    ag_pass(PROJ_M, (1,))
    ag_pass(UP_M, (1,))
    ag_pass_middle((PROJ_M, 2), (UP_M, 2))
    ag_cross(QKV_M)
    ag_done(QKV_M)

    lanes_w = pl.ds(pl.multiple_of(t * width, 128), width)
    for i in range(3):

        @pl.loop(0, IMG)
        def _(img):
            out = nn(k.FL[img], W[0][:, :, :, i].reshape(D, width))
            if i != 1:
                out = out + k.qvb[i // 2 : i // 2 + 1, lanes_w]
            low = out.astype(BF)
            for p in range(pairs):
                k.QKV[i, p, img] = low[:, p * PAIR : (p + 1) * PAIR]

    ag_pass_end((PROJ_M, 2), (UP_M, 2))
    ag_pass_middle((PROJ_M, 3), (UP_M, 3))
    ag_send(DOWN_M)
    ag_own(DOWN_M)

    def head_mask(i):
        return k.MSK[i][0:1]

    def attend(step):
        img, p = step // pairs, lax.rem(step, pairs)
        q, key, val = k.QKV[0, p, img], k.QKV[1, p, img], k.QKV[2, p, img]
        qr = nt(q, k.TBF[...])
        ext = jnp.where(
            (lane64 >= 15) & (lane64 < 31),
            spread_rows(qr),
            jnp.where((lane64 >= 47) & (lane64 < 63), spread_cols(qr), 0.0),
        )
        high = ext.astype(BF).astype(F32)
        ext = (high + pltpu.roll(ext - high, GRID, 1)).astype(BF)
        k_ext = jnp.concatenate([key, k.OHF[...]], axis=1)
        probs, vals = [], []
        for head in range(2):
            q_ext = jnp.concatenate(
                [q * (head_mask(head) * SCALE).astype(BF), ext * head_mask(2 + head)], axis=1
            )
            scores = nt(k_ext, q_ext)
            e = jnp.exp(scores - jnp.max(scores, axis=0, keepdims=True))
            low = (e * (1.0 / jnp.sum(e, axis=0, keepdims=True))).astype(BF)
            k.PT[p, img, head] = low
            probs.append(low)
            vals.append(val * head_mask(head))
        mixed = tn(jnp.concatenate(probs, axis=0), jnp.concatenate(vals, axis=0))
        k.MX[t, img, :, pl.ds(pl.multiple_of(p * PAIR, PAIR), PAIR)] = mixed.astype(BF)

    part, each = width // NZ, width // RING

    def proj_ready(pieces):
        ag_done(PROJ_M, pieces)
        for i in pieces:
            zz = relay_of[i]
            for tt in range(2):
                for n in range(NX * NC):
                    k.G1F[n * each : (n + 1) * each] = W[1][zz, n // NC, n % NC, tt].astype(F32)
                k.WPB[tt, pl.ds(pl.multiple_of(zz * part, 16), part)] = k.G1F[...].astype(BF)

    attend(0)
    attend(1)
    attend(2)
    y_attn(0).start()
    ag_pass_end((PROJ_M, 3))
    ag_cross(PROJ_M, (0, 1))
    attend(3)
    ag_pass_end((UP_M, 3))
    ag_pass(DOWN_M, (1,))
    ag_pass_middle((DOWN_M, 2))
    attend(4)
    ag_cross(UP_M, (0, 1))
    ag_cross(PROJ_M, (2, 3))
    proj_ready((0, 1))
    attend(5)
    y_attn(1).start()
    ag_pass_middle((DOWN_M, 3))
    ag_pass_end((DOWN_M, 2))
    proj_ready((2, 3))

    def second_norm(img):
        y_attn(img).wait_recv()

        @pl.loop(0, D // 256)
        def _(j):
            cols = pl.ds(pl.multiple_of(j * 256, 256), 256)
            k.MID[img, :, cols] = nn(k.MX[0, img], k.WPB[0, :, cols]) + nn(k.MX[1, img], k.WPB[1, :, cols])

        @pl.loop(0, TOK // CH)
        def _(i):
            at = rows(0, i)
            mid = k.MID[img, at] + k.XT[img, at].astype(F32) + pjb[...]
            k.MID[img, at] = mid
            n, rstd = normalize(mid)
            k.N2[img, at] = n
            k.RS2[img, at] = jnp.broadcast_to(rstd, (CH, 128))
            k.SEC[img, at] = (n * g2[...] + b2[...]).astype(BF)

    def hidden(img):
        @pl.loop(0, hid // 256)
        def _(j):
            cols = pl.ds(pl.multiple_of(j * 256, 256), 256)
            bias = k.UPB[:, cols]
            pre = nn(k.SEC[img], W[2][:, :, :, :, cols].reshape(D, 256)) + bias
            phi = 0.5 + 0.5 * lax.erf(pre * 0.7071067811865476)
            k.ACT[img, :, cols] = (pre * phi).astype(BF)
            k.PRE[img, :, cols] = pre
            k.PHI[img, :, cols] = phi.astype(BF)

    second_norm(0)
    ag_cross(UP_M, (2, 3))
    ag_done(UP_M)
    hidden(0)
    ag_pass_end((DOWN_M, 3))
    ag_cross(DOWN_M, (0, 1))
    second_norm(1)
    hidden(1)
    ag_cross(DOWN_M, (2,))

    def down(img):
        @pl.loop(0, D // 256)
        def _(j):
            cols = pl.ds(pl.multiple_of(j * 256, 256), 256)
            k.DP[img, :, cols] = nn(k.ACT[img], W[3][:, :, :, :, cols].reshape(hid, 256)).astype(BF)

    y_cot().wait_recv()

    tile = hid // NZ

    for i in (3, 2, 1, 0):
        m = relay_of[i]
        lhs = k.ACT[:, :, pl.ds(pl.multiple_of(m * tile, 128), tile)].reshape(IMG * TOK, tile)
        for j in range(D // 256):
            cols = slice(j * 256, (j + 1) * 256)
            out = tn(lhs, k.CT[:, :, cols].reshape(IMG * TOK, 256)).astype(BF)
            G[3][m, :, :, :, cols] = out.reshape(NX, NC, hid // RING, 256)
        rs_core_send(DOWN_M, (i,))
        if i == 1:
            rs_core_done(DOWN_M, (3,))
            rs_feed(1)

    ag_cross(DOWN_M, (3,))
    rs_core_done(DOWN_M, (2,))
    rs_feed(1)
    per_row = D // tile
    ag_done(DOWN_M)

    def hidden_back(img):
        @pl.loop(0, NZ)
        def _(m):
            cols = pl.ds(pl.multiple_of(m * tile, 128), tile)
            pre = k.PRE[img, :, cols]
            slope = k.PHI[img, :, cols].astype(F32) + pre * (0.3989422804014327 * jnp.exp(-0.5 * pre * pre))
            grad = nt(k.CT[img], W[3][m].reshape(tile, D)) * slope
            low = grad.astype(BF)
            k.GPRE[img, :, cols] = low
            row = pl.ds(4 + t * (hid // D) + m // per_row, 1)
            lanes = pl.ds(pl.multiple_of(lax.rem(m, per_row) * tile, 128), tile)
            k.S0[0, row, lanes] = k.S0[0, row, lanes] + jnp.sum(low.astype(F32), axis=0, keepdims=True)

        @pl.loop(0, 2)
        def _(j):
            w = W[2][pl.ds(j * 2, 2)].reshape(D // 2, hid)
            k.GS[img, :, pl.ds(pl.multiple_of(j * (D // 2), 128), D // 2)] = nt(k.GPRE[img], w).astype(BF)

        y_sec(img).start()

    hidden_back(0)
    rs_core_done(DOWN_M, (1, 0))
    rs_feed(1)
    hidden_back(1)
    rs_feed(1)

    @pl.loop(0, hid // 256)
    def _(j):
        cols = pl.ds(pl.multiple_of(j * 256, 256), 256)
        rhs = k.GPRE[:, :, cols].reshape(IMG * TOK, 256)
        for m in range(2):
            lhs = k.SEC[:, :, m * (D // 2) : (m + 1) * (D // 2)].reshape(IMG * TOK, D // 2)
            out = tn(lhs, rhs).astype(BF)
            G[2][2 * m : 2 * m + 2, :, :, :, cols] = out.reshape(2, NX, NC, D // RING, 256)

    rs_core_send(UP_M)
    rs_take(1)
    down(0)
    rs_core_done(UP_M)
    rs_feed(2)
    down(1)
    rs_take(1, 1)

    def middle_back(img, base, own):
        zero = jnp.zeros((1, D), F32)

        def chunk(i, sums):
            at = rows(base, i)
            grad = k.GS[img, at].astype(F32) + k.GSR[img, at].astype(F32)
            n = k.N2[img, at]
            rstd = jnp.concatenate([k.RS2[img, at]] * (D // 128), axis=1)
            cot = k.CT[img, at].astype(F32)
            gm = cot + norm_back(grad, n, rstd, g2[...])
            k.MIDL[img, at] = gm.astype(BF)
            if own:
                k.GM[img, rows(0, i)] = gm
                terms = (grad * n, grad, gm, cot)
                sums = tuple(a + jnp.sum(b, axis=0, keepdims=True) for a, b in zip(sums, terms))
            return sums

        return lax.fori_loop(0, half // CH, chunk, (zero,) * 4 if own else ())

    def middle(img):
        y_sec(img).wait_recv()
        sums = middle_back(img, own0, True)
        for row, value in enumerate(sums):
            k.S0[0, row : row + 1] = k.S0[0, row : row + 1] + value
        middle_back(img, other0, False)
        k.GMX[img] = nt(k.MIDL[img], k.WPB[t]).astype(BF)

    def attend_back(step):
        img, p = step // pairs, lax.rem(step, pairs)
        cols = pl.ds(pl.multiple_of(p * PAIR, PAIR), PAIR)
        q, key, val = k.QKV[0, p, img], k.QKV[1, p, img], k.QKV[2, p, img]
        gmx = k.GMX[img, :, cols]
        pts, gss, gms, qs, kes = [], [], [], [], []
        for head in range(2):
            m = head_mask(head)
            low = k.PT[p, img, head]
            probs = low.astype(F32)
            gp = nt(val * m, gmx)
            inner = jnp.sum(gp * probs, axis=0, keepdims=True)
            pts.append(low)
            gss.append((probs * (gp - inner)).astype(BF))
            gms.append(gmx * m)
            qs.append(q * (m * SCALE).astype(BF))
            kes.append(jnp.concatenate([key * (m * SCALE).astype(BF), k.OHB[...] * m], axis=1))
        grad_v = nn(jnp.concatenate(pts, axis=1), jnp.concatenate(gms, axis=0))
        grad_k = nn(jnp.concatenate(gss, axis=1), jnp.concatenate(qs, axis=0))
        both = tn(jnp.concatenate(gss, axis=0), jnp.concatenate(kes, axis=0))
        rel = both[:, PAIR:]
        rel = jnp.where(lane64 < 32, spread_rows(rel), spread_cols(rel))
        high = rel.astype(BF)
        rest = (rel - high.astype(F32)).astype(BF)
        grad_q = both[:, :PAIR] + nn(
            jnp.concatenate([high, rest], axis=1), jnp.concatenate([k.TBB[...]] * 2, axis=0)
        )
        k.RG[...] += tn(jnp.concatenate([high, rest], axis=0), jnp.concatenate([q, q], axis=0))
        lanes = pl.ds(pl.multiple_of(t * width + p * PAIR, PAIR), PAIR)
        for i, grad in enumerate((grad_q, grad_k, grad_v)):
            low = grad.astype(BF)
            k.GQKV[i, img, :, cols] = low
            if i != 1:
                row = i // 2
                k.S1[0, row : row + 1, lanes] = k.S1[0, row : row + 1, lanes] + jnp.sum(
                    low.astype(F32), axis=0, keepdims=True
                )

    def gradient_first(img):
        @pl.loop(0, 2)
        def _(m):
            total = jnp.zeros((TOK, D // 2), F32)
            for i in range(3):
                total = total + nt(k.GQKV[i, img], W[0][pl.ds(2 * m, 2), :, :, i].reshape(D // 2, width))
            lanes = pl.ds(pl.multiple_of(m * (D // 2), 128), D // 2)
            k.GF[img, :, lanes] = total.astype(BF)
            for row, value in ((2, total * k.N1[img, :, lanes].astype(F32)), (3, total)):
                k.S1[0, row : row + 1, lanes] = k.S1[0, row : row + 1, lanes] + jnp.sum(value, axis=0, keepdims=True)

    middle(0)
    rs_take(1, 1)
    rs_relay(DOWN_M)

    @pl.loop(0, pairs)
    def _(step):
        attend_back(step)

    rs_take(1)
    gradient_first(0)
    middle(1)
    rs_take(1)
    y_first(0).start()
    y_mlp(0).start()
    ar_send(0, 0)

    for j in range(D // 256):
        cols = slice(j * 256, (j + 1) * 256)
        out = tn(k.MX[t].reshape(IMG * TOK, width), k.MIDL[:, :, cols].reshape(IMG * TOK, 256))
        G[1][:, :, :, :, cols] = out.reshape(NZ, NX, NC, width // RING, 256).astype(BF)
    rs_core_send(PROJ_M)
    ar_done(0, 0)
    ar_send(1, 0)

    attend_back(pairs)
    rs_core_done(PROJ_M)
    rs_feed(1)
    rs_take(1, 1)
    rs_relay(UP_M)

    @pl.loop(pairs + 1, 2 * pairs)
    def _(step):
        attend_back(step)

    rs_take(1, 1)
    gradient_first(1)
    y_first(1).start()
    rg = k.RG[...]
    turned = pltpu.roll(rg, HD, 1)
    packed = pltpu.roll(rg[32:64] + turned[96:128], HD, 1)
    k.S2[0] = jnp.where(iota((32, 128), 1) < HD, rg[0:32] + turned[64:96], packed)
    ar_send(0, 1, 2)

    for far in (1, 0):
        part = 1 - side if far else side
        lhs = k.FL[:, :, pl.ds(pl.multiple_of(part * (D // 2), 128), D // 2)].reshape(IMG * TOK, D // 2)
        for i in range(3):
            out = tn(lhs, k.GQKV[i].reshape(IMG * TOK, width)).astype(BF)
            G[0][pl.ds(2 * part, 2), :, :, i] = out.reshape(2, NX, NC, D // RING, width)
        rs_core_send(QKV_M, (3, 2) if far else (1, 0))

    ar_done(1, 0)
    ar_send(2, 0)
    ar_done(0, 1, 2)
    ar_send(1, 1, 2)
    rs_take(1, 1)
    rs_core_done(QKV_M)
    rs_take(3, 3)

    def finish_grad(img):
        y_first(img).wait_recv()

        @pl.loop(0, half // CH)
        def _(i):
            at, here = rows(own0, i), rows(0, i)
            n, rstd = normalize(k.tok[img, here].astype(F32))
            grad = k.GF[img, at].astype(F32) + k.GFR[img, here].astype(F32)
            k.o_gtok[img, here] = k.GM[img, here] + norm_back(grad, n, rstd, g1[...])

    def finish_block(img):
        y_mlp(img).wait_recv()

        @pl.loop(0, half // CH)
        def _(i):
            at, here = rows(own0, i), rows(0, i)
            k.o_blk[img, here] = (
                k.MID[img, at] + k.DP[img, at].astype(F32) + k.DPR[img, here].astype(F32) + dnb[...]
            ).astype(BF)

    finish_grad(0)
    rs_take(1, 1)
    rs_take(1)
    finish_block(0)
    finish_grad(1)
    y_mlp(1).start()
    ar_done(1, 1, 2)
    ar_send(2, 1, 2)
    rs_done(DOWN_M, k.o_gd)
    rs_take(1)
    rs_done(UP_M, k.o_gu)
    ar_done(2, 0)
    rs_done(PROJ_M, k.o_gp)
    finish_block(1)
    rs_take(1)
    ar_done(2, 1, 2)
    k.o_sm[0:8] = k.S0[3]
    k.o_sm[8:12] = k.S1[3]
    k.o_rel[...] = k.S2[3]
    rs_take(1)
    rs_done(QKV_M, k.o_gq)

    @pl.when(middle_chip)
    def _():
        for m in relayed:
            for n in range(4):
                ag_relay(m, n).wait_send()
        for m in range(4):
            if m not in straight:
                rs_z(m, 3).wait_send()

    @pl.when(jnp.logical_not(middle_chip))
    def _():
        for m in range(4):
            if m not in straight:
                rs_y(m).wait_send()

    for m in range(4):
        for i in (1, 2, 3):
            if i == 1 or m not in relayed:
                ag_z(m, i).wait_send()
            if i != 3 or m in straight:
                rs_z(m, i).wait_send()
        for i in range(4):
            if i == 0 or m not in broad:
                ag_x(m, i).wait_send()
            ag_c(m, i, 0).wait_send()
            if m not in broad:
                ag_c(m, i, 1).wait_send()
            rs_x(m, i).wait_send()
            rs_core(m, i).wait_send()
    for copy in (y_tok(), y_cot(), y_proj()):
        copy.wait_send()
    for img in range(IMG):
        for make in (y_attn, y_mlp, y_sec, y_first):
            make(img).wait_send()
    for b in range(3):
        for i in range(7):
            ar(b, i).wait_send()


def fused_block(ratio, args):
    width, hid = args[2].shape[2], args[4].shape[1]
    table, sems, shards = scratch_table(width, hid)
    table["G1F"] = ((width // NZ, D), F32)
    names = list(NAMES_IN) + list(NAMES_OUT) + list(table)
    scratch = [pltpu.VMEM(shape, kind) for shape, kind in table.values()]
    for name, shape in sems.items():
        names += [name + "_s", name + "_r"]
        scratch += [pltpu.SemaphoreType.DMA(shape)] * 2
    tok = args[0].shape
    outs = [(tok, BF), (tok, F32)] + [(shape, F32) for shape in shards] + [((16, D), F32), ((32, 128), F32)]
    vmem = pl.BlockSpec(memory_space=pltpu.VMEM)
    return pl.pallas_call(
        functools.partial(block_kernel, ratio, width, hid, names),
        out_shape=[jax.ShapeDtypeStruct(shape, kind) for shape, kind in outs],
        in_specs=[vmem] * len(NAMES_IN),
        out_specs=[vmem] * len(outs),
        scratch_shapes=scratch,
        compiler_params=pltpu.CompilerParams(
            collective_id=0, has_side_effects=True, vmem_limit_bytes=62 << 20
        ),
        name="fused_block",
    )(*args)


def finish_kernel(*refs):
    big, (small, rel), outs = refs[:6], refs[6:8], refs[8:24]
    held, sem_in, sem = refs[24:30], refs[30], refs[31]
    where = (0, 1, 2, 4, 6, 8)
    loads = [pltpu.make_async_copy(src, dst, sem_in.at[n]) for n, (src, dst) in enumerate(zip(big, held))]
    copies = [pltpu.make_async_copy(src, outs[i], sem.at[n]) for n, (src, i) in enumerate(zip(held, where))]
    for copy in loads:
        copy.start()
    for load, copy in zip(loads, copies):
        load.wait()
        copy.start()
    outs[3][...] = small[8:10]
    for i, row in ((5, 2), (9, 3), (10, 10), (11, 11), (12, 0), (13, 1)):
        outs[i][...] = small[row : row + 1].reshape(D)
    for j in range(FF // D):
        outs[7][j * D : (j + 1) * D] = small[4 + j : 5 + j].reshape(D)
    outs[14][...] = rel[:RELS, :HD]
    outs[15][...] = rel[:RELS, HD:]
    for copy in copies:
        copy.wait()


def hand_out(block_out, grad_tokens, grads, small, rel):
    big = [block_out, grad_tokens, *grads]
    vec = jax.ShapeDtypeStruct((D,), F32)
    table = jax.ShapeDtypeStruct((RELS, HD), F32)
    like = [jax.ShapeDtypeStruct(v.shape, v.dtype) for v in big]
    outs = [like[0], like[1], like[2], jax.ShapeDtypeStruct((2, D), F32), like[3], vec, like[4],
            jax.ShapeDtypeStruct((FF,), F32), like[5], vec, vec, vec, vec, vec, table, table]
    vmem, whole = pl.BlockSpec(memory_space=pltpu.VMEM), pl.BlockSpec(memory_space=pl.ANY)
    return pl.pallas_call(
        finish_kernel,
        out_shape=outs,
        in_specs=[whole] * 6 + [vmem] * 2,
        out_specs=[whole if i in (0, 1, 2, 4, 6, 8) else vmem for i in range(16)],
        scratch_shapes=[pltpu.VMEM(v.shape, v.dtype) for v in big] + [pltpu.SemaphoreType.DMA((6,))] * 2,
        compiler_params=pltpu.CompilerParams(vmem_limit_bytes=62 << 20),
        name="hand_out",
    )(*big, small, rel)


def on_device(dp_size, *args):
    (tokens, w_qkv, qv_bias, w_proj, proj_bias, w_up, up_bias, w_down, down_bias,
     norm1_gain, norm1_shift, norm2_gain, norm2_shift, rel_rows, rel_cols, cotangent) = args
    ratio = dp_size // RING
    weights = [w_qkv, w_proj, w_up, w_down]
    dims = (1, 0, 0, 0)
    groups = [[i * ratio + j for j in range(ratio)] for i in range(RING)]
    across = [[i * ratio + j for i in range(RING)] for j in range(ratio)]
    if ratio > 1:
        weights = [
            lax.all_gather(w, "dp", axis=dim, tiled=True, axis_index_groups=groups)
            for w, dim in zip(weights, dims)
        ]
    outs = fused_block(
        ratio,
        (tokens, cotangent, *weights, qv_bias, proj_bias, up_bias, down_bias,
         norm1_gain, norm1_shift, norm2_gain, norm2_shift, rel_rows, rel_cols),
    )
    block_out, grad_tokens, *grads, small, rel = outs
    if ratio > 1:
        grads = [
            lax.psum_scatter(g, "dp", scatter_dimension=dim, tiled=True, axis_index_groups=groups)
            for g, dim in zip(grads, dims)
        ]
        small, rel = lax.psum((small, rel), "dp", axis_index_groups=groups)
    return hand_out(block_out, grad_tokens, grads, small, rel)


def solution(mesh):
    split = P("dp", "tensor", None)
    specs = (split, P(None, "dp", "tensor"), P(), P(("tensor", "dp"), None), P(), P("dp", "tensor"), P(),
             P(("tensor", "dp"), None))
    return jax.shard_map(
        functools.partial(on_device, mesh.shape["dp"]),
        mesh=mesh,
        in_specs=specs + (P(),) * 7 + (split,),
        out_specs=(split,) + specs + (P(),) * 7,
        check_vma=False,
    )
```

```python
import functools

import jax
import jax.numpy as jnp
from jax import lax
from jax.experimental import pallas as pl
from jax.experimental.pallas import tpu as pltpu
from jax.sharding import PartitionSpec as P

D = 768
HD = 64
FF = 3072
GRID = 16
TOK = 256
RELS = 31
NZ, NX, NC = 4, 2, 2
RING = NZ * NX * NC
IMG = 2
PAIR = 2 * HD
CH = 64
EPS = 1e-06
F32 = jnp.float32
BF = jnp.bfloat16
MESH = pl.DeviceIdType.MESH
SCALE = HD ** (-0.5)
QKV_M, PROJ_M, UP_M, DOWN_M = range(4)


def nn(a, b):
    return lax.dot_general(a, b, (((1,), (0,)), ((), ())), preferred_element_type=F32)


def nt(a, b):
    return lax.dot_general(a, b, (((1,), (1,)), ((), ())), preferred_element_type=F32)


def tn(a, b):
    return lax.dot_general(a, b, (((0,), (0,)), ((), ())), preferred_element_type=F32)


def iota(shape, dim):
    return lax.broadcasted_iota(jnp.int32, shape, dim)


def one_hot(cond):
    return jnp.where(cond, 1.0, 0.0).astype(BF)


def mean_last(v):
    return jnp.sum(v, axis=-1, keepdims=True) * (1.0 / v.shape[-1])


def normalize(v):
    centred = v - mean_last(v)
    rstd = lax.rsqrt(mean_last(centred * centred) + EPS)
    return centred * rstd, rstd


def norm_back(grad, n, rstd, gain):
    e = grad * gain
    return (e - mean_last(e) - n * mean_last(e * n)) * rstd


def spread_rows(v):
    return jnp.concatenate(
        [pltpu.roll(v[g * GRID : (g + 1) * GRID], g, 1) if g else v[:GRID] for g in range(GRID)], axis=0
    )


def spread_cols(v):
    return jnp.concatenate(
        [
            pltpu.roll(v[g * GRID : (g + 1) * GRID], 0, 1, stride=1, stride_axis=0)
            for g in range(GRID)
        ],
        axis=0,
    )


NAMES_IN = (
    "tok", "cot", "sq", "sp", "su", "sd",
    "qvb", "pjb", "upb", "dnb", "g1", "b1",
    "g2", "b2", "relr", "relc",
)
NAMES_OUT = (
    "h_blk", "h_gtok", "o_gq", "h_gp", "h_gu", "h_gd",
    "o_sm", "o_rel",
)


def scratch_table(width, hid):
    pairs = width // PAIR
    half = TOK // 2
    shards = [(3, D // RING, width), (width // RING, D), (D // RING, hid), (hid // RING, D)]
    gathered = [shards[0], (2,) + shards[1], shards[2], shards[3]]
    table = {
        "XT": ((IMG, TOK, D), BF),
        "CT": ((IMG, TOK, D), BF),
        "WPB": ((2, width, D), BF),
        "PSH": ((2, width // RING, D), BF),
        "N1": ((IMG, TOK, D), BF),
        "FL": ((IMG, TOK, D), BF),
        "QKV": ((3, pairs, IMG, TOK, PAIR), BF),
        "PT": ((pairs, IMG, 2, TOK, TOK), BF),
        "MX": ((2, IMG, TOK, width), BF),
        "MID": ((IMG, TOK, D), F32),
        "N2": ((IMG, TOK, D), F32),
        "RS2": ((IMG, TOK, 128), F32),
        "SEC": ((IMG, TOK, D), BF),
        "ACT": ((IMG, TOK, hid), BF),
        "PHI": ((IMG, TOK, hid), BF),
        "PRE": ((IMG, TOK, hid), F32),
        "DP": ((IMG, TOK, D), BF),
        "DPR": ((IMG, half, D), BF),
        "GPRE": ((IMG, TOK, hid), BF),
        "GS": ((IMG, TOK, D), BF),
        "GSR": ((IMG, TOK, D), BF),
        "GM": ((IMG, half, D), F32),
        "MIDL": ((IMG, TOK, D), BF),
        "GMX": ((IMG, TOK, width), BF),
        "GQKV": ((3, IMG, TOK, width), BF),
        "GF": ((IMG, TOK, D), BF),
        "GFR": ((IMG, half, D), BF),
        "RG": ((PAIR, PAIR), F32),
        "TBF": ((PAIR, PAIR), BF),
        "TBB": ((PAIR, PAIR), BF),
        "OHF": ((TOK, PAIR), BF),
        "OHB": ((TOK, PAIR), BF),
        "MSK": ((4, 16, PAIR), BF),
        "PAR": ((6, 1, D), F32),
        "UPB": ((1, hid), F32),
        "S0": ((4, 8, D), F32),
        "S1": ((4, 4, D), F32),
        "S2": ((4, 32, 128), F32),
        "R0": ((7, 8, D), F32),
        "R1": ((7, 4, D), F32),
        "R2": ((7, 32, 128), F32),
    }
    for i, shard in enumerate(shards):
        table[f"W{i}"] = ((NZ, NX, NC) + gathered[i], BF)
        table[f"G{i}"] = ((NZ, NX, NC) + shard, BF)
        table[f"C{i}"] = ((NZ, NX) + shard, BF)
        table[f"X{i}"] = ((NZ,) + shard, BF)
        table[f"Z{i}"] = ((NZ - 1,) + shard, BF)
        table[f"Y{i}"] = (shard, BF)
    sems = {
        "agz": (4, 3),
        "agh": (4, 4),
        "agx": (4, 4),
        "agc": (4, 8),
        "ysem": (11,),
        "rsc": (4, 4),
        "rsx": (4, 4),
        "rsz": (4, 3),
        "rsy": (4, 1),
        "outs": (5,),
        "ars": (3, 7),
    }
    return table, sems, shards


class Refs:
    pass


def block_kernel(ratio, width, hid, names, *refs):
    k = Refs()
    for name, ref in zip(names, refs):
        setattr(k, name, ref)
    pairs = width // PAIR
    half = TOK // 2
    dp = lax.axis_index("dp")
    t = lax.axis_index("tensor")
    sub = lax.rem(dp, ratio)
    s = dp // ratio
    z, x, c = s // (NX * NC), lax.rem(s // NC, NX), lax.rem(s, NC)

    def device(zz, xx, cc, tt=t):
        return (((zz * NX + xx) * NC + cc) * ratio + sub, tt)

    z_of = (z, z + 1 - 2 * lax.rem(z, 2), lax.rem(z + 2, NZ), NZ - 1 - z)
    core_peer, x_peer, y_peer = device(z, x, 1 - c), device(z, 1 - x, c), device(z, x, c, 1 - t)
    xy_peer = device(z, 1 - x, c, 1 - t)
    z_peer = [device(zz, x, c) for zz in z_of]
    own0 = pl.multiple_of(t * half, half)
    other0 = pl.multiple_of((1 - t) * half, half)

    def remote(src, dst, sems, idx, peer):
        return pltpu.make_async_remote_copy(
            src_ref=src,
            dst_ref=dst,
            send_sem=getattr(k, sems + "_s").at[idx],
            recv_sem=getattr(k, sems + "_r").at[idx],
            device_id=peer,
            device_id_type=MESH,
        )

    shard_in = [k.sq, k.PSH, k.su, k.sd]
    W = [k.W0, k.W1, k.W2, k.W3]
    G = [k.G0, k.G1, k.G2, k.G3]
    C = [k.C0, k.C1, k.C2, k.C3]
    X = [k.X0, k.X1, k.X2, k.X3]
    Z = [k.Z0, k.Z1, k.Z2, k.Z3]
    Y = [k.Y0, k.Y1, k.Y2, k.Y3]

    side = z // 2
    relayed = (PROJ_M, UP_M, DOWN_M)
    broad = ()
    middle_chip = (z == 1) | (z == 2)
    relay_of = (z, z_of[1], 2 - side, 3 - 3 * side)
    origin = [relay_of if m in relayed else z_of for m in range(4)]

    def piece(m, i, other=False):
        if m in broad:
            return W[m].at[origin[m][i], :, c]
        if i == 0 and not other:
            return shard_in[m]
        return W[m].at[origin[m][i], 1 - x if other else x, c]

    def ag_z(m, i):
        dst = W[m].at[z, :, c] if m in broad else W[m].at[z, x, c]
        return remote(piece(m, 0), dst, "agz", (m, i - 1), z_peer[i])

    def ag_relay(m, n):
        i, arrives, peer = ((0, 2, 3), (1, 3, 3), (2, 2, 1), (3, 3, 1))[n]
        return pltpu.make_async_remote_copy(
            src_ref=piece(m, i),
            dst_ref=piece(m, i) if m in broad else W[m].at[origin[m][i], x, c],
            send_sem=k.agh_s.at[m, n],
            recv_sem=k.agz_r.at[m, arrives - 1],
            device_id=z_peer[peer],
            device_id_type=MESH,
        )

    def relay(m, n):
        @pl.when(middle_chip)
        def _():
            ag_relay(m, n).start()

    def ag_x(m, i):
        src = shard_in[m] if m in broad else piece(m, i)
        return remote(src, W[m].at[origin[m][i], x, c], "agx", (m, i), x_peer)

    def ag_c(m, i, other):
        if m in broad:
            return remote(piece(m, i), piece(m, i), "agc", (m, i), core_peer)
        xx = 1 - x if other else x
        return remote(piece(m, i, other), W[m].at[origin[m][i], xx, c], "agc", (m, i + 4 * other), core_peer)

    def ag_send(m, slots=(1,)):
        if m in broad:
            ag_x(m, 0).wait_recv()
            ag_c(m, 0, 0).start()
        for i in slots:
            ag_z(m, i).start()
        if m in relayed:
            relay(m, 0)

    def ag_own(m):
        ag_x(m, 0).start()
        if m not in broad:
            ag_c(m, 0, 0).start()

    def ag_on(m, i, cross=True):
        if m not in broad and cross:
            ag_x(m, i).start()
        ag_c(m, i, 0).start()

    def ag_pass(m, slots, cross=True):
        for i in slots:
            ag_z(m, i).wait_recv()
            if m in relayed:
                relay(m, i)
            ag_on(m, i, cross)

    def ag_pass_middle(*pairs, cross=True):
        @pl.when(middle_chip)
        def _():
            for m, i in pairs:
                ag_z(m, i).wait_recv()
                ag_relay(m, i).start()
                ag_on(m, i, cross)

    def ag_pass_end(*pairs, cross=True):
        @pl.when(jnp.logical_not(middle_chip))
        def _():
            for m, i in pairs:
                ag_z(m, i).wait_recv()
                ag_on(m, i, cross)

    def ag_late_cross(m, slots):
        for i in slots:
            ag_x(m, i).start()

    def ag_cross(m, slots=(0, 1, 2, 3)):
        for i in slots:
            ag_x(m, i).wait_recv()
            ag_c(m, i, 1).start()

    def ag_done(m, pieces=range(NZ)):
        for other in (0,) if m in broad else (0, 1):
            for i in pieces:
                ag_c(m, i, other).wait_recv()

    def rs_core(m, i):
        at = relay_of[i]
        return remote(G[m].at[at, :, 1 - c], C[m].at[at], "rsc", (m, i), core_peer)

    def rs_core_send(m, slots=(3, 2, 1, 0)):
        for i in slots:
            rs_core(m, i).start()

    def rs_x(m, i):
        return remote(G[m].at[relay_of[i], 1 - x, c], X[m].at[i], "rsx", (m, i), x_peer)

    via = jnp.where(middle_chip, 1, 2)
    straight = (PROJ_M, QKV_M)

    def rs_z(m, i):
        slot = (None, 0, via, via if m in straight else 1)[i]
        return pltpu.make_async_remote_copy(
            src_ref=G[m].at[relay_of[i], x, c],
            dst_ref=Z[m].at[slot],
            send_sem=k.rsz_s.at[m, i - 1],
            recv_sem=k.rsz_r.at[m, slot],
            device_id=device(relay_of[i], x, c),
            device_id_type=MESH,
        )

    def rs_arrived(m, slot):
        pltpu.make_async_remote_copy(
            src_ref=Z[m].at[slot],
            dst_ref=Z[m].at[slot],
            send_sem=k.rsz_s.at[m, slot],
            recv_sem=k.rsz_r.at[m, slot],
            device_id=z_peer[1],
            device_id_type=MESH,
        ).wait_recv()

    def rs_y(m):
        return remote(G[m].at[relay_of[3], x, c], Y[m], "rsy", (m, 0), z_peer[1])

    def rs_relay(m):
        @pl.when(middle_chip)
        def _():
            rs_y(m).wait_recv()
            add_into(G[m], (relay_of[3], x, c), Y[m], ())
            rs_z(m, 3).start()

    def add_into(dst, where, src, which):
        if len(dst.shape) - len(where) == 3:
            for j in range(3):
                dst[(*where, j)] = dst[(*where, j)] + src[(*which, j)]
        else:
            dst[where] = dst[where] + src[which or ...]

    def rs_core_done(m, slots=(3, 2, 1, 0)):
        for i in slots:
            rs_core(m, i).wait_recv()
            for xx in range(NX):
                add_into(G[m], (relay_of[i], xx, c), C[m], (relay_of[i], xx))

    queue = [(m, i) for m in (DOWN_M, UP_M, PROJ_M, QKV_M) for i in (3, 2, 1, 0)]
    fed, taken = list(queue), list(queue)

    def rs_feed(count):
        for _ in range(count):
            rs_x(*fed.pop(0)).start()

    def rs_take(count, feed=0):
        for _ in range(count):
            m, i = taken.pop(0)
            rs_x(m, i).wait_recv()
            if feed:
                rs_feed(1)
                feed -= 1
            add_into(G[m], (relay_of[i], x, c), X[m], (i,))
            if i == 3 and m not in straight:

                @pl.when(jnp.logical_not(middle_chip))
                def _():
                    rs_y(m).start()

            elif i:
                rs_z(m, i).start()

    def rs_done(m, out):
        rs_arrived(m, 0)
        rs_arrived(m, 1)
        parts = range(3) if m == QKV_M else (None,)

        def add_slots(start, slots):
            for j in parts:
                at = () if j is None else (j,)
                here = ... if j is None else j
                total = start(at, here)
                for slot in slots:
                    total = total + Z[m][(slot, *at)].astype(F32)
                out[here] = total

        own = lambda at, here: G[m][(z, x, c, *at)].astype(F32)
        if m in straight:
            rs_arrived(m, 2)
            return add_slots(own, (0, 1, 2))
        add_slots(own, (0, 1))

        @pl.when(middle_chip)
        def _():
            rs_arrived(m, 2)
            add_slots(lambda at, here: out[here], (2,))

    S = [k.S0, k.S1, k.S2]
    R = [k.R0, k.R1, k.R2]
    hops = ((0,), (1, 2, 3), (4, 5, 6))

    def ar(b, i):
        step = 0 if i == 0 else 1 if i < 4 else 2
        peer = ([core_peer, x_peer, y_peer, xy_peer] + z_peer[1:])[i]
        return remote(S[b].at[step], R[b].at[i], "ars", (b, i), peer)

    def ar_send(step, *which):
        for b in which:
            for i in hops[step]:
                ar(b, i).start()

    def ar_done(step, *which):
        for b in which:
            for i in hops[step]:
                ar(b, i).wait_recv()
            if step == 0:
                S[b][1] = S[b][0] + R[b][0]
            else:
                first, i = S[b][step], hops[step][0]
                S[b][step + 1] = (first + R[b][i]) + (R[b][i + 1] + R[b][i + 2])

    def y_rows(img, base):
        return (img, pl.ds(base, half))

    def y_tok():
        return remote(k.tok, k.XT.at[:, pl.ds(own0, half)], "ysem", (0,), y_peer)

    def y_cot():
        return remote(k.cot, k.CT.at[:, pl.ds(own0, half)], "ysem", (1,), y_peer)

    def y_attn(img):
        return remote(k.MX.at[t, img], k.MX.at[t, img], "ysem", (2 + img,), y_peer)

    def y_proj():
        return remote(k.sp, k.PSH.at[t], "ysem", (10,), y_peer)

    def y_mlp(img):
        return remote(k.DP.at[img, pl.ds(other0, half)], k.DPR.at[img], "ysem", (4 + img,), y_peer)

    def y_sec(img):
        return remote(k.GS.at[img], k.GSR.at[img], "ysem", (6 + img,), y_peer)

    def y_first(img):
        return remote(k.GF.at[img, pl.ds(other0, half)], k.GFR.at[img], "ysem", (8 + img,), y_peer)

    def rows(base, i):
        return pl.ds(pl.multiple_of(base + i * CH, CH), CH)

    def hand_over(n):
        src, dst = ((k.o_gd, k.h_gd), (k.o_gu, k.h_gu), (k.o_gp, k.h_gp), (k.o_gtok, k.h_gtok), (k.o_blk, k.h_blk))[n]
        return pltpu.make_async_copy(src, dst, k.outs_s.at[n])

    barrier = pltpu.get_barrier_semaphore()
    peers = [core_peer, x_peer, y_peer, xy_peer] + z_peer[1:]
    for peer in peers:
        pl.semaphore_signal(barrier, inc=1, device_id=peer, device_id_type=MESH)
    pl.semaphore_wait(barrier, len(peers))

    ag_send(QKV_M, (1, 2))
    y_proj().start()
    y_tok().start()
    ag_own(QKV_M)

    for row, ref in enumerate((k.g1, k.b1, k.g2, k.b2, k.pjb, k.dnb)):
        k.PAR[row] = ref[...].reshape(1, D)
    g1, b1, g2, b2, pjb, dnb = (k.PAR.at[row] for row in range(6))
    k.UPB[...] = k.upb[pl.ds(pl.multiple_of(t * hid, 128), hid)].reshape(1, hid)
    lane = iota((TOK, PAIR), 1)
    lane64 = lax.rem(lane, HD)
    urow, ucol = iota((TOK, PAIR), 0) // GRID, lax.rem(iota((TOK, PAIR), 0), GRID)
    shifted = lax.rem(lane + (PAIR - GRID + 1), HD)
    seg, pos = shifted // GRID, lax.rem(shifted, GRID)
    k.OHF[...] = one_hot(((seg < 2) & (urow == pos)) | ((seg >= 2) & (ucol == pos)))
    k.OHB[...] = one_hot(
        ((lane64 < GRID) & (urow == GRID - 1 - lane64))
        | ((lane64 >= 2 * GRID) & (lane64 < 3 * GRID) & (ucol == 3 * GRID - 1 - lane64))
    )
    mlane = iota((16, PAIR), 1)
    in_first = mlane < HD
    ext_first = (mlane >= GRID - 1) & (mlane < HD + GRID - 1)
    k.MSK[0] = one_hot(in_first)
    k.MSK[1] = one_hot(mlane >= HD)
    k.MSK[2] = one_hot(ext_first)
    k.MSK[3] = one_hot((mlane < GRID - 1) | (mlane >= HD + GRID - 1))
    tl, td = iota((PAIR, RELS), 0), iota((PAIR, RELS), 1)
    fwd_tab = jnp.zeros((PAIR, PAIR), F32)
    bwd_tab = jnp.zeros((PAIR, PAIR), F32)
    for head in range(2):
        place = one_hot(iota((HD, PAIR), 1) == iota((HD, PAIR), 0) + head * HD)
        for base, rel in ((0, k.relr), (32, k.relc)):
            wide = nn(rel[...], place).astype(BF)
            at = tl - (head * HD + base)
            fwd_tab = fwd_tab + nn(one_hot(at == RELS - 1 - td), wide)
            bwd_tab = bwd_tab + nn(one_hot(at == td), wide)
    k.TBF[...] = fwd_tab.astype(BF)
    k.TBB[...] = bwd_tab.astype(BF)
    k.S0[0] = jnp.zeros((8, D), F32)
    k.S1[0] = jnp.zeros((4, D), F32)
    k.RG[...] = jnp.zeros((PAIR, PAIR), F32)

    def first_norm(base):
        @pl.loop(0, IMG)
        def _(img):
            @pl.loop(0, half // CH)
            def _(i):
                at = rows(base, i)
                n, _ = normalize(k.XT[img, at].astype(F32))
                k.N1[img, at] = n.astype(BF)
                k.FL[img, at] = (n * g1[...] + b1[...]).astype(BF)

    for img in range(IMG):
        k.XT[img, pl.ds(own0, half)] = k.tok[img]
        k.CT[img, pl.ds(own0, half)] = k.cot[img]
    k.PSH[t] = k.sp[...]
    y_proj().wait_recv()
    ag_own(PROJ_M)
    ag_own(UP_M)
    first_norm(own0)
    ag_send(QKV_M, (3,))
    for m in range(4):
        W[m][z, x, c] = shard_in[m][...]
    ag_pass(QKV_M, (1, 2))
    ag_send(PROJ_M)
    ag_send(UP_M)
    ag_pass(QKV_M, (3,))
    y_tok().wait_recv()
    y_cot().start()
    first_norm(other0)
    ag_pass(PROJ_M, (1,))
    ag_pass(UP_M, (1,))
    ag_pass_middle((PROJ_M, 2), (UP_M, 2))
    ag_cross(QKV_M)
    ag_done(QKV_M)

    lanes_w = pl.ds(pl.multiple_of(t * width, 128), width)
    for i in range(3):

        @pl.loop(0, IMG)
        def _(img):
            out = nn(k.FL[img], W[0][:, :, :, i].reshape(D, width))
            if i != 1:
                out = out + k.qvb[i // 2 : i // 2 + 1, lanes_w]
            low = out.astype(BF)
            for p in range(pairs):
                k.QKV[i, p, img] = low[:, p * PAIR : (p + 1) * PAIR]

    ag_pass_end((PROJ_M, 2), (UP_M, 2))
    ag_pass_middle((PROJ_M, 3), (UP_M, 3))
    ag_send(DOWN_M)
    ag_own(DOWN_M)

    def head_mask(i):
        return k.MSK[i][0:1]

    def attend(step):
        img, p = step // pairs, lax.rem(step, pairs)
        q, key, val = k.QKV[0, p, img], k.QKV[1, p, img], k.QKV[2, p, img]
        qr = nt(q, k.TBF[...])
        ext = jnp.where(
            (lane64 >= 15) & (lane64 < 31),
            spread_rows(qr),
            jnp.where((lane64 >= 47) & (lane64 < 63), spread_cols(qr), 0.0),
        )
        high = ext.astype(BF).astype(F32)
        ext = (high + pltpu.roll(ext - high, GRID, 1)).astype(BF)
        k_ext = jnp.concatenate([key, k.OHF[...]], axis=1)
        probs, vals = [], []
        for head in range(2):
            q_ext = jnp.concatenate(
                [q * (head_mask(head) * SCALE).astype(BF), ext * head_mask(2 + head)], axis=1
            )
            scores = nt(k_ext, q_ext)
            e = jnp.exp(scores - jnp.max(scores, axis=0, keepdims=True))
            low = (e * (1.0 / jnp.sum(e, axis=0, keepdims=True))).astype(BF)
            k.PT[p, img, head] = low
            probs.append(low)
            vals.append(val * head_mask(head))
        mixed = tn(jnp.concatenate(probs, axis=0), jnp.concatenate(vals, axis=0))
        k.MX[t, img, :, pl.ds(pl.multiple_of(p * PAIR, PAIR), PAIR)] = mixed.astype(BF)

    part, each = width // NZ, width // RING

    def proj_ready(pieces):
        ag_done(PROJ_M, pieces)
        for i in pieces:
            zz = relay_of[i]
            for tt in range(2):
                for n in range(NX * NC):
                    k.G1F[n * each : (n + 1) * each] = W[1][zz, n // NC, n % NC, tt].astype(F32)
                k.WPB[tt, pl.ds(pl.multiple_of(zz * part, 16), part)] = k.G1F[...].astype(BF)

    attend(0)
    attend(1)
    attend(2)
    y_attn(0).start()
    ag_pass_end((PROJ_M, 3))
    ag_cross(PROJ_M, (0, 1))
    attend(3)
    ag_pass_end((UP_M, 3))
    ag_pass(DOWN_M, (1,))
    ag_pass_middle((DOWN_M, 2))
    attend(4)
    ag_cross(UP_M, (0, 1))
    ag_cross(PROJ_M, (2, 3))
    proj_ready((0, 1))
    attend(5)
    y_attn(1).start()
    ag_pass_middle((DOWN_M, 3))
    ag_pass_end((DOWN_M, 2))
    proj_ready((2, 3))

    def second_norm(img):
        y_attn(img).wait_recv()

        @pl.loop(0, D // 256)
        def _(j):
            cols = pl.ds(pl.multiple_of(j * 256, 256), 256)
            k.MID[img, :, cols] = nn(k.MX[0, img], k.WPB[0, :, cols]) + nn(k.MX[1, img], k.WPB[1, :, cols])

        @pl.loop(0, TOK // CH)
        def _(i):
            at = rows(0, i)
            mid = k.MID[img, at] + k.XT[img, at].astype(F32) + pjb[...]
            k.MID[img, at] = mid
            n, rstd = normalize(mid)
            k.N2[img, at] = n
            k.RS2[img, at] = jnp.broadcast_to(rstd, (CH, 128))
            k.SEC[img, at] = (n * g2[...] + b2[...]).astype(BF)

    def hidden(img):
        @pl.loop(0, hid // 256)
        def _(j):
            cols = pl.ds(pl.multiple_of(j * 256, 256), 256)
            bias = k.UPB[:, cols]
            pre = nn(k.SEC[img], W[2][:, :, :, :, cols].reshape(D, 256)) + bias
            phi = 0.5 + 0.5 * lax.erf(pre * 0.7071067811865476)
            k.ACT[img, :, cols] = (pre * phi).astype(BF)
            k.PRE[img, :, cols] = pre
            k.PHI[img, :, cols] = phi.astype(BF)

    second_norm(0)
    ag_cross(UP_M, (2, 3))
    ag_done(UP_M)
    hidden(0)
    ag_pass_end((DOWN_M, 3))
    ag_cross(DOWN_M, (0, 1))
    second_norm(1)
    hidden(1)
    ag_cross(DOWN_M, (2,))

    def down(img):
        @pl.loop(0, D // 256)
        def _(j):
            cols = pl.ds(pl.multiple_of(j * 256, 256), 256)
            k.DP[img, :, cols] = nn(k.ACT[img], W[3][:, :, :, :, cols].reshape(hid, 256)).astype(BF)

    y_cot().wait_recv()

    tile = hid // NZ

    for i in (3, 2, 1, 0):
        m = relay_of[i]
        lhs = k.ACT[:, :, pl.ds(pl.multiple_of(m * tile, 128), tile)].reshape(IMG * TOK, tile)
        for j in range(D // 256):
            cols = slice(j * 256, (j + 1) * 256)
            out = tn(lhs, k.CT[:, :, cols].reshape(IMG * TOK, 256)).astype(BF)
            G[3][m, :, :, :, cols] = out.reshape(NX, NC, hid // RING, 256)
        rs_core_send(DOWN_M, (i,))
        if i == 1:
            rs_core_done(DOWN_M, (3,))
            rs_feed(1)

    ag_cross(DOWN_M, (3,))
    rs_core_done(DOWN_M, (2,))
    rs_feed(1)
    per_row = D // tile
    ag_done(DOWN_M)

    def hidden_back(img):
        @pl.loop(0, NZ)
        def _(m):
            cols = pl.ds(pl.multiple_of(m * tile, 128), tile)
            pre = k.PRE[img, :, cols]
            slope = k.PHI[img, :, cols].astype(F32) + pre * (0.3989422804014327 * jnp.exp(-0.5 * pre * pre))
            grad = nt(k.CT[img], W[3][m].reshape(tile, D)) * slope
            low = grad.astype(BF)
            k.GPRE[img, :, cols] = low
            row = pl.ds(4 + t * (hid // D) + m // per_row, 1)
            lanes = pl.ds(pl.multiple_of(lax.rem(m, per_row) * tile, 128), tile)
            k.S0[0, row, lanes] = k.S0[0, row, lanes] + jnp.sum(low.astype(F32), axis=0, keepdims=True)

        @pl.loop(0, 2)
        def _(j):
            w = W[2][pl.ds(j * 2, 2)].reshape(D // 2, hid)
            k.GS[img, :, pl.ds(pl.multiple_of(j * (D // 2), 128), D // 2)] = nt(k.GPRE[img], w).astype(BF)

        y_sec(img).start()

    hidden_back(0)
    rs_core_done(DOWN_M, (1, 0))
    rs_feed(1)
    hidden_back(1)
    rs_feed(1)

    @pl.loop(0, hid // 256)
    def _(j):
        cols = pl.ds(pl.multiple_of(j * 256, 256), 256)
        rhs = k.GPRE[:, :, cols].reshape(IMG * TOK, 256)
        for m in range(2):
            lhs = k.SEC[:, :, m * (D // 2) : (m + 1) * (D // 2)].reshape(IMG * TOK, D // 2)
            out = tn(lhs, rhs).astype(BF)
            G[2][2 * m : 2 * m + 2, :, :, :, cols] = out.reshape(2, NX, NC, D // RING, 256)

    rs_core_send(UP_M)
    rs_take(1)
    down(0)
    rs_core_done(UP_M)
    rs_feed(2)
    down(1)
    rs_take(1, 1)

    def middle_back(img, base, own):
        zero = jnp.zeros((1, D), F32)

        def chunk(i, sums):
            at = rows(base, i)
            grad = k.GS[img, at].astype(F32) + k.GSR[img, at].astype(F32)
            n = k.N2[img, at]
            rstd = jnp.concatenate([k.RS2[img, at]] * (D // 128), axis=1)
            cot = k.CT[img, at].astype(F32)
            gm = cot + norm_back(grad, n, rstd, g2[...])
            k.MIDL[img, at] = gm.astype(BF)
            if own:
                k.GM[img, rows(0, i)] = gm
                terms = (grad * n, grad, gm, cot)
                sums = tuple(a + jnp.sum(b, axis=0, keepdims=True) for a, b in zip(sums, terms))
            return sums

        return lax.fori_loop(0, half // CH, chunk, (zero,) * 4 if own else ())

    def middle(img):
        y_sec(img).wait_recv()
        sums = middle_back(img, own0, True)
        for row, value in enumerate(sums):
            k.S0[0, row : row + 1] = k.S0[0, row : row + 1] + value
        middle_back(img, other0, False)
        k.GMX[img] = nt(k.MIDL[img], k.WPB[t]).astype(BF)

    def attend_back(step):
        img, p = step // pairs, lax.rem(step, pairs)
        cols = pl.ds(pl.multiple_of(p * PAIR, PAIR), PAIR)
        q, key, val = k.QKV[0, p, img], k.QKV[1, p, img], k.QKV[2, p, img]
        gmx = k.GMX[img, :, cols]
        pts, gss, gms, qs, kes = [], [], [], [], []
        for head in range(2):
            m = head_mask(head)
            low = k.PT[p, img, head]
            probs = low.astype(F32)
            gp = nt(val * m, gmx)
            inner = jnp.sum(gp * probs, axis=0, keepdims=True)
            pts.append(low)
            gss.append((probs * (gp - inner)).astype(BF))
            gms.append(gmx * m)
            qs.append(q * (m * SCALE).astype(BF))
            kes.append(jnp.concatenate([key * (m * SCALE).astype(BF), k.OHB[...] * m], axis=1))
        grad_v = nn(jnp.concatenate(pts, axis=1), jnp.concatenate(gms, axis=0))
        grad_k = nn(jnp.concatenate(gss, axis=1), jnp.concatenate(qs, axis=0))
        both = tn(jnp.concatenate(gss, axis=0), jnp.concatenate(kes, axis=0))
        rel = both[:, PAIR:]
        rel = jnp.where(lane64 < 32, spread_rows(rel), spread_cols(rel))
        high = rel.astype(BF)
        rest = (rel - high.astype(F32)).astype(BF)
        grad_q = both[:, :PAIR] + nn(
            jnp.concatenate([high, rest], axis=1), jnp.concatenate([k.TBB[...]] * 2, axis=0)
        )
        k.RG[...] += tn(jnp.concatenate([high, rest], axis=0), jnp.concatenate([q, q], axis=0))
        lanes = pl.ds(pl.multiple_of(t * width + p * PAIR, PAIR), PAIR)
        for i, grad in enumerate((grad_q, grad_k, grad_v)):
            low = grad.astype(BF)
            k.GQKV[i, img, :, cols] = low
            if i != 1:
                row = i // 2
                k.S1[0, row : row + 1, lanes] = k.S1[0, row : row + 1, lanes] + jnp.sum(
                    low.astype(F32), axis=0, keepdims=True
                )

    def gradient_first(img):
        @pl.loop(0, 2)
        def _(m):
            total = jnp.zeros((TOK, D // 2), F32)
            for i in range(3):
                total = total + nt(k.GQKV[i, img], W[0][pl.ds(2 * m, 2), :, :, i].reshape(D // 2, width))
            lanes = pl.ds(pl.multiple_of(m * (D // 2), 128), D // 2)
            k.GF[img, :, lanes] = total.astype(BF)
            for row, value in ((2, total * k.N1[img, :, lanes].astype(F32)), (3, total)):
                k.S1[0, row : row + 1, lanes] = k.S1[0, row : row + 1, lanes] + jnp.sum(value, axis=0, keepdims=True)

    middle(0)
    rs_take(1, 1)
    rs_relay(DOWN_M)

    @pl.loop(0, pairs)
    def _(step):
        attend_back(step)

    rs_take(1)
    gradient_first(0)
    middle(1)
    rs_take(1)
    y_first(0).start()
    y_mlp(0).start()
    ar_send(0, 0)

    for j in range(D // 256):
        cols = slice(j * 256, (j + 1) * 256)
        out = tn(k.MX[t].reshape(IMG * TOK, width), k.MIDL[:, :, cols].reshape(IMG * TOK, 256))
        G[1][:, :, :, :, cols] = out.reshape(NZ, NX, NC, width // RING, 256).astype(BF)
    rs_core_send(PROJ_M)
    ar_done(0, 0)
    ar_send(1, 0)

    attend_back(pairs)
    rs_core_done(PROJ_M)
    rs_feed(1)
    rs_take(1, 1)
    rs_relay(UP_M)

    @pl.loop(pairs + 1, 2 * pairs)
    def _(step):
        attend_back(step)

    rs_take(1, 1)
    gradient_first(1)
    y_first(1).start()
    rg = k.RG[...]
    turned = pltpu.roll(rg, HD, 1)
    packed = pltpu.roll(rg[32:64] + turned[96:128], HD, 1)
    k.S2[0] = jnp.where(iota((32, 128), 1) < HD, rg[0:32] + turned[64:96], packed)
    ar_send(0, 1, 2)

    for far in (1, 0):
        part = 1 - side if far else side
        lhs = k.FL[:, :, pl.ds(pl.multiple_of(part * (D // 2), 128), D // 2)].reshape(IMG * TOK, D // 2)
        for i in range(3):
            out = tn(lhs, k.GQKV[i].reshape(IMG * TOK, width)).astype(BF)
            G[0][pl.ds(2 * part, 2), :, :, i] = out.reshape(2, NX, NC, D // RING, width)
        rs_core_send(QKV_M, (3, 2) if far else (1, 0))

    ar_done(1, 0)
    ar_send(2, 0)
    ar_done(0, 1, 2)
    ar_send(1, 1, 2)
    rs_take(1, 1)
    rs_core_done(QKV_M)
    rs_take(3, 3)

    def finish_grad(img):
        y_first(img).wait_recv()

        @pl.loop(0, half // CH)
        def _(i):
            at, here = rows(own0, i), rows(0, i)
            n, rstd = normalize(k.tok[img, here].astype(F32))
            grad = k.GF[img, at].astype(F32) + k.GFR[img, here].astype(F32)
            k.o_gtok[img, here] = k.GM[img, here] + norm_back(grad, n, rstd, g1[...])

    def finish_block(img):
        y_mlp(img).wait_recv()

        @pl.loop(0, half // CH)
        def _(i):
            at, here = rows(own0, i), rows(0, i)
            k.o_blk[img, here] = (
                k.MID[img, at] + k.DP[img, at].astype(F32) + k.DPR[img, here].astype(F32) + dnb[...]
            ).astype(BF)

    finish_grad(0)
    rs_take(1, 1)
    rs_take(1)
    finish_block(0)
    finish_grad(1)
    y_mlp(1).start()
    ar_done(1, 1, 2)
    ar_send(2, 1, 2)
    hand_over(3).start()
    rs_done(DOWN_M, k.o_gd)
    hand_over(0).start()
    rs_take(1)
    rs_done(UP_M, k.o_gu)
    hand_over(1).start()
    ar_done(2, 0)
    rs_done(PROJ_M, k.o_gp)
    hand_over(2).start()
    finish_block(1)
    hand_over(4).start()
    rs_take(1)
    ar_done(2, 1, 2)
    k.o_sm[0:8] = k.S0[3]
    k.o_sm[8:12] = k.S1[3]
    k.o_rel[...] = k.S2[3]
    rs_take(1)
    rs_done(QKV_M, k.o_gq)

    for n in range(5):
        hand_over(n).wait()

    @pl.when(middle_chip)
    def _():
        for m in relayed:
            for n in range(4):
                ag_relay(m, n).wait_send()
        for m in range(4):
            if m not in straight:
                rs_z(m, 3).wait_send()

    @pl.when(jnp.logical_not(middle_chip))
    def _():
        for m in range(4):
            if m not in straight:
                rs_y(m).wait_send()

    for m in range(4):
        for i in (1, 2, 3):
            if i == 1 or m not in relayed:
                ag_z(m, i).wait_send()
            if i != 3 or m in straight:
                rs_z(m, i).wait_send()
        for i in range(4):
            if i == 0 or m not in broad:
                ag_x(m, i).wait_send()
            ag_c(m, i, 0).wait_send()
            if m not in broad:
                ag_c(m, i, 1).wait_send()
            rs_x(m, i).wait_send()
            rs_core(m, i).wait_send()
    for copy in (y_tok(), y_cot(), y_proj()):
        copy.wait_send()
    for img in range(IMG):
        for make in (y_attn, y_mlp, y_sec, y_first):
            make(img).wait_send()
    for b in range(3):
        for i in range(7):
            ar(b, i).wait_send()


def fused_block(ratio, args):
    width, hid = args[2].shape[2], args[4].shape[1]
    table, sems, shards = scratch_table(width, hid)
    table["G1F"] = ((width // NZ, D), F32)
    names = list(NAMES_IN) + list(NAMES_OUT) + list(table)
    scratch = [pltpu.VMEM(shape, kind) for shape, kind in table.values()]
    for name, shape in sems.items():
        names += [name + "_s", name + "_r"]
        scratch += [pltpu.SemaphoreType.DMA(shape)] * 2
    tok = args[0].shape
    outs = [(tok, BF), (tok, F32)] + [(shape, F32) for shape in shards] + [((16, D), F32), ((32, 128), F32)]
    for name, (shape, kind) in zip(("o_blk", "o_gtok", "o_gp", "o_gu", "o_gd"), (outs[0], outs[1], outs[3], outs[4], outs[5])):
        names.append(name)
        scratch.append(pltpu.VMEM(shape, kind))
    vmem = pl.BlockSpec(memory_space=pltpu.VMEM)
    whole = pl.BlockSpec(memory_space=pl.ANY)
    return pl.pallas_call(
        functools.partial(block_kernel, ratio, width, hid, names),
        out_shape=[jax.ShapeDtypeStruct(shape, kind) for shape, kind in outs],
        in_specs=[vmem] * len(NAMES_IN),
        out_specs=[whole, whole, vmem, whole, whole, whole, vmem, vmem],
        scratch_shapes=scratch,
        compiler_params=pltpu.CompilerParams(
            collective_id=0, has_side_effects=True, vmem_limit_bytes=62 << 20
        ),
        name="fused_block",
    )(*args)


def finish_kernel(*refs):
    big, (small, rel), outs = refs[:6], refs[6:8], refs[8:24]
    held, sem_in, sem = refs[24:30], refs[30], refs[31]
    where = (0, 1, 2, 4, 6, 8)
    loads = [pltpu.make_async_copy(src, dst, sem_in.at[n]) for n, (src, dst) in enumerate(zip(big, held))]
    copies = [pltpu.make_async_copy(src, outs[i], sem.at[n]) for n, (src, i) in enumerate(zip(held, where))]
    for copy in loads:
        copy.start()
    for load, copy in zip(loads, copies):
        load.wait()
        copy.start()
    outs[3][...] = small[8:10]
    for i, row in ((5, 2), (9, 3), (10, 10), (11, 11), (12, 0), (13, 1)):
        outs[i][...] = small[row : row + 1].reshape(D)
    for j in range(FF // D):
        outs[7][j * D : (j + 1) * D] = small[4 + j : 5 + j].reshape(D)
    outs[14][...] = rel[:RELS, :HD]
    outs[15][...] = rel[:RELS, HD:]
    for copy in copies:
        copy.wait()


def hand_out(block_out, grad_tokens, grads, small, rel):
    big = [block_out, grad_tokens, *grads]
    vec = jax.ShapeDtypeStruct((D,), F32)
    table = jax.ShapeDtypeStruct((RELS, HD), F32)
    like = [jax.ShapeDtypeStruct(v.shape, v.dtype) for v in big]
    outs = [like[0], like[1], like[2], jax.ShapeDtypeStruct((2, D), F32), like[3], vec, like[4],
            jax.ShapeDtypeStruct((FF,), F32), like[5], vec, vec, vec, vec, vec, table, table]
    vmem, whole = pl.BlockSpec(memory_space=pltpu.VMEM), pl.BlockSpec(memory_space=pl.ANY)
    return pl.pallas_call(
        finish_kernel,
        out_shape=outs,
        in_specs=[whole] * 6 + [vmem] * 2,
        out_specs=[whole if i in (0, 1, 2, 4, 6, 8) else vmem for i in range(16)],
        scratch_shapes=[pltpu.VMEM(v.shape, v.dtype) for v in big] + [pltpu.SemaphoreType.DMA((6,))] * 2,
        compiler_params=pltpu.CompilerParams(vmem_limit_bytes=62 << 20),
        name="hand_out",
    )(*big, small, rel)


def on_device(dp_size, *args):
    (tokens, w_qkv, qv_bias, w_proj, proj_bias, w_up, up_bias, w_down, down_bias,
     norm1_gain, norm1_shift, norm2_gain, norm2_shift, rel_rows, rel_cols, cotangent) = args
    ratio = dp_size // RING
    weights = [w_qkv, w_proj, w_up, w_down]
    dims = (1, 0, 0, 0)
    groups = [[i * ratio + j for j in range(ratio)] for i in range(RING)]
    across = [[i * ratio + j for i in range(RING)] for j in range(ratio)]
    if ratio > 1:
        weights = [
            lax.all_gather(w, "dp", axis=dim, tiled=True, axis_index_groups=groups)
            for w, dim in zip(weights, dims)
        ]
    outs = fused_block(
        ratio,
        (tokens, cotangent, *weights, qv_bias, proj_bias, up_bias, down_bias,
         norm1_gain, norm1_shift, norm2_gain, norm2_shift, rel_rows, rel_cols),
    )
    block_out, grad_tokens, *grads, small, rel = outs
    if ratio > 1:
        grads = [
            lax.psum_scatter(g, "dp", scatter_dimension=dim, tiled=True, axis_index_groups=groups)
            for g, dim in zip(grads, dims)
        ]
        small, rel = lax.psum((small, rel), "dp", axis_index_groups=groups)
    return hand_out(block_out, grad_tokens, grads, small, rel)


def solution(mesh):
    split = P("dp", "tensor", None)
    specs = (split, P(None, "dp", "tensor"), P(), P(("tensor", "dp"), None), P(), P("dp", "tensor"), P(),
             P(("tensor", "dp"), None))
    return jax.shard_map(
        functools.partial(on_device, mesh.shape["dp"]),
        mesh=mesh,
        in_specs=specs + (P(),) * 7 + (split,),
        out_specs=(split,) + specs + (P(),) * 7,
        check_vma=False,
    )
```
